32 devices in a mesh: groups: 2 (over y), region: 16 (over z, x, core).
Axes of the slice: x: 2, y: 2, z: 4, core: 2. Of those that a mesh axis runs over, the one named last changes fastest.
Arguments:
- ray_code: bfloat16 [8192, 128], P(('groups', 'region')), parts along dimension 0, may hold values from -6 to 6
- seg_region: int32 [8192, 4], P(('groups', 'region')), parts along dimension 0, may hold values from 0 to 15, all different within a row; in each aligned block of 256 rows (0 to 255, 256 to 511, ...) at most 128 rows name the same one
- seg_count: int32 [8192, 4], P(('groups', 'region')), parts along dimension 0, may hold values from 1 to 16
- pixel_of_ray: int32 [8192], P(('groups', 'region')), parts along dimension 0, may hold values from 0 to 4095, as said below
- sample_code: bfloat16 [16, 16, 128], P('region'), may hold values from -5 to 5
- w_hidden: bfloat16 [16, 128, 128], P('region'), may hold values from -0.5 to 0.5
- w_feat: bfloat16 [16, 128, 64], P('region'), may hold values from -0.5 to 0.5
- w_density: bfloat16 [16, 128], P('region'), may hold values from -0.5 to 0.5
- decoder: bfloat16 [576, 384], replicated, may hold values from -0.25 to 0.25
- target: bfloat16 [8192, 384], P(('groups', 'region')), parts along dimension 0, may hold values from -6 to 6
Outputs:
- hidden_grad: float32 [16, 256, 128], P('region', 'groups'), parts along dimension 1
- feat_grad: float32 [16, 256, 64], P('region', 'groups'), parts along dimension 1
- density_grad: float32 [16, 256], P('region', 'groups'), parts along dimension 1
- code_grad: float32 [16, 32, 128], P('region', 'groups'), parts along dimension 1
The draws below stay inside these ranges and needn't reach their ends.
There are 2 independent parts, one for each index of `groups`. The reference program is written for one: setup_inputs(seed, part) draws one part's arguments, and reference() takes and returns one part's arrays. A program takes and returns all parts, laid end to end along the dimension named above; an argument that names none is the same for every part. Nothing has to cross between parts.
Inputs may be any that keep to these rules, and one draw needn't show every extreme that they name: `seg_region`: each ray lists 4 different regions, front to back. Among the rays of one device no region is listed more than 128 times, a bound that some block reaches. `pixel_of_ray`: every pixel is named by exactly one ray. The rays of one device name exactly 16 pixels in each block of 256 consecutive pixels.
All inputs are finite; a program needn't handle non-finite values.
Results may differ from the reference program's by a relative error of at most 0.0085.
The reference program's roundings to bfloat16 on the way count: a program that leaves them out, or rounds other values in their place, can miss the bound.
Values may be sent and summed in bfloat16 or wider, within the bound.
No kernel may reach another device: no remote copies, remote signals or barrier semaphores. Data moves between devices by JAX's collectives and lax.ppermute only.
A program may use at most 192 MiB of HBM per device.

```python
import math
import jax
import jax.numpy as jnp
import numpy as np
from jax import lax

CODE = 128
HID = 128
FEAT = 64
DINO = 384
SAMPLES = 16
SEGS = 4
IW = 128
RAY_DEV = 256
REGIONS = 16
RAYS = 4096
ROWS = 32
MOST = 128


def draw_pixel_of_ray(key, part):
    group_size = RAY_DEV // REGIONS
    key_rays, key_tiles = jax.random.split(key)

    def shuffle(sub_key):
        return jax.random.permutation(sub_key, RAY_DEV).astype(jnp.int32)
    order = jax.vmap(shuffle)(jax.random.split(key_rays, REGIONS))
    spots = jax.vmap(shuffle)(jax.random.split(key_tiles, REGIONS))
    tile_index = order // group_size
    slot_index = order % group_size
    source = jnp.arange(REGIONS, dtype=jnp.int32)[:, None]
    chosen = spots[tile_index, source * group_size + slot_index]
    return (tile_index * RAY_DEV + chosen).reshape(-1).astype(jnp.int32)


def plant(result, rng, least, largest):
    longest = result.shape.index(max(result.shape))
    spots = []
    for shift in (0, 1):
        where = [jax.random.randint(jax.random.fold_in(rng, axis), (), 0, length) for axis, length in enumerate(result.shape)]
        where[longest] = (where[longest] + shift) % result.shape[longest]
        spots.append(tuple(where))
    return result.at[spots[0]].set(least).at[spots[1]].set(largest)


def levels(key, shape, shards, least, top_value):
    loudness = 1.0
    for axis_at, parts in shards:
        heights = jax.random.uniform(jax.random.fold_in(jax.random.fold_in(key, 6), axis_at), (parts,), jnp.float32, least / len(shards), top_value / len(shards))
        loudness = loudness * jnp.repeat(jnp.exp(heights), shape[axis_at] // parts).reshape((-1,) + (1,) * (len(shape) - 1 - axis_at))
    return loudness


def deal_out(key, own, number, rows, number_of, top, most, slope):
    ranking = jax.random.permutation(key, number_of)
    packed, ordinary = shares(number_of, rows * top, most, slope, True), shares(number_of, rows * top, most, slope, False)
    places = jnp.arange(number_of)

    def named(sizes, offset_by):
        used = int((sizes > 0).sum())
        fixed = max(1, used // 4)
        shifted = fixed + (places - fixed + offset_by * (used - fixed)) % max(1, number_of - fixed)
        return jnp.zeros((number_of,), jnp.int32).at[ranking[jnp.where(places < fixed, places, shifted)]].set(jnp.asarray(sizes, jnp.int32))

    sizes = jnp.where(number % 4 == 0, named(packed, number // 4), named(ordinary, number - number // 4 - 1))
    mixed = jax.random.permutation(jax.random.fold_in(own, 3), number_of)
    source_of, receiver = mixed[0:number_of // 2 * 2:2], mixed[1:number_of // 2 * 2:2]
    slack = jnp.minimum(sizes[source_of] - 1, most - sizes[receiver]) // 2
    slack = jnp.where((source_of == ranking[0]) | (receiver == ranking[0]) | (sizes[receiver] == 0), 0, jnp.maximum(slack, 0))
    shifted = jax.random.randint(jax.random.fold_in(own, 4), (number_of // 2,), 0, 1 << 20) % (slack + 1)
    sizes = sizes.at[source_of].add(-shifted).at[receiver].add(shifted)
    members = jnp.searchsorted(jnp.cumsum(sizes), jnp.arange(rows * top), side="right").astype(jnp.int32)
    listing = members.reshape(top, rows).T
    listing = listing[jax.random.permutation(jax.random.fold_in(own, 1), rows)]
    offset_by = jax.random.randint(jax.random.fold_in(own, 2), (rows, 1), 0, top)
    return jnp.take_along_axis(listing, (jnp.arange(top)[None, :] + offset_by) % top, axis=1)


def shares(count, total, most, lean, full):
    weights = [(1 << 20) // math.isqrt(grade ** lean) + 1 for grade in range(1, count + 1)]
    largest = most if full else min(most, max(-(-total // count), total * weights[0] // sum(weights)))
    least = 1 if total - largest >= count - 1 else 0
    holding, surplus = [largest] + [least] * (count - 1), total - largest - least * (count - 1)
    while surplus > 0:
        movable = [i for i in range(1, count) if holding[i] < largest] or [i for i in range(1, count) if holding[i] < most]
        mass, left = sum([weights[i] for i in movable]), surplus
        for i in movable:
            more = min(most - holding[i], max(1, left * weights[i] // mass), surplus)
            holding[i] = holding[i] + more
            surplus = surplus - more
    return np.array(holding)


def noise(stream_key, dims, scale, reach, shards=(), kind=jnp.bfloat16):
    factor_of = levels(stream_key, dims, shards, -0.22, 0.18) if shards else 1.0
    values = jax.random.normal(stream_key, dims, jnp.float32) * scale * factor_of
    return jnp.minimum(jnp.maximum(values, -reach), reach).astype(kind)


def setup_inputs(seed: int = 0, part: int = 0) -> dict:
    keys = jax.random.split(jax.random.key(seed), 11)
    part_keys = jax.random.split(jax.random.fold_in(keys[10], part), 11)
    ray_code = noise(part_keys[0], (RAYS, CODE), 1.0, 6.0, ((0, 16),))
    seg_region_keys = jax.random.split(jax.random.fold_in(part_keys[1], 1), RAYS // RAY_DEV)
    seg_region_turns = jax.random.permutation(jax.random.fold_in(part_keys[1], 3), RAYS // RAY_DEV)
    seg_region = jax.vmap(lambda own, number: deal_out(jax.random.fold_in(part_keys[1], 2), own, number, RAY_DEV, REGIONS, SEGS, MOST, 2))(seg_region_keys, seg_region_turns).reshape((RAYS, SEGS))
    seg_count = plant(jax.random.randint(part_keys[2], (RAYS, SEGS), 1, SAMPLES + 1), jax.random.fold_in(part_keys[2], 1), 1, SAMPLES).astype(jnp.int32)
    pixel_of_ray = draw_pixel_of_ray(jax.random.fold_in(jax.random.fold_in(keys[10], part), 71), part)
    sample_code = noise(keys[4], (REGIONS, SAMPLES, CODE), 0.7, 5.0, ((0, 16),))
    w_hidden = noise(keys[5], (REGIONS, CODE, HID), CODE ** -0.5, 0.5, ((0, 16),))
    w_feat = noise(keys[6], (REGIONS, HID, FEAT), HID ** -0.5, 0.5, ((0, 16),))
    w_density = noise(keys[7], (REGIONS, HID), HID ** -0.5, 0.5, ((0, 16),))
    decoder = noise(keys[8], (9 * FEAT, DINO), (9 * FEAT) ** -0.5, 0.25)
    target = noise(part_keys[9], (RAYS, DINO), 1.0, 6.0, ((0, 16),))
    return {"ray_code": ray_code, "seg_region": seg_region, "seg_count": seg_count, "pixel_of_ray": pixel_of_ray, "sample_code": sample_code, "w_hidden": w_hidden, "w_feat": w_feat, "w_density": w_density, "decoder": decoder, "target": target}


STEP = 0.08


def segment_forward(ray_codes, sample_counts, sample_codes, w_first, w_second, w_sigma):
    seg_total = ray_codes.shape[0]
    samp_total = sample_codes.shape[0]
    inputs = (ray_codes[:, None, :] + sample_codes[None, :, :]).reshape(seg_total * samp_total, ray_codes.shape[1])
    before_relu = jnp.dot(inputs, w_first, preferred_element_type=jnp.float32)
    hidden = jnp.maximum(before_relu, 0.0).astype(jnp.bfloat16)
    feature = jnp.dot(hidden, w_second, preferred_element_type=jnp.float32).reshape(seg_total, samp_total, w_second.shape[1])
    density = jnp.dot(hidden, w_sigma, preferred_element_type=jnp.float32).reshape(seg_total, samp_total)
    is_live = jnp.arange(samp_total, dtype=jnp.int32)[None, :] < sample_counts[:, None]
    thickness = jnp.where(is_live, STEP * jax.nn.softplus(density), 0.0)
    ahead = jnp.cumsum(thickness, axis=1) - thickness
    passing = jnp.exp(-ahead)
    keeping = jnp.exp(-thickness)
    weight = passing * (1.0 - keeping)
    seg_feat = jnp.einsum("bs,bsf->bf", weight, feature)
    seg_depth = jnp.sum(thickness, axis=1)
    return seg_feat, seg_depth, (inputs, before_relu, hidden, feature, density, is_live, passing, keeping, weight)


def segment_backward(grad_feat, grad_depth, saved_acts, w_first, w_second, w_sigma):
    inputs, before_relu, hidden, feature, density, is_live, passing, keeping, weight = saved_acts
    seg_total, samp_total = weight.shape
    along_feat = jnp.einsum("bsf,bf->bs", feature, grad_feat)
    carried = along_feat * weight
    later_sum = jnp.sum(carried, axis=1, keepdims=True) - jnp.cumsum(carried, axis=1)
    grad_thick = grad_depth[:, None] + along_feat * passing * keeping - later_sum
    grad_density = jnp.where(is_live, grad_thick * STEP * jax.nn.sigmoid(density), 0.0).astype(jnp.bfloat16).reshape(seg_total * samp_total)
    grad_feature = (weight[:, :, None] * grad_feat[:, None, :]).astype(jnp.bfloat16).reshape(seg_total * samp_total, grad_feat.shape[1])
    contract_rows = (((0,), (0,)), ((), ()))
    contract_cols = (((1,), (1,)), ((), ()))
    second_grad = lax.dot_general(hidden, grad_feature, contract_rows, preferred_element_type=jnp.float32)
    sigma_grad = jnp.dot(grad_density, hidden, preferred_element_type=jnp.float32)
    grad_hidden = lax.dot_general(grad_feature, w_second, contract_cols, preferred_element_type=jnp.float32)
    grad_hidden = grad_hidden + grad_density.astype(jnp.float32)[:, None] * w_sigma.astype(jnp.float32)[None, :]
    grad_pre = jnp.where(before_relu > 0.0, grad_hidden, 0.0).astype(jnp.bfloat16)
    first_grad = lax.dot_general(inputs, grad_pre, contract_rows, preferred_element_type=jnp.float32)
    grad_inputs = lax.dot_general(grad_pre, w_first, contract_cols, preferred_element_type=jnp.float32)
    code_grad = jnp.sum(grad_inputs.reshape(seg_total, samp_total, w_first.shape[0]), axis=0)
    return first_grad, second_grad, sigma_grad, code_grad


def unfold(framed, height, col_total):
    pieces = [framed[row_step:row_step + height, col_step:col_step + col_total] for row_step in range(3) for col_step in range(3)]
    return jnp.concatenate(pieces, axis=-1).reshape(height * col_total, 9 * framed.shape[2])


def fold_back(grad_padded, out_rows, col_total):
    term_list = [grad_padded[2 - row_step:2 - row_step + out_rows, 2 - col_step:2 - col_step + col_total, row_step, col_step] for row_step in range(3) for col_step in range(3)]
    summed = term_list[0]
    for term in term_list[1:]:
        summed = summed + term
    return summed


def reference(ray_code, seg_region, seg_count, pixel_of_ray, sample_code, w_hidden, w_feat, w_density, decoder, target):
    region_total = REGIONS
    entries = RAY_DEV * SEGS
    slot_total = region_total * MOST
    by_source = seg_region.reshape(region_total, entries)
    region_ids = jnp.arange(region_total, dtype=jnp.int32)

    def entry_ranks(row_ids):
        one_hot = (row_ids[:, None] == region_ids[None, :]).astype(jnp.int32)
        return jnp.sum((jnp.cumsum(one_hot, axis=0) - one_hot) * one_hot, axis=1)

    rank_table = lax.map(entry_ranks, by_source)
    target_slot = (by_source * slot_total + region_ids[:, None] * MOST + rank_table).reshape(-1).astype(jnp.int32)
    entry_ray = jnp.arange(RAYS * SEGS, dtype=jnp.int32) // SEGS
    table_codes = jnp.zeros((region_total * slot_total, CODE), jnp.bfloat16).at[target_slot].set(ray_code[entry_ray]).reshape(region_total, slot_total, CODE)
    table_counts = jnp.zeros((region_total * slot_total,), jnp.int32).at[target_slot].set(seg_count.reshape(-1)).reshape(region_total, slot_total)

    def region_forward(operands):
        ray_codes, sample_counts, codes_here, w_first, w_second, w_sigma = operands
        seg_feat, seg_depth, unused = segment_forward(ray_codes, sample_counts, codes_here, w_first, w_second, w_sigma)
        return seg_feat, seg_depth

    feat_table, depth_table = lax.map(region_forward, (table_codes, table_counts, sample_code, w_hidden, w_feat, w_density))
    part_feat = feat_table.reshape(region_total * slot_total, FEAT)[target_slot].reshape(RAYS, SEGS, FEAT)
    part_depth = depth_table.reshape(region_total * slot_total)[target_slot].reshape(RAYS, SEGS)
    depth_ahead = jnp.cumsum(part_depth, axis=1) - part_depth
    attenuation = jnp.exp(-depth_ahead)
    ray_feat = jnp.einsum("rk,rkf->rf", attenuation, part_feat)
    image_tile = jnp.zeros((RAYS, FEAT), jnp.float32).at[pixel_of_ray].set(ray_feat).astype(jnp.bfloat16).reshape(ROWS, IW, FEAT)
    framed = jnp.pad(image_tile, ((1, 1), (1, 1), (0, 0)))
    patches = unfold(framed, ROWS, IW)
    decoded = jnp.dot(patches, decoder, preferred_element_type=jnp.float32)
    grad_dec = (decoded - target.astype(jnp.float32)).astype(jnp.bfloat16)
    contract_cols = (((1,), (1,)), ((), ()))
    grad_patch = lax.dot_general(grad_dec, decoder, contract_cols, preferred_element_type=jnp.float32).reshape(ROWS, IW, 3, 3, FEAT)
    grad_padded = jnp.pad(grad_patch, ((1, 1), (1, 1), (0, 0), (0, 0), (0, 0)))
    grad_image = fold_back(grad_padded, ROWS, IW).reshape(RAYS, FEAT)
    grad_ray = grad_image[pixel_of_ray]
    grad_seg = attenuation[:, :, None] * grad_ray[:, None, :]
    pulled = attenuation * jnp.einsum("rkf,rf->rk", part_feat, grad_ray)
    grad_depth = jnp.cumsum(pulled, axis=1) - jnp.sum(pulled, axis=1, keepdims=True)
    grad_feat_table = jnp.zeros((region_total * slot_total, FEAT), jnp.float32).at[target_slot].set(grad_seg.reshape(RAYS * SEGS, FEAT)).reshape(region_total, slot_total, FEAT)
    grad_depth_table = jnp.zeros((region_total * slot_total,), jnp.float32).at[target_slot].set(grad_depth.reshape(-1)).reshape(region_total, slot_total)

    def region_backward(operands):
        ray_codes, sample_counts, codes_here, w_first, w_second, w_sigma, grad_feat, grad_dep = operands
        unused_feat, unused_depth, saved_acts = segment_forward(ray_codes, sample_counts, codes_here, w_first, w_second, w_sigma)
        return segment_backward(grad_feat, grad_dep, saved_acts, w_first, w_second, w_sigma)

    first_grad, second_grad, sigma_grad, code_grad = lax.map(region_backward, (table_codes, table_counts, sample_code, w_hidden, w_feat, w_density, grad_feat_table, grad_depth_table))
    return (first_grad, second_grad, sigma_grad, code_grad)
```

```python
import functools

import jax
import jax.numpy as jnp
from jax import lax
from jax.experimental import pallas as pl
from jax.experimental.pallas import tpu as pltpu
from jax.sharding import PartitionSpec as P

IW = 128
STEP = 0.08
F32 = jnp.float32
BF16 = jnp.bfloat16
LANES = 128

WF_AT = 128
SAMPLE_AT = 192
META_AT = 208
RAYS_AT = 224
G2_AT = 192
DG_AT = 208
PART_ROWS = 224

PARAMS = pltpu.CompilerParams(vmem_limit_bytes=52 << 20)


def iota(shape, dim):
    return lax.broadcasted_iota(jnp.int32, shape, dim)


def dot(lhs, rhs, left=1, right=0):
    return lax.dot_general(lhs, rhs, (((left,), (right,)), ((), ())), preferred_element_type=F32)


def split(values):
    high = values.astype(BF16)
    return high, (values - high.astype(F32)).astype(BF16)


def running_sum(values):
    rows = values.shape[0]
    row = iota(values.shape, 0)
    step = 1
    while step < rows:
        values = values + jnp.where(row >= step, pltpu.roll(values, step, 0), 0.0)
        step *= 2
    return values


def pack_kernel(half, group, room, pix_ref, reg_ref, cnt_ref, code_ref, samp_ref, wh_ref, wf_ref, wd_ref, out_ref, meta_ref):
    rays = code_ref.shape[0]
    regions = 2 * half
    shift = rays.bit_length() - 1
    pix = pix_ref[...]
    tile = lax.shift_right_logical(pix, shift)
    spot = pix & (rays - 1)
    mine = iota((regions, rays), 0) == tile
    mine_f = jnp.where(mine, 1.0, 0.0)
    earlier = jnp.where(iota((rays, rays), 0) < iota((rays, rays), 1), 1.0, 0.0).astype(BF16)
    counts = dot(mine_f.astype(BF16), earlier)
    rank = jnp.sum(counts * mine_f, axis=0, keepdims=True).astype(jnp.int32)
    row_place = lax.shift_right_logical(tile, 1) * room + (tile & 1) * group + rank
    lane_place = tile * group + rank
    meta_ref[...] = jnp.zeros(meta_ref.shape, F32)
    meta_ref[1:2, :] = spot.astype(F32)
    meta_ref[2:6, :] = reg_ref[...].astype(F32)
    meta_ref[6:10, :] = cnt_ref[...].astype(F32)
    row_hot = jnp.where(iota((half * room, rays), 0) == row_place, 1.0, 0.0).astype(BF16)
    codes = dot(row_hot, code_ref[...]).astype(BF16)
    lane_hot = jnp.where(iota((rays, rays), 0) == lane_place, 1.0, 0.0).astype(BF16)
    meta = dot(meta_ref[...].astype(BF16), lane_hot, 1, 1)
    meta_ref[...] = meta
    wh_t = wh_ref[0].astype(F32).T.astype(BF16)
    wf_t = wf_ref[0].astype(F32).T.astype(BF16)
    samples = samp_ref[0]
    density = wd_ref[...].astype(F32)
    first = iota((16, LANES), 0) == 0
    for chip in range(half):
        out_ref[chip, 0:WF_AT] = wh_t
        out_ref[chip, WF_AT:SAMPLE_AT] = wf_t
        out_ref[chip, SAMPLE_AT:META_AT] = samples
        here = pltpu.roll(meta, (rays - chip * 2 * group) % rays, 1)[:, :LANES]
        out_ref[chip, META_AT:RAYS_AT] = jnp.where(first, density, here).astype(BF16)
        out_ref[chip, RAYS_AT : RAYS_AT + room] = codes[chip * room : (chip + 1) * room]


def pick(source_ref, wanted, out_ref):
    regions = source_ref.shape[0]
    segs = len(wanted)
    for part in range(2):
        lanes = slice(part * LANES, (part + 1) * LANES)
        rel = [jnp.broadcast_to(row[:, lanes], (8, LANES)) for row in wanted]

        def step(index, carry):
            rows = pl.ds(pl.multiple_of(index * 8, 8), 8)
            found = [jnp.zeros((8, LANES), F32)] * segs
            for region in range(regions):
                value = source_ref[region, rows, lanes]
                found = [jnp.where(rel[k] == region, value, found[k]) for k in range(segs)]
            for k in range(segs):
                out_ref[2 * k + part, rows, :] = found[k]
            return carry

        lax.fori_loop(0, 16, step, 0)


def spread(source_ref, wanted, region):
    segs = len(wanted)
    pieces = []
    for part in range(2):
        lanes = slice(part * LANES, (part + 1) * LANES)
        total = jnp.zeros((LANES, LANES), F32)
        for k in range(segs):
            total = jnp.where(wanted[k][:, lanes] == region, source_ref[2 * k + part], total)
        pieces.append(total)
    return jnp.concatenate(pieces, axis=1)


def block_of(a_ref, b_ref, half, region):
    return (a_ref, region) if region < half else (b_ref, region - half)


def seg_hot(wanted, regions):
    return jnp.concatenate(
        [jnp.where(iota((regions, row.shape[1]), 0) == row, 1.0, 0.0) for row in wanted], axis=1
    )


def expand_samples(table_ref, hot2, base_ref):
    tiles = base_ref.shape[0]

    def one(sample):
        values = dot(table_ref[sample], hot2, 0, 0)
        at = slice(sample * LANES, (sample + 1) * LANES)
        for tile in range(tiles):
            base_ref[tile, at, :] = values[:, tile * LANES : (tile + 1) * LANES]

    for sample in range(table_ref.shape[0]):
        one(sample)


def forward_kernel(
    half, group, room, a_ref, b_ref,
    image_ref, a_out, table_ref, att_hw_ref, weight_ref, pass_ref, slope_ref, att_ref, rel_ref, codes_ref,
    meta_ref, plain_ref, proj_ref, base_ref, h_ref, row_ref, ahead_ref,
):
    regions = 2 * half
    rays = codes_ref.shape[0]
    segs = rel_ref.shape[0]
    samples = weight_ref.shape[1]
    core = lax.axis_index("region") & 1
    per_tile = LANES // room
    lane = iota((16, LANES), 1)
    chunk = lax.div(lane, room)
    inside = lane - chunk * room
    mine = (inside < 2 * group) & (lax.div(inside, group) == core)
    for tile in range(regions // per_tile):
        total = jnp.zeros((16, LANES), F32)
        for spot in range(per_tile):
            ref, at = block_of(a_ref, b_ref, half, tile * per_tile + spot)
            block = ref[at, META_AT:RAYS_AT].astype(F32)
            total = jnp.where(chunk == spot, pltpu.roll(block, spot * room, 1), total)
        meta_ref[:, tile * LANES : (tile + 1) * LANES] = jnp.where(mine, total, -1.0)
    meta_src = meta_ref[...]
    places = regions * room
    to_pixel = jnp.where(
        iota((rays, places), 0).astype(F32) == meta_src[1:2, :], 1.0, 0.0
    ).astype(BF16)
    sources = jnp.concatenate(
        [a_ref[i, RAYS_AT : RAYS_AT + room] for i in range(half)]
        + [b_ref[i, RAYS_AT : RAYS_AT + room] for i in range(half)],
        axis=0,
    )
    codes = dot(to_pixel, sources)
    codes_ref[...] = codes.astype(BF16)
    codes_t = codes.T.astype(BF16)
    meta = dot(meta_src.astype(BF16), to_pixel, 1, 1)
    region = meta[2 : 2 + segs].astype(jnp.int32)
    rel = jnp.bitwise_xor(region & 1, core) * half + lax.shift_right_logical(region, 1)
    rel_ref[...] = rel
    for k in range(segs):
        for part in range(2):
            row_ref[2 * k + part] = meta[6 + k : 7 + k, part * LANES : (part + 1) * LANES]
    wanted = [rel_ref[k : k + 1, :] for k in range(segs)]
    for r in range(regions):
        ref, at = block_of(a_ref, b_ref, half, r)
        w_t = ref[at, 0:WF_AT]
        proj_ref[r] = dot(w_t, codes_t)
        own = dot(ref[at, SAMPLE_AT:META_AT], w_t, 1, 1)
        plain_ref[0:samples, r, :] = own
        plain_ref[samples, r : r + 1, :] = ref[at, META_AT:RAYS_AT].astype(F32)[0:1, :]
    for s in range(samples + 1):
        high, low = split(plain_ref[s])
        table_ref[s] = jnp.concatenate([high, low], axis=0)
    pick(proj_ref, wanted, a_out)
    hot = seg_hot(wanted, regions).astype(BF16)
    expand_samples(table_ref, jnp.concatenate([hot, hot], axis=0), base_ref)
    ahead_ref[...] = jnp.zeros(ahead_ref.shape, F32)
    order = iota((samples, LANES), 0).astype(F32)

    def step(tile, carry):
        sums = [jnp.zeros((8, LANES), F32)] * samples
        for ht in range(16):
            rows = slice(ht * 8, ht * 8 + 8)
            a = a_out[tile, rows, :]
            wd = base_ref[tile, samples * LANES + ht * 8 : samples * LANES + ht * 8 + 8, :]
            for s in range(samples):
                h = jnp.maximum(a + base_ref[tile, s * LANES + ht * 8 : s * LANES + ht * 8 + 8, :], 0.0)
                h_ref[ht * samples + s] = h
                sums[s] = sums[s] + h * wd
        density = jnp.concatenate([jnp.sum(v, axis=0, keepdims=True) for v in sums], axis=0)
        part = tile & 1
        live = order < row_ref[tile]
        soft = jnp.maximum(density, 0.0) + jnp.log1p(jnp.exp(-jnp.abs(density)))
        thick = jnp.where(live, STEP * soft, 0.0)
        through = running_sum(thick)
        passing = jnp.exp(-(through - thick))
        keeping = jnp.exp(-thick)
        weight = passing * (1.0 - keeping)
        weight_ref[tile] = weight
        pass_ref[tile] = passing * keeping
        slope_ref[tile] = jnp.where(live, STEP / (1.0 + jnp.exp(-density)), 0.0)
        before = ahead_ref[part]
        att = jnp.exp(-before)
        ahead_ref[part] = before + through[samples - 1 : samples, :]
        att_ref[tile] = att
        scale = [jnp.broadcast_to(weight[s : s + 1, :] * att, (8, LANES)) for s in range(samples)]
        for ht in range(16):
            total = scale[0] * h_ref[ht * samples]
            for s in range(1, samples):
                total = total + scale[s] * h_ref[ht * samples + s]
            att_hw_ref[tile, ht * 8 : ht * 8 + 8, :] = total
        return carry

    lax.fori_loop(0, 2 * segs, step, 0)
    feat = jnp.zeros(image_ref.shape, F32)
    for r in range(regions):
        ref, at = block_of(a_ref, b_ref, half, r)
        high, low = split(spread(att_hw_ref, wanted, r))
        wf_t = ref[at, WF_AT:SAMPLE_AT]
        feat = feat + dot(wf_t, high) + dot(wf_t, low)
    image_ref[...] = feat.astype(BF16)


def shifted(values, by):
    lane = iota(values.shape, 1)
    if by == 0:
        return values
    if by > 0:
        return jnp.where(lane == 0, 0.0, pltpu.roll(values, 1, 1))
    return jnp.where(lane == LANES - 1, 0.0, pltpu.roll(values, LANES - 1, 1))


def backward_kernel(
    half, own_ref, inner_ref, cross_ref, tgt_ref, tin_ref, tcr_ref, dec_ref, dect_ref,
    wa_ref, wb_ref, a_ref, table_ref, att_hw_ref, weight_ref, pass_ref, slope_ref, att_ref, rel_ref, codes_ref,
    mine_ref, other_ref,
    patch_ref, proj_ref, q_ref, base_ref, h_ref, gp_ref, g1_ref, hd_ref, tail_ref, row_ref,
):
    regions = 2 * half
    feats, rays = own_ref.shape
    segs = rel_ref.shape[0]
    samples = weight_ref.shape[1]
    me = lax.axis_index("region")
    core = me & 1
    own = own_ref[...].astype(F32)
    inner = inner_ref[...].astype(F32)
    cross = cross_ref[...].astype(F32)
    top = jnp.where(core == 0, cross, inner)
    bottom = jnp.where(core == 0, inner, cross)
    rows = [v[:, i * IW : (i + 1) * IW] for v in (top, own, bottom) for i in range(2)]
    for at, row in enumerate(rows):
        for dx in range(3):
            piece = shifted(row, 1 - dx).astype(BF16)
            for dy in range(3):
                if 0 <= at - dy < 4:
                    patch_ref[(3 * dy + dx) * feats : (3 * dy + dx + 1) * feats, (at - dy) * IW : (at - dy + 1) * IW] = piece
    tin = tin_ref[...].astype(F32)
    tcr = tcr_ref[...].astype(F32)
    t_top = jnp.where(core == 0, tcr, tin)
    t_bottom = jnp.where(core == 0, tin, tcr)
    decoded = dot(dect_ref[...], patch_ref[...])
    tgt = tgt_ref[...].astype(F32)
    g_top = jnp.where(me > 0, decoded[:, 0:IW] - t_top, 0.0)
    g_own = decoded[:, IW : 3 * IW] - tgt
    g_bottom = jnp.where(me < regions - 1, decoded[:, 3 * IW :] - t_bottom, 0.0)
    grad_dec = jnp.concatenate([g_top, g_own, g_bottom], axis=1).astype(BF16)
    grad_patch = dot(dec_ref[...], grad_dec)
    image_rows = []
    for i in range(2):
        total = jnp.zeros((feats, IW), F32)
        for dx in range(3):
            term = jnp.zeros((feats, IW), F32)
            for dy in range(3):
                at = (3 * dy + dx) * feats
                term = term + grad_patch[at : at + feats, (i - dy + 2) * IW : (i - dy + 3) * IW]
            total = total + shifted(term, dx - 1)
        image_rows.append(total)
    grad_ray = jnp.concatenate(image_rows, axis=1)
    g_high, g_low = split(grad_ray)
    g_both = jnp.concatenate([g_high, g_low], axis=0)
    wanted = [rel_ref[k : k + 1, :] for k in range(segs)]

    for r in range(regions):
        ref, at = block_of(wa_ref, wb_ref, half, r)
        out, to = block_of(mine_ref, other_ref, half, r)
        wf_t = ref[at]
        proj_ref[r] = dot(jnp.concatenate([wf_t, wf_t], axis=0), g_both, 0, 0)
        held = spread(att_hw_ref, wanted, r).astype(BF16)
        out[to, WF_AT:G2_AT] = dot(g_high, held, 1, 1).astype(BF16)
    pick(proj_ref, wanted, q_ref)
    hot = seg_hot(wanted, regions).astype(BF16)
    expand_samples(table_ref, jnp.concatenate([hot, hot], axis=0), base_ref)
    for part in range(2):
        later = jnp.zeros((1, LANES), F32)
        for k in reversed(range(segs)):
            row_ref[2 * k + part] = -later
            pulled = jnp.sum(att_hw_ref[2 * k + part] * q_ref[2 * k + part], axis=0, keepdims=True)
            later = later + pulled

    def step(tile, carry):
        att = jnp.broadcast_to(att_ref[tile], (8, LANES))
        sums = [jnp.zeros((8, LANES), F32)] * samples
        for ht in range(16):
            rows = slice(ht * 8, ht * 8 + 8)
            a = a_ref[tile, rows, :]
            q = q_ref[tile, rows, :] * att
            q_ref[tile, rows, :] = q
            for s in range(samples):
                h = jnp.maximum(a + base_ref[tile, s * LANES + ht * 8 : s * LANES + ht * 8 + 8, :], 0.0)
                h_ref[ht * samples + s] = h
                sums[s] = sums[s] + h * q
        along = jnp.concatenate([jnp.sum(v, axis=0, keepdims=True) for v in sums], axis=0)
        weight = weight_ref[tile]
        carried = along * weight
        through = running_sum(carried)
        later = through[samples - 1 : samples, :] - through
        grad_thick = row_ref[tile] + along * pass_ref[tile] - later
        grad_density = (grad_thick * slope_ref[tile]).astype(BF16).astype(F32)
        scale = [jnp.broadcast_to(weight[s : s + 1, :], (8, LANES)) for s in range(samples)]
        slant = [jnp.broadcast_to(grad_density[s : s + 1, :], (8, LANES)) for s in range(samples)]
        lanes = pl.ds(pl.multiple_of(tile * LANES, LANES), LANES)
        for pair in range(8):
            at = [slice((2 * pair + u) * 8, (2 * pair + u) * 8 + 8) for u in range(2)]
            q = [q_ref[tile, rows, :] for rows in at]
            wd = [base_ref[tile, samples * LANES + rows.start : samples * LANES + rows.stop, :] for rows in at]
            g1 = [jnp.zeros((8, LANES), F32)] * 2
            hd = [jnp.zeros((8, LANES), F32)] * 2
            for s in range(samples):
                both = []
                for u in range(2):
                    h = h_ref[(2 * pair + u) * samples + s]
                    gp = jnp.where(h > 0.0, scale[s] * q[u] + slant[s] * wd[u], 0.0)
                    g1[u] = g1[u] + gp
                    hd[u] = hd[u] + slant[s] * h
                    both.append(gp)
                gp_ref[s, 16 * pair : 16 * pair + 16, lanes] = jnp.concatenate(both, axis=0).astype(BF16)
            for u in range(2):
                g1_ref[tile, at[u], :] = g1[u]
            hd_ref[16 * pair : 16 * pair + 16, lanes] = jnp.concatenate(hd, axis=0).astype(BF16)
        return carry

    lax.fori_loop(0, 2 * segs, step, 0)
    codes = codes_ref[...]
    tail_ref[...] = jnp.zeros(tail_ref.shape, F32)
    for s in range(samples):
        tail_ref[:, s, :] = dot(hot, gp_ref[s], 1, 1)
    tail_ref[:, samples, :] = dot(hot, hd_ref[...], 1, 1)
    for r in range(regions):
        out, to = block_of(mine_ref, other_ref, half, r)
        held = spread(g1_ref, wanted, r).astype(BF16)
        out[to, 0:WF_AT] = dot(held, codes).astype(BF16)
        out[to, G2_AT:PART_ROWS] = tail_ref[r].astype(BF16)


def finish_kernel(part_ref, samp_ref, wh_ref, hid_ref, feat_ref, dens_ref, code_ref):
    total = part_ref[0].astype(F32)
    for i in range(1, part_ref.shape[0]):
        total = total + part_ref[i].astype(F32)
    g2 = total[G2_AT:DG_AT]
    high, low = split(g2)
    samples = samp_ref[0]
    wh = wh_ref[0]
    hid_ref[0] = total[0:WF_AT].T + dot(samples, high, 0, 0) + dot(samples, low, 0, 0)
    feat_ref[0] = total[WF_AT:G2_AT].T
    dens_ref[...] = total[DG_AT : DG_AT + 1]
    code_ref[0] = dot(high, wh, 1, 1) + dot(low, wh, 1, 1)


def local(ray_code, seg_region, seg_count, pixel_of_ray, sample_code, w_hidden, w_feat, w_density, decoder, target):
    regions = lax.axis_size("region")
    half = regions // 2
    rays, segs = seg_region.shape
    code_width = ray_code.shape[1]
    hid_width = w_hidden.shape[2]
    feat_width = w_feat.shape[2]
    samples = sample_code.shape[1]
    group = rays // regions
    room = max(16, 2 * group)
    pack_rows = RAYS_AT + room
    tiles = 2 * segs
    lanes = segs * rays
    core = lax.axis_index("region") & 1
    same_core = [list(range(c, regions, 2)) for c in range(2)]
    inner = [(i, i ^ 1) for i in range(regions)]
    cross = [(i, i + 1) for i in range(1, regions - 1, 2)] + [(i + 1, i) for i in range(1, regions - 1, 2)]

    packed = pl.pallas_call(
        functools.partial(pack_kernel, half, group, room),
        out_shape=jax.ShapeDtypeStruct((half, pack_rows, LANES), BF16),
        scratch_shapes=[pltpu.VMEM((16, rays), F32)],
        compiler_params=PARAMS,
        name="pack",
    )(
        pixel_of_ray.reshape(1, rays), seg_region.T, seg_count.T,
        ray_code, sample_code, w_hidden, w_feat, w_density,
    )
    block_a = lax.all_to_all(packed, "region", 0, 0, axis_index_groups=same_core, tiled=True)
    block_b = lax.ppermute(block_a, "region", inner)

    target_t = target.T
    first, last = target_t[:, :IW], target_t[:, rays - IW :]
    target_in = lax.ppermute(jnp.where(core == 0, last, first), "region", inner)
    target_cr = lax.ppermute(jnp.where(core == 0, first, last), "region", cross)

    image, a, table, att_hw, weight, passing, slope, att, rel, codes = pl.pallas_call(
        functools.partial(forward_kernel, half, group, room),
        out_shape=(
            jax.ShapeDtypeStruct((feat_width, rays), BF16),
            jax.ShapeDtypeStruct((tiles, hid_width, LANES), F32),
            jax.ShapeDtypeStruct((samples + 1, 2 * regions, hid_width), BF16),
            jax.ShapeDtypeStruct((tiles, hid_width, LANES), F32),
            jax.ShapeDtypeStruct((tiles, samples, LANES), F32),
            jax.ShapeDtypeStruct((tiles, samples, LANES), F32),
            jax.ShapeDtypeStruct((tiles, samples, LANES), F32),
            jax.ShapeDtypeStruct((tiles, 1, LANES), F32),
            jax.ShapeDtypeStruct((segs, rays), jnp.int32),
            jax.ShapeDtypeStruct((rays, code_width), BF16),
        ),
        scratch_shapes=[
            pltpu.VMEM((16, regions * room), F32),
            pltpu.VMEM((samples + 1, regions, hid_width), F32),
            pltpu.VMEM((regions, hid_width, rays), F32),
            pltpu.VMEM((tiles, (samples + 1) * hid_width, LANES), F32),
            pltpu.VMEM((16 * samples, 8, LANES), F32),
            pltpu.VMEM((tiles, 1, LANES), F32),
            pltpu.VMEM((2, 1, LANES), F32),
        ],
        compiler_params=PARAMS,
        name="forward",
    )(block_a, block_b)

    image_in = lax.ppermute(image, "region", inner)
    image_cr = lax.ppermute(image, "region", cross)

    def whole(x):
        return pl.BlockSpec(x.shape, lambda i: (0,) * len(x.shape))

    wf_spec = pl.BlockSpec((half, feat_width, LANES), lambda i: (0, WF_AT // feat_width, 0))
    operands = (
        image, image_in, image_cr, target_t, target_in, target_cr, decoder, decoder.T,
        block_a, block_b, a, table, att_hw, weight, passing, slope, att, rel, codes,
    )
    part = jax.ShapeDtypeStruct((half, PART_ROWS, LANES), BF16)
    mine, other = pl.pallas_call(
        functools.partial(backward_kernel, half),
        out_shape=(part, part),
        grid=(1,),
        out_specs=(whole(part), whole(part)),
        in_specs=[wf_spec if i in (8, 9) else whole(x) for i, x in enumerate(operands)],
        scratch_shapes=[
            pltpu.VMEM((decoder.shape[0], 4 * IW), BF16),
            pltpu.VMEM((regions, hid_width, rays), F32),
            pltpu.VMEM((tiles, hid_width, LANES), F32),
            pltpu.VMEM((tiles, (samples + 1) * hid_width, LANES), F32),
            pltpu.VMEM((16 * samples, 8, LANES), F32),
            pltpu.VMEM((samples, hid_width, lanes), BF16),
            pltpu.VMEM((tiles, hid_width, LANES), F32),
            pltpu.VMEM((hid_width, lanes), BF16),
            pltpu.VMEM((regions, PART_ROWS - G2_AT, hid_width), F32),
            pltpu.VMEM((tiles, 1, LANES), F32),
        ],
        compiler_params=PARAMS,
        name="backward",
    )(*operands)

    theirs = lax.ppermute(other, "region", inner)
    chip = (mine.astype(F32) + theirs.astype(F32)).astype(BF16)
    parts = lax.all_to_all(chip, "region", 0, 0, axis_index_groups=same_core, tiled=True)
    return pl.pallas_call(
        finish_kernel,
        out_shape=(
            jax.ShapeDtypeStruct((1, code_width, hid_width), F32),
            jax.ShapeDtypeStruct((1, hid_width, feat_width), F32),
            jax.ShapeDtypeStruct((1, hid_width), F32),
            jax.ShapeDtypeStruct((1, samples, code_width), F32),
        ),
        compiler_params=PARAMS,
        name="finish",
    )(parts, sample_code, w_hidden)


def solution(mesh):
    in_specs = (
        P(("groups", "region"), None),
        P(("groups", "region"), None),
        P(("groups", "region"), None),
        P(("groups", "region")),
        P("region", None, None),
        P("region", None, None),
        P("region", None, None),
        P("region", None),
        P(),
        P(("groups", "region"), None),
    )
    out_specs = (
        P("region", "groups", None),
        P("region", "groups", None),
        P("region", "groups"),
        P("region", "groups", None),
    )
    return jax.shard_map(local, mesh=mesh, in_specs=in_specs, out_specs=out_specs, check_vma=False)
```

```python
import functools

import jax
import jax.numpy as jnp
from jax import lax
from jax.experimental import pallas as pl
from jax.experimental.pallas import tpu as pltpu
from jax.sharding import PartitionSpec as P

IW = 128
STEP = 0.08
F32 = jnp.float32
BF16 = jnp.bfloat16
LANES = 128

WF_AT = 128
SAMPLE_AT = 192
META_AT = 208
RAYS_AT = 224
G2_AT = 192
DG_AT = 208
PART_ROWS = 216

PARAMS = pltpu.CompilerParams(vmem_limit_bytes=40 << 20)


def iota(shape, dim):
    return lax.broadcasted_iota(jnp.int32, shape, dim)


def dot(lhs, rhs, left=1, right=0):
    return lax.dot_general(lhs, rhs, (((left,), (right,)), ((), ())), preferred_element_type=F32)


def split(values):
    high = values.astype(BF16)
    return high, (values - high.astype(F32)).astype(BF16)


def running_sum(values):
    rows = values.shape[0]
    row = iota(values.shape, 0)
    step = 1
    while step < rows:
        values = values + jnp.where(row >= step, pltpu.roll(values, step, 0), 0.0)
        step *= 2
    return values


def pack_kernel(half, group, room, *refs):
    hbm, blocks, halos, held, sems = refs[:9], refs[9 : 9 + half], refs[9 + half : 11 + half], refs[11 + half : 19 + half], refs[19 + half]
    meta_ref, codes_ref = refs[20 + half :]
    me = lax.axis_index("region")
    core = me & 1
    mine = lax.shift_right_logical(me, 1)
    copies = [pltpu.make_async_copy(hbm[i], held[i], sems.at[i]) for i in range(8)]
    target, width = hbm[8], halos[0].shape[0]
    inward = pl.multiple_of((1 - core) * width, width)
    outward = pl.multiple_of(core * width, width)
    copies.append(pltpu.make_async_copy(target.at[pl.ds(inward, width)], halos[0], sems.at[8]))
    copies.append(pltpu.make_async_copy(target.at[pl.ds(outward, width)], halos[1], sems.at[9]))
    for copy in copies:
        copy.start()
    for copy in copies[:8]:
        copy.wait()
    pix_ref, reg_ref, cnt_ref, code_ref, samp_ref, wh_ref, wf_ref, wd_ref = held
    rays = code_ref.shape[0]
    regions = 2 * half
    shift = rays.bit_length() - 1
    pix = pix_ref[...]
    tile = lax.shift_right_logical(pix, shift)
    spot = pix & (rays - 1)
    same = jnp.where(iota((regions, rays), 0) == tile, 1.0, 0.0)
    earlier = jnp.where(iota((rays, rays), 0) < iota((rays, rays), 1), 1.0, 0.0).astype(BF16)
    counts = dot(same.astype(BF16), earlier)
    rank = jnp.sum(counts * same, axis=0, keepdims=True).astype(jnp.int32)
    row_place = lax.shift_right_logical(tile, 1) * room + (tile & 1) * group + rank
    lane_place = tile * group + rank
    meta_ref[...] = jnp.zeros(meta_ref.shape, F32)
    meta_ref[1:2, :] = spot.astype(F32)
    meta_ref[2:6, :] = reg_ref[...].astype(F32)
    meta_ref[6:10, :] = cnt_ref[...].astype(F32)
    row_hot = jnp.where(iota((half * room, rays), 0) == row_place, 1.0, 0.0).astype(BF16)
    codes_ref[...] = dot(row_hot, code_ref[...]).astype(BF16)
    lane_hot = jnp.where(iota((rays, rays), 0) == lane_place, 1.0, 0.0).astype(BF16)
    meta = dot(meta_ref[...].astype(BF16), lane_hot, 1, 1)
    wh_t = wh_ref[0].astype(F32).T.astype(BF16)
    density = wd_ref[...].astype(F32)
    first = iota((16, LANES), 0) == 0
    for k, out_ref in enumerate(blocks):
        chip = jnp.bitwise_xor(mine, k)
        out_ref[0:WF_AT] = wh_t
        out_ref[WF_AT:SAMPLE_AT] = wf_ref[0]
        out_ref[SAMPLE_AT:META_AT] = samp_ref[0]
        here = pltpu.roll(meta, (rays - chip * 2 * group) & (rays - 1), 1)[:, :LANES]
        out_ref[META_AT:RAYS_AT] = jnp.where(first, density, here).astype(BF16)
        out_ref[RAYS_AT : RAYS_AT + room] = codes_ref[pl.ds(pl.multiple_of(chip * room, 16), room), :]
    for copy in copies[8:]:
        copy.wait()


def bits_of(row, regions):
    count = regions.bit_length() - 1
    row = jnp.broadcast_to(row, (8, LANES))
    return [(lax.shift_right_logical(row, b) & 1) == 1 for b in range(count)]


def choose(values, bits):
    for bit in bits:
        values = [jnp.where(bit, values[i + 1], values[i]) for i in range(0, len(values), 2)]
    return values[0]


def seg_hot(wanted, regions):
    return jnp.concatenate(
        [jnp.where(iota((regions, row.shape[1]), 0) == row, 1.0, 0.0) for row in wanted], axis=1
    )


def forward_kernel(half, group, room, *refs):
    regions = 2 * half
    blocks = refs[:regions]
    (
        image_ref, h_ref, wd_ref, att_hw_ref, wide_hw_ref, weight_ref, pass_ref, slope_ref, att_ref, rel_ref, codes_ref, wf_out,
        meta_ref, plain_ref, table_ref, proj_ref, a_ref, picked_ref, row_ref, ahead_ref,
    ) = refs[regions:]
    rays = codes_ref.shape[1]
    segs = rel_ref.shape[0]
    samples = weight_ref.shape[1]
    feats = image_ref.shape[0]
    me = lax.axis_index("region")
    core = me & 1
    chip = lax.shift_right_logical(me, 1)
    per_tile = LANES // room
    lane = iota((16, LANES), 1)
    chunk = lax.div(lane, room)
    inside = lane - chunk * room
    mine = (inside < 2 * group) & (lax.div(inside, group) == core)
    for tile in range(regions // per_tile):
        total = jnp.zeros((16, LANES), F32)
        for spot in range(per_tile):
            block = blocks[tile * per_tile + spot][META_AT:RAYS_AT].astype(F32)
            total = jnp.where(chunk == spot, pltpu.roll(block, spot * room, 1), total)
        meta_ref[:, tile * LANES : (tile + 1) * LANES] = jnp.where(mine, total, -1.0)
    meta_src = meta_ref[...]
    places = regions * room
    to_pixel = jnp.where(
        iota((rays, places), 0).astype(F32) == meta_src[1:2, :], 1.0, 0.0
    ).astype(BF16)
    sources = jnp.concatenate([block[RAYS_AT : RAYS_AT + room] for block in blocks], axis=0)
    codes_t = dot(to_pixel, sources).T.astype(BF16)
    codes_ref[...] = codes_t
    meta = dot(meta_src.astype(BF16), to_pixel, 1, 1)
    region = meta[2 : 2 + segs].astype(jnp.int32)
    rel = jnp.bitwise_xor(region & 1, core) * half + jnp.bitwise_xor(lax.shift_right_logical(region, 1), chip)
    rel_ref[...] = rel
    for k in range(segs):
        for part in range(2):
            row_ref[2 * k + part] = meta[6 + k : 7 + k, part * LANES : (part + 1) * LANES]
    wanted = [rel_ref[k : k + 1, :] for k in range(segs)]
    for r, block in enumerate(blocks):
        w_t = block[0:WF_AT]
        proj_ref[r] = dot(w_t, codes_t)
        plain_ref[0:samples, r, :] = dot(block[SAMPLE_AT:META_AT], w_t, 1, 1)
        plain_ref[samples, r : r + 1, :] = block[META_AT:RAYS_AT].astype(F32)[0:1, :]
        wf_out[r * feats : (r + 1) * feats] = block[WF_AT:SAMPLE_AT]
    for s in range(samples + 1):
        high, low = split(plain_ref[s])
        table_ref[s] = jnp.concatenate([high.astype(F32), low.astype(F32)], axis=0).T.astype(BF16)
    for part in range(2):
        lanes = slice(part * LANES, (part + 1) * LANES)

        def pick_rows(index, carry):
            rows = pl.ds(pl.multiple_of(index * 8, 8), 8)
            bits = [bits_of(row[:, lanes], regions) for row in wanted]
            values = [proj_ref[r, rows, lanes] for r in range(regions)]
            for k in range(segs):
                a_ref[2 * k + part, rows, :] = choose(values, bits[k])
            return carry

        lax.fori_loop(0, 16, pick_rows, 0)
    hot = seg_hot(wanted, regions).astype(BF16)
    hot2 = jnp.concatenate([hot, hot], axis=0)
    for tile in range(2 * segs):
        picked_ref[tile] = hot2[:, tile * LANES : (tile + 1) * LANES]
    ahead_ref[...] = jnp.zeros(ahead_ref.shape, F32)
    order = iota((samples, LANES), 0).astype(F32)

    def step(tile, carry):
        here = picked_ref[tile]
        wd = dot(table_ref[samples], here)
        wd_ref[tile] = wd
        sums = []
        for s in range(samples):
            h = jnp.maximum(a_ref[tile] + dot(table_ref[s], here), 0.0)
            h_ref[tile, s] = h
            sums.append(jnp.sum(h * wd_ref[tile], axis=0, keepdims=True))
        density = jnp.concatenate(sums, axis=0)
        part = tile & 1
        live = order < row_ref[tile]
        soft = jnp.maximum(density, 0.0) + jnp.log1p(jnp.exp(-jnp.abs(density)))
        thick = jnp.where(live, STEP * soft, 0.0)
        through = running_sum(thick)
        passing = jnp.exp(-(through - thick))
        keeping = jnp.exp(-thick)
        weight = passing * (1.0 - keeping)
        weight_ref[tile] = weight
        pass_ref[tile] = passing * keeping
        slope_ref[tile] = jnp.where(live, STEP / (1.0 + jnp.exp(-density)), 0.0)
        before = ahead_ref[part]
        att = jnp.exp(-before)
        ahead_ref[part] = before + through[samples - 1 : samples, :]
        att_ref[tile] = att
        scale = [jnp.broadcast_to(weight[s : s + 1, :] * att, (8, LANES)) for s in range(samples)]
        lanes = pl.ds(pl.multiple_of(tile * LANES, LANES), LANES)
        for pair in range(8):
            both = []
            for ht in (2 * pair, 2 * pair + 1):
                rows = slice(ht * 8, ht * 8 + 8)
                total = scale[0] * h_ref[tile, 0, rows, :]
                for s in range(1, samples):
                    total = total + scale[s] * h_ref[tile, s, rows, :]
                att_hw_ref[tile, rows, :] = total
                both.append(total)
            wide_hw_ref[pair * 16 : pair * 16 + 16, lanes] = jnp.concatenate(both, axis=0).astype(BF16)
        return carry

    lax.fori_loop(0, 2 * segs, step, 0)
    wf_twice = jnp.concatenate([wf_out[...], wf_out[...]], axis=1)
    for part in range(2):
        feat = [jnp.zeros((8, LANES), F32)] * (feats // 8)
        for k in range(segs):
            tile = 2 * k + part
            high, low = split(att_hw_ref[tile])
            proj_ref[0 : regions * feats // LANES, :, 0:LANES] = dot(wf_twice, jnp.concatenate([high, low], axis=0)).reshape(
                regions * feats // LANES, LANES, LANES
            )
            bits = bits_of(wanted[k][:, part * LANES : (part + 1) * LANES], regions)
            for ft in range(feats // 8):
                values = []
                for r in range(regions):
                    at = r * feats + ft * 8
                    values.append(proj_ref[at // LANES, at % LANES : at % LANES + 8, 0:LANES])
                feat[ft] = feat[ft] + choose(values, bits)
        image_ref[:, part * LANES : (part + 1) * LANES] = jnp.concatenate(feat, axis=0).astype(BF16)


def shifted(values, by):
    lane = iota(values.shape, 1)
    if by == 0:
        return values
    if by > 0:
        return jnp.where(lane == 0, 0.0, pltpu.roll(values, 1, 1))
    return jnp.where(lane == LANES - 1, 0.0, pltpu.roll(values, LANES - 1, 1))


def backward_kernel(
    half, own_ref, inner_ref, cross_ref, tgt_ref, tin_ref, tcr_ref, dec_ref, dect_ref,
    h_in, wd_ref, att_hw_ref, wide_hw_ref, weight_ref, pass_ref, slope_ref, att_ref, rel_ref, codes_ref, wf_ref,
    mine_ref, other_ref,
    patch_ref, masked_ref, q_ref, gp_ref, g1_ref, hd_ref, tail_ref, row_ref,
):
    regions = 2 * half
    feats, rays = own_ref.shape
    segs = rel_ref.shape[0]
    samples = weight_ref.shape[1]
    me = lax.axis_index("region")
    core = me & 1
    own = own_ref[...].astype(F32)
    inner = inner_ref[...].astype(F32)
    cross = cross_ref[...].astype(F32)
    top = jnp.where(core == 0, cross, inner)
    bottom = jnp.where(core == 0, inner, cross)
    rows = [v[:, i * IW : (i + 1) * IW] for v in (top, own, bottom) for i in range(2)]
    for at, row in enumerate(rows):
        for dx in range(3):
            piece = shifted(row, 1 - dx).astype(BF16)
            for dy in range(3):
                if 0 <= at - dy < 4:
                    patch_ref[(3 * dy + dx) * feats : (3 * dy + dx + 1) * feats, (at - dy) * IW : (at - dy + 1) * IW] = piece
    tin = tin_ref[...].astype(F32)
    tcr = tcr_ref[...].astype(F32)
    t_top = jnp.where(core == 0, tcr, tin)
    t_bottom = jnp.where(core == 0, tin, tcr)
    decoded = dot(dect_ref[...], patch_ref[...])
    tgt = tgt_ref[...].astype(F32)
    g_top = jnp.where(me > 0, decoded[:, 0:IW] - t_top, 0.0)
    g_own = decoded[:, IW : 3 * IW] - tgt
    g_bottom = jnp.where(me < regions - 1, decoded[:, 3 * IW :] - t_bottom, 0.0)
    grad_dec = jnp.concatenate([g_top, g_own, g_bottom], axis=1).astype(BF16)
    grad_patch = dot(dec_ref[...], grad_dec)
    image_rows = []
    for i in range(2):
        total = jnp.zeros((feats, IW), F32)
        for dx in range(3):
            term = jnp.zeros((feats, IW), F32)
            for dy in range(3):
                at = (3 * dy + dx) * feats
                term = term + grad_patch[at : at + feats, (i - dy + 2) * IW : (i - dy + 3) * IW]
            total = total + shifted(term, dx - 1)
        image_rows.append(total)
    grad_ray = jnp.concatenate(image_rows, axis=1)
    wanted = [rel_ref[k : k + 1, :] for k in range(segs)]
    for r in range(regions):
        for k in range(segs):
            masked = jnp.where(wanted[k] == r, grad_ray, 0.0).astype(BF16)
            masked_ref[r * feats : (r + 1) * feats, k * rays : (k + 1) * rays] = masked
    raw = dot(wf_ref[...], masked_ref[...], 0, 0)
    for tile in range(2 * segs):
        q_ref[tile] = raw[:, tile * LANES : (tile + 1) * LANES]
    feat_grad = dot(masked_ref[...], wide_hw_ref[...], 1, 1).astype(BF16)
    for r in range(regions):
        out, to = (mine_ref, r) if r < half else (other_ref, r - half)
        out[to, WF_AT:G2_AT] = feat_grad[r * feats : (r + 1) * feats]
    hot = seg_hot(wanted, regions).astype(BF16)
    for part in range(2):
        later = jnp.zeros((1, LANES), F32)
        for k in reversed(range(segs)):
            row_ref[2 * k + part] = -later
            pulled = jnp.sum(att_hw_ref[2 * k + part] * q_ref[2 * k + part], axis=0, keepdims=True)
            later = later + pulled

    def step(tile, carry):
        att = jnp.broadcast_to(att_ref[tile], (8, LANES))
        sums = [jnp.zeros((8, LANES), F32)] * samples
        for ht in range(16):
            rows = slice(ht * 8, ht * 8 + 8)
            q = q_ref[tile, rows, :] * att
            q_ref[tile, rows, :] = q
            for s in range(samples):
                sums[s] = sums[s] + h_in[tile, s, rows, :] * q
        along = jnp.concatenate([jnp.sum(v, axis=0, keepdims=True) for v in sums], axis=0)
        weight = weight_ref[tile]
        through = running_sum(along * weight)
        later = through[samples - 1 : samples, :] - through
        grad_thick = row_ref[tile] + along * pass_ref[tile] - later
        grad_density = (grad_thick * slope_ref[tile]).astype(BF16).astype(F32)
        scale = [jnp.broadcast_to(weight[s : s + 1, :], (8, LANES)) for s in range(samples)]
        slant = [jnp.broadcast_to(grad_density[s : s + 1, :], (8, LANES)) for s in range(samples)]
        lanes = pl.ds(pl.multiple_of(tile * LANES, LANES), LANES)
        for pair in range(8):
            at = [slice((2 * pair + u) * 8, (2 * pair + u) * 8 + 8) for u in range(2)]
            q = [q_ref[tile, rows, :] for rows in at]
            wd = [wd_ref[tile, rows, :] for rows in at]
            g1 = [jnp.zeros((8, LANES), F32)] * 2
            hd = [jnp.zeros((8, LANES), F32)] * 2
            for s in range(samples):
                both = []
                for u in range(2):
                    h = h_in[tile, s, at[u], :]
                    gp = jnp.where(h > 0.0, scale[s] * q[u] + slant[s] * wd[u], 0.0)
                    g1[u] = g1[u] + gp
                    hd[u] = hd[u] + slant[s] * h
                    both.append(gp)
                gp_ref[s, 16 * pair : 16 * pair + 16, lanes] = jnp.concatenate(both, axis=0).astype(BF16)
            g1_ref[16 * pair : 16 * pair + 16, lanes] = jnp.concatenate(g1, axis=0).astype(BF16)
            hd_ref[16 * pair : 16 * pair + 16, lanes] = jnp.concatenate(hd, axis=0).astype(BF16)
        return carry

    lax.fori_loop(0, 2 * segs, step, 0)
    codes = codes_ref[...].astype(F32)
    tail_ref[...] = jnp.zeros(tail_ref.shape, F32)
    for s in range(samples):
        tail_ref[:, s, :] = dot(hot, gp_ref[s], 1, 1)
    tail_ref[:, samples, :] = dot(hot, hd_ref[...], 1, 1)
    g1 = g1_ref[...]
    for r in range(regions):
        out, to = (mine_ref, r) if r < half else (other_ref, r - half)
        held = jnp.concatenate([jnp.where(row == r, codes, 0.0).astype(BF16) for row in wanted], axis=1)
        out[to, 0:WF_AT] = dot(held, g1, 1, 1).astype(BF16)
        out[to, G2_AT:PART_ROWS] = tail_ref[r].astype(BF16)


def merge_kernel(mine_ref, theirs_ref, *outs):
    for k, out in enumerate(outs):
        out[...] = (mine_ref[k].astype(F32) + theirs_ref[k].astype(F32)).astype(BF16)


def finish_kernel(*refs):
    parts, (samp_ref, wh_ref, hid_ref, feat_ref, dens_ref, code_ref) = refs[:-6], refs[-6:]
    total = parts[0][...].astype(F32)
    for part in parts[1:]:
        total = total + part[...].astype(F32)
    high, low = split(total[G2_AT:DG_AT])
    samples = samp_ref[0]
    wh = wh_ref[0]
    hid_ref[0] = total[0:WF_AT] + dot(samples, high, 0, 0) + dot(samples, low, 0, 0)
    feat_ref[0] = total[WF_AT:G2_AT]
    dens_ref[...] = total[DG_AT : DG_AT + 1]
    code_ref[0] = dot(high, wh, 1, 1) + dot(low, wh, 1, 1)


def local(ray_code, seg_region, seg_count, pixel_of_ray, sample_code, w_hidden, w_feat, w_density, decoder, target):
    regions = lax.axis_size("region")
    half = regions // 2
    rays, segs = seg_region.shape
    code_width = ray_code.shape[1]
    hid_width = w_hidden.shape[2]
    feat_width = w_feat.shape[2]
    dino_width = target.shape[1]
    samples = sample_code.shape[1]
    group = rays // regions
    room = max(16, 2 * group)
    tiles = 2 * segs
    lanes = segs * rays
    inner = [(i, i ^ 1) for i in range(regions)]
    cross = [(i, i + 1) for i in range(1, regions - 1, 2)] + [(i + 1, i) for i in range(1, regions - 1, 2)]

    def shape(*dims, kind=F32):
        return jax.ShapeDtypeStruct(dims, kind)

    def to_chips(blocks):
        return [blocks[0]] + [
            lax.ppermute(blocks[k], "region", [(i, i ^ (2 * k)) for i in range(regions)]) for k in range(1, half)
        ]

    pack_args = (
        pixel_of_ray.reshape(1, rays), seg_region.T, seg_count.T,
        ray_code, sample_code, w_hidden, w_feat.swapaxes(1, 2), w_density, target,
    )
    outs = pl.pallas_call(
        functools.partial(pack_kernel, half, group, room),
        out_shape=[shape(RAYS_AT + room, LANES, kind=BF16)] * half + [shape(IW, dino_width, kind=BF16)] * 2,
        in_specs=[pl.BlockSpec(memory_space=pltpu.HBM)] * 9,
        scratch_shapes=[pltpu.VMEM(x.shape, x.dtype) for x in pack_args[:8]]
        + [
            pltpu.SemaphoreType.DMA((10,)),
            pltpu.VMEM((16, rays), F32),
            pltpu.VMEM((half * room, LANES), BF16),
        ],
        compiler_params=PARAMS,
        name="pack",
    )(*pack_args)
    blocks = to_chips(outs[:half])
    blocks = blocks + [lax.ppermute(block, "region", inner) for block in blocks]
    target_in = lax.ppermute(outs[half], "region", inner)
    target_cr = lax.ppermute(outs[half + 1], "region", cross)

    image, *kept = pl.pallas_call(
        functools.partial(forward_kernel, half, group, room),
        out_shape=(
            shape(feat_width, rays, kind=BF16),
            shape(tiles, samples, hid_width, LANES),
            shape(tiles, hid_width, LANES),
            shape(tiles, hid_width, LANES),
            shape(hid_width, lanes, kind=BF16),
            shape(tiles, samples, LANES),
            shape(tiles, samples, LANES),
            shape(tiles, samples, LANES),
            shape(tiles, 1, LANES),
            shape(segs, rays, kind=jnp.int32),
            shape(code_width, rays, kind=BF16),
            shape(regions * feat_width, hid_width, kind=BF16),
        ),
        scratch_shapes=[
            pltpu.VMEM((16, regions * room), F32),
            pltpu.VMEM((samples + 1, regions, hid_width), F32),
            pltpu.VMEM((samples + 1, hid_width, 2 * regions), BF16),
            pltpu.VMEM((regions, hid_width, rays), F32),
            pltpu.VMEM((tiles, hid_width, LANES), F32),
            pltpu.VMEM((tiles, 2 * regions, LANES), BF16),
            pltpu.VMEM((tiles, 1, LANES), F32),
            pltpu.VMEM((2, 1, LANES), F32),
        ],
        compiler_params=PARAMS,
        name="forward",
    )(*blocks)

    image_in = lax.ppermute(image, "region", inner)
    image_cr = lax.ppermute(image, "region", cross)

    part = shape(half, PART_ROWS, LANES, kind=BF16)
    mine, other = pl.pallas_call(
        functools.partial(backward_kernel, half),
        out_shape=(part, part),
        scratch_shapes=[
            pltpu.VMEM((decoder.shape[0], 4 * IW), BF16),
            pltpu.VMEM((regions * feat_width, lanes), BF16),
            pltpu.VMEM((tiles, hid_width, LANES), F32),
            pltpu.VMEM((samples, hid_width, lanes), BF16),
            pltpu.VMEM((hid_width, lanes), BF16),
            pltpu.VMEM((hid_width, lanes), BF16),
            pltpu.VMEM((regions, PART_ROWS - G2_AT, hid_width), F32),
            pltpu.VMEM((tiles, 1, LANES), F32),
        ],
        compiler_params=PARAMS,
        name="backward",
    )(image, image_in, image_cr, target.T, target_in.T, target_cr.T, decoder, decoder.T, *kept)

    theirs = lax.ppermute(other, "region", inner)
    chip = pl.pallas_call(
        merge_kernel,
        out_shape=[shape(PART_ROWS, LANES, kind=BF16)] * half,
        compiler_params=PARAMS,
        name="merge",
    )(mine, theirs)
    hid_grad, feat_grad, dens_grad, code_grad = pl.pallas_call(
        finish_kernel,
        out_shape=(
            shape(1, code_width, hid_width),
            shape(1, feat_width, hid_width),
            shape(1, hid_width),
            shape(1, samples, code_width),
        ),
        compiler_params=PARAMS,
        name="finish",
    )(*to_chips(chip), sample_code, w_hidden)
    return hid_grad, feat_grad.swapaxes(1, 2), dens_grad, code_grad


def solution(mesh):
    in_specs = (
        P(("groups", "region"), None),
        P(("groups", "region"), None),
        P(("groups", "region"), None),
        P(("groups", "region")),
        P("region", None, None),
        P("region", None, None),
        P("region", None, None),
        P("region", None),
        P(),
        P(("groups", "region"), None),
    )
    out_specs = (
        P("region", "groups", None),
        P("region", "groups", None),
        P("region", "groups"),
        P("region", "groups", None),
    )
    return jax.shard_map(local, mesh=mesh, in_specs=in_specs, out_specs=out_specs, check_vma=False)
```

```python
import functools

import jax
import jax.numpy as jnp
from jax import lax
from jax.experimental import pallas as pl
from jax.experimental.pallas import tpu as pltpu
from jax.sharding import PartitionSpec as P

IW = 128
STEP = 0.08
F32 = jnp.float32
BF16 = jnp.bfloat16
LANES = 128

WF_AT = 128
SAMPLE_AT = 192
META_AT = 208
RAYS_AT = 224
G2_AT = 192
DG_AT = 208
PART_ROWS = 216


def grant(mib):
    return pltpu.CompilerParams(vmem_limit_bytes=int(mib * (1 << 20)))


def iota(shape, dim):
    return lax.broadcasted_iota(jnp.int32, shape, dim)


def dot(lhs, rhs, left=1, right=0):
    return lax.dot_general(lhs, rhs, (((left,), (right,)), ((), ())), preferred_element_type=F32)


def split(values):
    high = values.astype(BF16)
    return high, (values - high.astype(F32)).astype(BF16)


def running_sum(values):
    rows = values.shape[0]
    row = iota(values.shape, 0)
    step = 1
    while step < rows:
        values = values + jnp.where(row >= step, pltpu.roll(values, step, 0), 0.0)
        step *= 2
    return values


def pack_kernel(half, group, room, *refs):
    hbm, blocks, held, sems = refs[:8], refs[8 : 8 + half], refs[8 + half : 16 + half], refs[16 + half]
    meta_ref, codes_ref = refs[17 + half :]
    me = lax.axis_index("region")
    mine = lax.shift_right_logical(me, 1)
    copies = [pltpu.make_async_copy(hbm[i], held[i], sems.at[i]) for i in range(8)]
    for copy in copies:
        copy.start()
    for copy in copies:
        copy.wait()
    pix_ref, reg_ref, cnt_ref, code_ref, samp_ref, wh_ref, wf_ref, wd_ref = held
    rays = code_ref.shape[0]
    regions = 2 * half
    shift = rays.bit_length() - 1
    pix = pix_ref[...]
    tile = lax.shift_right_logical(pix, shift)
    spot = pix & (rays - 1)
    same = jnp.where(iota((regions, rays), 0) == tile, 1.0, 0.0)
    earlier = jnp.where(iota((rays, rays), 0) < iota((rays, rays), 1), 1.0, 0.0).astype(BF16)
    counts = dot(same.astype(BF16), earlier)
    rank = jnp.sum(counts * same, axis=0, keepdims=True).astype(jnp.int32)
    row_place = lax.shift_right_logical(tile, 1) * room + (tile & 1) * group + rank
    lane_place = tile * group + rank
    meta_ref[...] = jnp.zeros(meta_ref.shape, F32)
    meta_ref[1:2, :] = spot.astype(F32)
    meta_ref[2:6, :] = reg_ref[...].astype(F32)
    meta_ref[6:10, :] = cnt_ref[...].astype(F32)
    row_hot = jnp.where(iota((half * room, rays), 0) == row_place, 1.0, 0.0).astype(BF16)
    codes_ref[...] = dot(row_hot, code_ref[...]).astype(BF16)
    lane_hot = jnp.where(iota((rays, rays), 0) == lane_place, 1.0, 0.0).astype(BF16)
    meta = dot(meta_ref[...].astype(BF16), lane_hot, 1, 1)
    wh_t = wh_ref[0].astype(F32).T.astype(BF16)
    density = wd_ref[...].astype(F32)
    first = iota((16, LANES), 0) == 0
    for k, out_ref in enumerate(blocks):
        chip = jnp.bitwise_xor(mine, k)
        out_ref[0:WF_AT] = wh_t
        out_ref[WF_AT:SAMPLE_AT] = wf_ref[0]
        out_ref[SAMPLE_AT:META_AT] = samp_ref[0]
        here = pltpu.roll(meta, (rays - chip * 2 * group) & (rays - 1), 1)[:, :LANES]
        out_ref[META_AT:RAYS_AT] = jnp.where(first, density, here).astype(BF16)
        out_ref[RAYS_AT : RAYS_AT + room] = codes_ref[pl.ds(pl.multiple_of(chip * room, 16), room), :]


def bits_of(row, regions):
    count = regions.bit_length() - 1
    row = jnp.broadcast_to(row, (8, LANES))
    return [(lax.shift_right_logical(row, b) & 1) == 1 for b in range(count)]


def choose(values, bits):
    for bit in bits:
        values = [jnp.where(bit, values[i + 1], values[i]) for i in range(0, len(values), 2)]
    return values[0]


def seg_hot(wanted, regions):
    return jnp.concatenate(
        [jnp.where(iota((regions, row.shape[1]), 0) == row, 1.0, 0.0) for row in wanted], axis=1
    )


def forward_kernel(half, group, room, *refs):
    regions = 2 * half
    blocks, target_ref = refs[:regions], refs[regions]
    (
        image_ref, halo_in_ref, halo_cr_ref, h_ref, wd_ref, att_hw_ref, wide_hw_ref, weight_ref, pass_ref, slope_ref, att_ref, rel_ref, codes_ref, wf_out,
        meta_ref, plain_ref, table_ref, proj_ref, a_ref, picked_ref, row_ref, ahead_ref,
    ) = refs[regions + 1 :]
    rays = codes_ref.shape[1]
    segs = rel_ref.shape[0]
    samples = weight_ref.shape[1]
    feats = image_ref.shape[0]
    me = lax.axis_index("region")
    core = me & 1
    chip = lax.shift_right_logical(me, 1)
    per_tile = LANES // room
    lane = iota((16, LANES), 1)
    chunk = lax.div(lane, room)
    inside = lane - chunk * room
    mine = (inside < 2 * group) & (lax.div(inside, group) == core)
    for tile in range(regions // per_tile):
        total = jnp.zeros((16, LANES), F32)
        for spot in range(per_tile):
            block = blocks[tile * per_tile + spot][META_AT:RAYS_AT].astype(F32)
            total = jnp.where(chunk == spot, pltpu.roll(block, spot * room, 1), total)
        meta_ref[:, tile * LANES : (tile + 1) * LANES] = jnp.where(mine, total, -1.0)
    meta_src = meta_ref[...]
    places = regions * room
    to_pixel = jnp.where(
        iota((rays, places), 0).astype(F32) == meta_src[1:2, :], 1.0, 0.0
    ).astype(BF16)
    sources = jnp.concatenate([block[RAYS_AT : RAYS_AT + room] for block in blocks], axis=0)
    codes_t = dot(to_pixel, sources).T.astype(BF16)
    codes_ref[...] = codes_t
    meta = dot(meta_src.astype(BF16), to_pixel, 1, 1)
    region = meta[2 : 2 + segs].astype(jnp.int32)
    rel = jnp.bitwise_xor(region & 1, core) * half + jnp.bitwise_xor(lax.shift_right_logical(region, 1), chip)
    rel_ref[...] = rel
    for k in range(segs):
        for part in range(2):
            row_ref[2 * k + part] = meta[6 + k : 7 + k, part * LANES : (part + 1) * LANES]
    wanted = [rel_ref[k : k + 1, :] for k in range(segs)]
    for r, block in enumerate(blocks):
        w_t = block[0:WF_AT]
        proj_ref[r] = dot(w_t, codes_t)
        plain_ref[0:samples, r, :] = dot(block[SAMPLE_AT:META_AT], w_t, 1, 1)
        plain_ref[samples, r : r + 1, :] = block[META_AT:RAYS_AT].astype(F32)[0:1, :]
        wf_out[r * feats : (r + 1) * feats] = block[WF_AT:SAMPLE_AT]
    for s in range(samples + 1):
        high, low = split(plain_ref[s])
        table_ref[s] = jnp.concatenate([high.astype(F32), low.astype(F32)], axis=0).T.astype(BF16)
    for part in range(2):
        lanes = slice(part * LANES, (part + 1) * LANES)

        def pick_rows(index, carry):
            rows = pl.ds(pl.multiple_of(index * 8, 8), 8)
            bits = [bits_of(row[:, lanes], regions) for row in wanted]
            values = [proj_ref[r, rows, lanes] for r in range(regions)]
            for k in range(segs):
                a_ref[2 * k + part, rows, :] = choose(values, bits[k])
            return carry

        lax.fori_loop(0, 16, pick_rows, 0)
    hot = seg_hot(wanted, regions).astype(BF16)
    hot2 = jnp.concatenate([hot, hot], axis=0)
    for tile in range(2 * segs):
        picked_ref[tile] = hot2[:, tile * LANES : (tile + 1) * LANES]
    ahead_ref[...] = jnp.zeros(ahead_ref.shape, F32)
    order = iota((samples, LANES), 0).astype(F32)

    def step(tile, carry):
        here = picked_ref[tile]
        wd = dot(table_ref[samples], here)
        wd_ref[tile] = wd
        sums = []
        for s in range(samples):
            h = jnp.maximum(a_ref[tile] + dot(table_ref[s], here), 0.0)
            h_ref[tile, s] = h
            sums.append(jnp.sum(h * wd_ref[tile], axis=0, keepdims=True))
        density = jnp.concatenate(sums, axis=0)
        part = tile & 1
        live = order < row_ref[tile]
        soft = jnp.maximum(density, 0.0) + jnp.log1p(jnp.exp(-jnp.abs(density)))
        thick = jnp.where(live, STEP * soft, 0.0)
        through = running_sum(thick)
        passing = jnp.exp(-(through - thick))
        keeping = jnp.exp(-thick)
        weight = passing * (1.0 - keeping)
        weight_ref[tile] = weight
        pass_ref[tile] = passing * keeping
        slope_ref[tile] = jnp.where(live, STEP / (1.0 + jnp.exp(-density)), 0.0)
        before = ahead_ref[part]
        att = jnp.exp(-before)
        ahead_ref[part] = before + through[samples - 1 : samples, :]
        att_ref[tile] = att
        scale = [jnp.broadcast_to(weight[s : s + 1, :] * att, (8, LANES)) for s in range(samples)]
        lanes = pl.ds(pl.multiple_of(tile * LANES, LANES), LANES)
        for pair in range(8):
            both = []
            for ht in (2 * pair, 2 * pair + 1):
                rows = slice(ht * 8, ht * 8 + 8)
                total = scale[0] * h_ref[tile, 0, rows, :]
                for s in range(1, samples):
                    total = total + scale[s] * h_ref[tile, s, rows, :]
                att_hw_ref[tile, rows, :] = total
                both.append(total)
            wide_hw_ref[pair * 16 : pair * 16 + 16, lanes] = jnp.concatenate(both, axis=0).astype(BF16)
        return carry

    lax.fori_loop(0, 2 * segs, step, 0)
    wf_twice = jnp.concatenate([wf_out[...], wf_out[...]], axis=1)
    for part in range(2):
        feat = [jnp.zeros((8, LANES), F32)] * (feats // 8)
        for k in range(segs):
            tile = 2 * k + part
            high, low = split(att_hw_ref[tile])
            proj_ref[0 : regions * feats // LANES, :, 0:LANES] = dot(wf_twice, jnp.concatenate([high, low], axis=0)).reshape(
                regions * feats // LANES, LANES, LANES
            )
            bits = bits_of(wanted[k][:, part * LANES : (part + 1) * LANES], regions)
            for ft in range(feats // 8):
                values = []
                for r in range(regions):
                    at = r * feats + ft * 8
                    values.append(proj_ref[at // LANES, at % LANES : at % LANES + 8, 0:LANES])
                feat[ft] = feat[ft] + choose(values, bits)
        image_ref[:, part * LANES : (part + 1) * LANES] = jnp.concatenate(feat, axis=0).astype(BF16)
    near, far = target_ref[:, :IW].astype(F32), target_ref[:, rays - IW :].astype(F32)
    for out_ref, row in ((halo_in_ref, jnp.where(core == 0, far, near)), (halo_cr_ref, jnp.where(core == 0, near, far))):
        out_ref[0:feats] = image_ref[...]
        depth = target_ref.shape[0] // 2
        out_ref[feats:, 0:IW] = row[:depth].astype(BF16)
        out_ref[feats:, rays - IW :] = row[depth:].astype(BF16)


def shifted(values, by):
    lane = iota(values.shape, 1)
    if by == 0:
        return values
    if by > 0:
        return jnp.where(lane == 0, 0.0, pltpu.roll(values, 1, 1))
    return jnp.where(lane == LANES - 1, 0.0, pltpu.roll(values, LANES - 1, 1))


def backward_kernel(
    half, own_ref, inner_ref, cross_ref, tgt_ref, dec_ref, dect_ref,
    h_in, wd_ref, att_hw_ref, wide_hw_ref, weight_ref, pass_ref, slope_ref, att_ref, rel_ref, codes_ref, wf_ref,
    mine_ref, other_ref,
    patch_ref, masked_ref, q_ref, gp_ref, g1_ref, hd_ref, tail_ref, row_ref,
):
    regions = 2 * half
    feats, rays = own_ref.shape
    segs = rel_ref.shape[0]
    samples = weight_ref.shape[1]
    me = lax.axis_index("region")
    core = me & 1
    own = own_ref[...].astype(F32)
    halo_in = inner_ref[...].astype(F32)
    halo_cr = cross_ref[...].astype(F32)
    inner, tin = halo_in[:feats], jnp.concatenate([halo_in[feats:, :IW], halo_in[feats:, rays - IW :]], axis=0)
    cross, tcr = halo_cr[:feats], jnp.concatenate([halo_cr[feats:, :IW], halo_cr[feats:, rays - IW :]], axis=0)
    top = jnp.where(core == 0, cross, inner)
    bottom = jnp.where(core == 0, inner, cross)
    rows = [v[:, i * IW : (i + 1) * IW] for v in (top, own, bottom) for i in range(2)]
    for at, row in enumerate(rows):
        for dx in range(3):
            piece = shifted(row, 1 - dx).astype(BF16)
            for dy in range(3):
                if 0 <= at - dy < 4:
                    patch_ref[(3 * dy + dx) * feats : (3 * dy + dx + 1) * feats, (at - dy) * IW : (at - dy + 1) * IW] = piece
    t_top = jnp.where(core == 0, tcr, tin)
    t_bottom = jnp.where(core == 0, tin, tcr)
    decoded = dot(dect_ref[...], patch_ref[...])
    tgt = tgt_ref[...].astype(F32)
    g_top = jnp.where(me > 0, decoded[:, 0:IW] - t_top, 0.0)
    g_own = decoded[:, IW : 3 * IW] - tgt
    g_bottom = jnp.where(me < regions - 1, decoded[:, 3 * IW :] - t_bottom, 0.0)
    grad_dec = jnp.concatenate([g_top, g_own, g_bottom], axis=1).astype(BF16)
    grad_patch = dot(dec_ref[...], grad_dec)
    image_rows = []
    for i in range(2):
        total = jnp.zeros((feats, IW), F32)
        for dx in range(3):
            term = jnp.zeros((feats, IW), F32)
            for dy in range(3):
                at = (3 * dy + dx) * feats
                term = term + grad_patch[at : at + feats, (i - dy + 2) * IW : (i - dy + 3) * IW]
            total = total + shifted(term, dx - 1)
        image_rows.append(total)
    grad_ray = jnp.concatenate(image_rows, axis=1)
    wanted = [rel_ref[k : k + 1, :] for k in range(segs)]
    for r in range(regions):
        for k in range(segs):
            masked = jnp.where(wanted[k] == r, grad_ray, 0.0).astype(BF16)
            masked_ref[r * feats : (r + 1) * feats, k * rays : (k + 1) * rays] = masked
    raw = dot(wf_ref[...], masked_ref[...], 0, 0)
    for tile in range(2 * segs):
        q_ref[tile] = raw[:, tile * LANES : (tile + 1) * LANES]
    feat_grad = dot(masked_ref[...], wide_hw_ref[...], 1, 1).astype(BF16)
    for r in range(regions):
        out, to = (mine_ref, r) if r < half else (other_ref, r - half)
        out[to, WF_AT:G2_AT] = feat_grad[r * feats : (r + 1) * feats]
    hot = seg_hot(wanted, regions).astype(BF16)
    for part in range(2):
        later = jnp.zeros((1, LANES), F32)
        for k in reversed(range(segs)):
            row_ref[2 * k + part] = -later
            pulled = jnp.sum(att_hw_ref[2 * k + part] * q_ref[2 * k + part], axis=0, keepdims=True)
            later = later + pulled

    def step(tile, carry):
        att = jnp.broadcast_to(att_ref[tile], (8, LANES))
        sums = [jnp.zeros((8, LANES), F32)] * samples
        for ht in range(16):
            rows = slice(ht * 8, ht * 8 + 8)
            q = q_ref[tile, rows, :] * att
            q_ref[tile, rows, :] = q
            for s in range(samples):
                sums[s] = sums[s] + h_in[tile, s, rows, :] * q
        along = jnp.concatenate([jnp.sum(v, axis=0, keepdims=True) for v in sums], axis=0)
        weight = weight_ref[tile]
        through = running_sum(along * weight)
        later = through[samples - 1 : samples, :] - through
        grad_thick = row_ref[tile] + along * pass_ref[tile] - later
        grad_density = (grad_thick * slope_ref[tile]).astype(BF16).astype(F32)
        scale = [jnp.broadcast_to(weight[s : s + 1, :], (8, LANES)) for s in range(samples)]
        slant = [jnp.broadcast_to(grad_density[s : s + 1, :], (8, LANES)) for s in range(samples)]
        lanes = pl.ds(pl.multiple_of(tile * LANES, LANES), LANES)
        for pair in range(8):
            at = [slice((2 * pair + u) * 8, (2 * pair + u) * 8 + 8) for u in range(2)]
            q = [q_ref[tile, rows, :] for rows in at]
            wd = [wd_ref[tile, rows, :] for rows in at]
            g1 = [jnp.zeros((8, LANES), F32)] * 2
            hd = [jnp.zeros((8, LANES), F32)] * 2
            for s in range(samples):
                both = []
                for u in range(2):
                    h = h_in[tile, s, at[u], :]
                    gp = jnp.where(h > 0.0, scale[s] * q[u] + slant[s] * wd[u], 0.0)
                    g1[u] = g1[u] + gp
                    hd[u] = hd[u] + slant[s] * h
                    both.append(gp)
                gp_ref[s, 16 * pair : 16 * pair + 16, lanes] = jnp.concatenate(both, axis=0).astype(BF16)
            g1_ref[16 * pair : 16 * pair + 16, lanes] = jnp.concatenate(g1, axis=0).astype(BF16)
            hd_ref[16 * pair : 16 * pair + 16, lanes] = jnp.concatenate(hd, axis=0).astype(BF16)
        return carry

    lax.fori_loop(0, 2 * segs, step, 0)
    codes = codes_ref[...].astype(F32)
    tail_ref[...] = jnp.zeros(tail_ref.shape, F32)
    for s in range(samples):
        tail_ref[:, s, :] = dot(hot, gp_ref[s], 1, 1)
    tail_ref[:, samples, :] = dot(hot, hd_ref[...], 1, 1)
    g1 = g1_ref[...]
    for r in range(regions):
        out, to = (mine_ref, r) if r < half else (other_ref, r - half)
        held = jnp.concatenate([jnp.where(row == r, codes, 0.0).astype(BF16) for row in wanted], axis=1)
        out[to, 0:WF_AT] = dot(held, g1, 1, 1).astype(BF16)
        out[to, G2_AT:PART_ROWS] = tail_ref[r].astype(BF16)


def flip_kernel(target_ref, decoder_ref, block_ref, target_out, decoder_out, same_out, block_out):
    block_out[...] = block_ref[...]
    same_out[...] = decoder_ref[...]
    target_out[...] = target_ref[...].astype(F32).T.astype(BF16)
    decoder_out[...] = decoder_ref[...].astype(F32).T.astype(BF16)


def merge_kernel(mine_ref, theirs_ref, *outs):
    for k, out in enumerate(outs):
        out[...] = (mine_ref[k].astype(F32) + theirs_ref[k].astype(F32)).astype(BF16)


def finish_kernel(*refs):
    parts, (samp_ref, wh_ref, hid_ref, feat_ref, dens_ref, code_ref) = refs[:-6], refs[-6:]
    total = parts[0][...].astype(F32)
    for part in parts[1:]:
        total = total + part[...].astype(F32)
    high, low = split(total[G2_AT:DG_AT])
    samples = samp_ref[0]
    wh = wh_ref[0]
    hid_ref[0] = total[0:WF_AT] + dot(samples, high, 0, 0) + dot(samples, low, 0, 0)
    feat_ref[0] = total[WF_AT:G2_AT]
    dens_ref[...] = total[DG_AT : DG_AT + 1]
    code_ref[0] = dot(high, wh, 1, 1) + dot(low, wh, 1, 1)


def local(ray_code, seg_region, seg_count, pixel_of_ray, sample_code, w_hidden, w_feat, w_density, decoder, target):
    regions = lax.axis_size("region")
    half = regions // 2
    rays, segs = seg_region.shape
    code_width = ray_code.shape[1]
    hid_width = w_hidden.shape[2]
    feat_width = w_feat.shape[2]
    dino_width = target.shape[1]
    samples = sample_code.shape[1]
    group = rays // regions
    room = max(16, 2 * group)
    tiles = 2 * segs
    lanes = segs * rays
    inner = [(i, i ^ 1) for i in range(regions)]
    cross = [(i, i + 1) for i in range(1, regions - 1, 2)] + [(i + 1, i) for i in range(1, regions - 1, 2)]

    def shape(*dims, kind=F32):
        return jax.ShapeDtypeStruct(dims, kind)

    def to_chips(blocks):
        return [blocks[0]] + [
            lax.ppermute(blocks[k], "region", [(i, i ^ (2 * k)) for i in range(regions)]) for k in range(1, half)
        ]

    pack_args = (
        pixel_of_ray.reshape(1, rays), seg_region.T, seg_count.T,
        ray_code, sample_code, w_hidden, w_feat.swapaxes(1, 2), w_density,
    )
    outs = pl.pallas_call(
        functools.partial(pack_kernel, half, group, room),
        out_shape=[shape(RAYS_AT + room, LANES, kind=BF16)] * half,
        in_specs=[pl.BlockSpec(memory_space=pltpu.HBM)] * 8,
        scratch_shapes=[pltpu.VMEM(x.shape, x.dtype) for x in pack_args]
        + [
            pltpu.SemaphoreType.DMA((8,)),
            pltpu.VMEM((16, rays), F32),
            pltpu.VMEM((half * room, LANES), BF16),
        ],
        compiler_params=grant(60),
        name="pack",
    )(*pack_args)
    target, decoder, own_block = lax.optimization_barrier((target, decoder, outs[0]))
    target_t, decoder_t, decoder, own_block = pl.pallas_call(
        flip_kernel,
        out_shape=(
            shape(dino_width, rays, kind=BF16),
            shape(*decoder.shape[::-1], kind=BF16),
            shape(*decoder.shape, kind=BF16),
            shape(*own_block.shape, kind=BF16),
        ),
        compiler_params=grant(8),
        name="flip",
    )(target, decoder, own_block)
    blocks = to_chips([own_block] + list(outs[1:]))
    blocks[1], (blocks[0], target_t) = lax.optimization_barrier((blocks[1], (blocks[0], target_t)))
    blocks = blocks + [lax.ppermute(block, "region", inner) for block in blocks]

    image, halo_in, halo_cr, *kept = pl.pallas_call(
        functools.partial(forward_kernel, half, group, room),
        out_shape=(
            shape(feat_width, rays, kind=BF16),
            shape(feat_width + dino_width // 2, rays, kind=BF16),
            shape(feat_width + dino_width // 2, rays, kind=BF16),
            shape(tiles, samples, hid_width, LANES),
            shape(tiles, hid_width, LANES),
            shape(tiles, hid_width, LANES),
            shape(hid_width, lanes, kind=BF16),
            shape(tiles, samples, LANES),
            shape(tiles, samples, LANES),
            shape(tiles, samples, LANES),
            shape(tiles, 1, LANES),
            shape(segs, rays, kind=jnp.int32),
            shape(code_width, rays, kind=BF16),
            shape(regions * feat_width, hid_width, kind=BF16),
        ),
        scratch_shapes=[
            pltpu.VMEM((16, regions * room), F32),
            pltpu.VMEM((samples + 1, regions, hid_width), F32),
            pltpu.VMEM((samples + 1, hid_width, 2 * regions), BF16),
            pltpu.VMEM((regions, hid_width, rays), F32),
            pltpu.VMEM((tiles, hid_width, LANES), F32),
            pltpu.VMEM((tiles, 2 * regions, LANES), BF16),
            pltpu.VMEM((tiles, 1, LANES), F32),
            pltpu.VMEM((2, 1, LANES), F32),
        ],
        compiler_params=grant(10 + regions / 4),
        name="forward",
    )(*blocks, target_t)

    halo_in = lax.ppermute(halo_in, "region", inner)
    halo_cr = lax.ppermute(halo_cr, "region", cross)

    part = shape(half, PART_ROWS, LANES, kind=BF16)
    mine, other = pl.pallas_call(
        functools.partial(backward_kernel, half),
        out_shape=(part, part),
        scratch_shapes=[
            pltpu.VMEM((decoder.shape[0], 4 * IW), BF16),
            pltpu.VMEM((regions * feat_width, lanes), BF16),
            pltpu.VMEM((tiles, hid_width, LANES), F32),
            pltpu.VMEM((samples, hid_width, lanes), BF16),
            pltpu.VMEM((hid_width, lanes), BF16),
            pltpu.VMEM((hid_width, lanes), BF16),
            pltpu.VMEM((regions, PART_ROWS - G2_AT, hid_width), F32),
            pltpu.VMEM((tiles, 1, LANES), F32),
        ],
        compiler_params=grant(16 + regions / 4),
        name="backward",
    )(image, halo_in, halo_cr, target_t, decoder, decoder_t, *kept)

    theirs = lax.ppermute(other, "region", inner)
    chip = pl.pallas_call(
        merge_kernel,
        out_shape=[shape(PART_ROWS, LANES, kind=BF16)] * half,
        compiler_params=grant(8 + regions / 8),
        name="merge",
    )(mine, theirs)
    hid_grad, feat_grad, dens_grad, code_grad = pl.pallas_call(
        finish_kernel,
        out_shape=(
            shape(1, code_width, hid_width),
            shape(1, feat_width, hid_width),
            shape(1, hid_width),
            shape(1, samples, code_width),
        ),
        compiler_params=grant(8 + regions / 8),
        name="finish",
    )(*to_chips(chip), sample_code, w_hidden)
    return hid_grad, feat_grad.swapaxes(1, 2), dens_grad, code_grad


def solution(mesh):
    in_specs = (
        P(("groups", "region"), None),
        P(("groups", "region"), None),
        P(("groups", "region"), None),
        P(("groups", "region")),
        P("region", None, None),
        P("region", None, None),
        P("region", None, None),
        P("region", None),
        P(),
        P(("groups", "region"), None),
    )
    out_specs = (
        P("region", "groups", None),
        P("region", "groups", None),
        P("region", "groups"),
        P("region", "groups", None),
    )
    return jax.shard_map(local, mesh=mesh, in_specs=in_specs, out_specs=out_specs, check_vma=False)
```

```python
import functools

import jax
import jax.numpy as jnp
from jax import lax
from jax.experimental import pallas as pl
from jax.experimental.pallas import tpu as pltpu
from jax.sharding import PartitionSpec as P

IW = 128
STEP = 0.08
F32 = jnp.float32
BF16 = jnp.bfloat16
LANES = 128

WF_AT = 128
SAMPLE_AT = 192
META_AT = 208
RAYS_AT = 224
G2_AT = 192
DG_AT = 208
PART_ROWS = 216


def grant(mib):
    return pltpu.CompilerParams(vmem_limit_bytes=int(mib * (1 << 20)))


def iota(shape, dim):
    return lax.broadcasted_iota(jnp.int32, shape, dim)


def dot(lhs, rhs, left=1, right=0):
    return lax.dot_general(lhs, rhs, (((left,), (right,)), ((), ())), preferred_element_type=F32)


def split(values):
    high = values.astype(BF16)
    return high, (values - high.astype(F32)).astype(BF16)


def running_sum(values):
    rows = values.shape[0]
    row = iota(values.shape, 0)
    step = 1
    while step < rows:
        values = values + jnp.where(row >= step, pltpu.roll(values, step, 0), 0.0)
        step *= 2
    return values


def pack_kernel(half, group, room, *refs):
    hbm, (near_ref, far_ref), held, sems = refs[:8], refs[8:10], refs[10:18], refs[18]
    meta_ref, codes_ref = refs[19:]
    me = lax.axis_index("region")
    mine = lax.shift_right_logical(me, 1)
    copies = [pltpu.make_async_copy(hbm[i], held[i], sems.at[i]) for i in range(8)]
    for copy in copies:
        copy.start()
    for copy in copies:
        copy.wait()
    pix_ref, reg_ref, cnt_ref, code_ref, samp_ref, wh_ref, wf_ref, wd_ref = held
    rays = code_ref.shape[0]
    regions = 2 * half
    shift = rays.bit_length() - 1
    pix = pix_ref[...]
    tile = lax.shift_right_logical(pix, shift)
    spot = pix & (rays - 1)
    same = jnp.where(iota((regions, rays), 0) == tile, 1.0, 0.0)
    earlier = jnp.where(iota((rays, rays), 0) < iota((rays, rays), 1), 1.0, 0.0).astype(BF16)
    counts = dot(same.astype(BF16), earlier)
    rank = jnp.sum(counts * same, axis=0, keepdims=True).astype(jnp.int32)
    row_place = lax.shift_right_logical(tile, 1) * room + (tile & 1) * group + rank
    lane_place = tile * group + rank
    meta_ref[...] = jnp.zeros(meta_ref.shape, F32)
    meta_ref[1:2, :] = spot.astype(F32)
    meta_ref[2:6, :] = reg_ref[...].astype(F32)
    meta_ref[6:10, :] = cnt_ref[...].astype(F32)
    row_hot = jnp.where(iota((half * room, rays), 0) == row_place, 1.0, 0.0).astype(BF16)
    codes_ref[...] = dot(row_hot, code_ref[...]).astype(BF16)
    lane_hot = jnp.where(iota((rays, rays), 0) == lane_place, 1.0, 0.0).astype(BF16)
    meta = dot(meta_ref[...].astype(BF16), lane_hot, 1, 1)
    wh_t = wh_ref[0].astype(F32).T.astype(BF16)
    density = wd_ref[...].astype(F32)
    first = iota((16, LANES), 0) == 0

    def rays_for(k):
        chip = jnp.bitwise_xor(mine, k)
        here = pltpu.roll(meta, (rays - chip * 2 * group) & (rays - 1), 1)[:, :LANES]
        codes = codes_ref[pl.ds(pl.multiple_of(chip * room, 16), room), :]
        return jnp.where(first, density, here).astype(BF16), codes

    for ref in [near_ref.at[k] for k in range(half // 2)] + [far_ref]:
        ref[0:WF_AT] = wh_t
        ref[WF_AT:SAMPLE_AT] = wf_ref[0]
        ref[SAMPLE_AT:META_AT] = samp_ref[0]
    for k in range(half // 2):
        near_ref[k, META_AT:RAYS_AT], near_ref[k, RAYS_AT:] = rays_for(k)
        at = META_AT + k * (16 + room)
        far_ref[at : at + 16], far_ref[at + 16 : at + 16 + room] = rays_for(k + half // 2)


def relay_kernel(near_ref, far_ref, *outs):
    for k, out in enumerate(outs):
        out[0] = near_ref[k]
        out[1, 0:META_AT] = far_ref[0:META_AT]
        rows = near_ref.shape[1] - META_AT
        out[1, META_AT:] = far_ref[META_AT + k * rows : META_AT + (k + 1) * rows]


def bits_of(row, regions):
    count = regions.bit_length() - 1
    row = jnp.broadcast_to(row, (8, LANES))
    return [(lax.shift_right_logical(row, b) & 1) == 1 for b in range(count)]


def choose(values, bits):
    for bit in bits:
        values = [jnp.where(bit, values[i + 1], values[i]) for i in range(0, len(values), 2)]
    return values[0]


def seg_hot(wanted, regions):
    return jnp.concatenate(
        [jnp.where(iota((regions, row.shape[1]), 0) == row, 1.0, 0.0) for row in wanted], axis=1
    )


def forward_kernel(half, group, room, *refs):
    regions = 2 * half
    quarter = half // 2
    received, target_ref = refs[:half], refs[half]
    blocks = [received[c * quarter + k].at[side] for c in range(2) for side in range(2) for k in range(quarter)]
    (
        image_ref, halo_in_ref, halo_cr_ref, h_ref, wd_ref, att_hw_ref, wide_hw_ref, weight_ref, pass_ref, slope_ref, att_ref, rel_ref, codes_ref, wf_out,
        meta_ref, plain_ref, table_ref, proj_ref, a_ref, picked_ref, row_ref, ahead_ref,
    ) = refs[half + 1 :]
    rays = codes_ref.shape[1]
    segs = rel_ref.shape[0]
    samples = weight_ref.shape[1]
    feats = image_ref.shape[0]
    me = lax.axis_index("region")
    core = me & 1
    chip = lax.shift_right_logical(me, 1)
    per_tile = LANES // room
    lane = iota((16, LANES), 1)
    chunk = lax.div(lane, room)
    inside = lane - chunk * room
    mine = (inside < 2 * group) & (lax.div(inside, group) == core)
    for tile in range(regions // per_tile):
        total = jnp.zeros((16, LANES), F32)
        for spot in range(per_tile):
            block = blocks[tile * per_tile + spot][META_AT:RAYS_AT].astype(F32)
            total = jnp.where(chunk == spot, pltpu.roll(block, spot * room, 1), total)
        meta_ref[:, tile * LANES : (tile + 1) * LANES] = jnp.where(mine, total, -1.0)
    meta_src = meta_ref[...]
    places = regions * room
    to_pixel = jnp.where(
        iota((rays, places), 0).astype(F32) == meta_src[1:2, :], 1.0, 0.0
    ).astype(BF16)
    sources = jnp.concatenate([block[RAYS_AT : RAYS_AT + room] for block in blocks], axis=0)
    codes_t = dot(to_pixel, sources).T.astype(BF16)
    codes_ref[...] = codes_t
    meta = dot(meta_src.astype(BF16), to_pixel, 1, 1)
    region = meta[2 : 2 + segs].astype(jnp.int32)
    rel = jnp.bitwise_xor(region & 1, core) * half + jnp.bitwise_xor(lax.shift_right_logical(region, 1), chip)
    rel_ref[...] = rel
    for k in range(segs):
        for part in range(2):
            row_ref[2 * k + part] = meta[6 + k : 7 + k, part * LANES : (part + 1) * LANES]
    wanted = [rel_ref[k : k + 1, :] for k in range(segs)]
    for r, block in enumerate(blocks):
        w_t = block[0:WF_AT]
        proj_ref[r] = dot(w_t, codes_t)
        plain_ref[0:samples, r, :] = dot(block[SAMPLE_AT:META_AT], w_t, 1, 1)
        plain_ref[samples, r : r + 1, :] = block[META_AT:RAYS_AT].astype(F32)[0:1, :]
        wf_out[r * feats : (r + 1) * feats] = block[WF_AT:SAMPLE_AT]
    for s in range(samples + 1):
        high, low = split(plain_ref[s])
        table_ref[s] = jnp.concatenate([high.astype(F32), low.astype(F32)], axis=0).T.astype(BF16)
    for part in range(2):
        lanes = slice(part * LANES, (part + 1) * LANES)

        def pick_rows(index, carry):
            rows = pl.ds(pl.multiple_of(index * 8, 8), 8)
            bits = [bits_of(row[:, lanes], regions) for row in wanted]
            values = [proj_ref[r, rows, lanes] for r in range(regions)]
            for k in range(segs):
                a_ref[2 * k + part, rows, :] = choose(values, bits[k])
            return carry

        lax.fori_loop(0, 16, pick_rows, 0)
    hot = seg_hot(wanted, regions).astype(BF16)
    hot2 = jnp.concatenate([hot, hot], axis=0)
    for tile in range(2 * segs):
        picked_ref[tile] = hot2[:, tile * LANES : (tile + 1) * LANES]
    ahead_ref[...] = jnp.zeros(ahead_ref.shape, F32)
    order = iota((samples, LANES), 0).astype(F32)

    def step(tile, carry):
        here = picked_ref[tile]
        wd = dot(table_ref[samples], here)
        wd_ref[tile] = wd
        sums = []
        for s in range(samples):
            h = jnp.maximum(a_ref[tile] + dot(table_ref[s], here), 0.0)
            h_ref[tile, s] = h
            sums.append(jnp.sum(h * wd_ref[tile], axis=0, keepdims=True))
        density = jnp.concatenate(sums, axis=0)
        part = tile & 1
        live = order < row_ref[tile]
        soft = jnp.maximum(density, 0.0) + jnp.log1p(jnp.exp(-jnp.abs(density)))
        thick = jnp.where(live, STEP * soft, 0.0)
        through = running_sum(thick)
        passing = jnp.exp(-(through - thick))
        keeping = jnp.exp(-thick)
        weight = passing * (1.0 - keeping)
        weight_ref[tile] = weight
        pass_ref[tile] = passing * keeping
        slope_ref[tile] = jnp.where(live, STEP / (1.0 + jnp.exp(-density)), 0.0)
        before = ahead_ref[part]
        att = jnp.exp(-before)
        ahead_ref[part] = before + through[samples - 1 : samples, :]
        att_ref[tile] = att
        scale = [jnp.broadcast_to(weight[s : s + 1, :] * att, (8, LANES)) for s in range(samples)]
        lanes = pl.ds(pl.multiple_of(tile * LANES, LANES), LANES)
        for pair in range(8):
            both = []
            for ht in (2 * pair, 2 * pair + 1):
                rows = slice(ht * 8, ht * 8 + 8)
                total = scale[0] * h_ref[tile, 0, rows, :]
                for s in range(1, samples):
                    total = total + scale[s] * h_ref[tile, s, rows, :]
                att_hw_ref[tile, rows, :] = total
                both.append(total)
            wide_hw_ref[pair * 16 : pair * 16 + 16, lanes] = jnp.concatenate(both, axis=0).astype(BF16)
        return carry

    lax.fori_loop(0, 2 * segs, step, 0)
    wf_twice = jnp.concatenate([wf_out[...], wf_out[...]], axis=1)
    for part in range(2):
        feat = [jnp.zeros((8, LANES), F32)] * (feats // 8)
        for k in range(segs):
            tile = 2 * k + part
            high, low = split(att_hw_ref[tile])
            proj_ref[0 : regions * feats // LANES, :, 0:LANES] = dot(wf_twice, jnp.concatenate([high, low], axis=0)).reshape(
                regions * feats // LANES, LANES, LANES
            )
            bits = bits_of(wanted[k][:, part * LANES : (part + 1) * LANES], regions)
            for ft in range(feats // 8):
                values = []
                for r in range(regions):
                    at = r * feats + ft * 8
                    values.append(proj_ref[at // LANES, at % LANES : at % LANES + 8, 0:LANES])
                feat[ft] = feat[ft] + choose(values, bits)
        image_ref[:, part * LANES : (part + 1) * LANES] = jnp.concatenate(feat, axis=0).astype(BF16)
    near, far = target_ref[:, :IW].astype(F32), target_ref[:, rays - IW :].astype(F32)
    for out_ref, row in ((halo_in_ref, jnp.where(core == 0, far, near)), (halo_cr_ref, jnp.where(core == 0, near, far))):
        out_ref[0:feats] = image_ref[...]
        depth = target_ref.shape[0] // 2
        out_ref[feats:, 0:IW] = row[:depth].astype(BF16)
        out_ref[feats:, rays - IW :] = row[depth:].astype(BF16)


def shifted(values, by):
    lane = iota(values.shape, 1)
    if by == 0:
        return values
    if by > 0:
        return jnp.where(lane == 0, 0.0, pltpu.roll(values, 1, 1))
    return jnp.where(lane == LANES - 1, 0.0, pltpu.roll(values, LANES - 1, 1))


def backward_kernel(
    half, own_ref, inner_ref, cross_ref, tgt_ref, dec_ref, dect_ref,
    h_in, wd_ref, att_hw_ref, wide_hw_ref, weight_ref, pass_ref, slope_ref, att_ref, rel_ref, codes_ref, wf_ref,
    mine_ref, other_ref,
    patch_ref, masked_ref, q_ref, gp_ref, g1_ref, hd_ref, tail_ref, row_ref,
):
    regions = 2 * half
    feats, rays = own_ref.shape
    segs = rel_ref.shape[0]
    samples = weight_ref.shape[1]
    me = lax.axis_index("region")
    core = me & 1
    own = own_ref[...].astype(F32)
    halo_in = inner_ref[...].astype(F32)
    halo_cr = cross_ref[...].astype(F32)
    inner, tin = halo_in[:feats], jnp.concatenate([halo_in[feats:, :IW], halo_in[feats:, rays - IW :]], axis=0)
    cross, tcr = halo_cr[:feats], jnp.concatenate([halo_cr[feats:, :IW], halo_cr[feats:, rays - IW :]], axis=0)
    top = jnp.where(core == 0, cross, inner)
    bottom = jnp.where(core == 0, inner, cross)
    rows = [v[:, i * IW : (i + 1) * IW] for v in (top, own, bottom) for i in range(2)]
    for at, row in enumerate(rows):
        for dx in range(3):
            piece = shifted(row, 1 - dx).astype(BF16)
            for dy in range(3):
                if 0 <= at - dy < 4:
                    patch_ref[(3 * dy + dx) * feats : (3 * dy + dx + 1) * feats, (at - dy) * IW : (at - dy + 1) * IW] = piece
    t_top = jnp.where(core == 0, tcr, tin)
    t_bottom = jnp.where(core == 0, tin, tcr)
    decoded = dot(dect_ref[...], patch_ref[...])
    tgt = tgt_ref[...].astype(F32)
    g_top = jnp.where(me > 0, decoded[:, 0:IW] - t_top, 0.0)
    g_own = decoded[:, IW : 3 * IW] - tgt
    g_bottom = jnp.where(me < regions - 1, decoded[:, 3 * IW :] - t_bottom, 0.0)
    grad_dec = jnp.concatenate([g_top, g_own, g_bottom], axis=1).astype(BF16)
    grad_patch = dot(dec_ref[...], grad_dec)
    image_rows = []
    for i in range(2):
        total = jnp.zeros((feats, IW), F32)
        for dx in range(3):
            term = jnp.zeros((feats, IW), F32)
            for dy in range(3):
                at = (3 * dy + dx) * feats
                term = term + grad_patch[at : at + feats, (i - dy + 2) * IW : (i - dy + 3) * IW]
            total = total + shifted(term, dx - 1)
        image_rows.append(total)
    grad_ray = jnp.concatenate(image_rows, axis=1)
    wanted = [rel_ref[k : k + 1, :] for k in range(segs)]
    for r in range(regions):
        for k in range(segs):
            masked = jnp.where(wanted[k] == r, grad_ray, 0.0).astype(BF16)
            masked_ref[r * feats : (r + 1) * feats, k * rays : (k + 1) * rays] = masked
    raw = dot(wf_ref[...], masked_ref[...], 0, 0)
    for tile in range(2 * segs):
        q_ref[tile] = raw[:, tile * LANES : (tile + 1) * LANES]
    feat_grad = dot(masked_ref[...], wide_hw_ref[...], 1, 1).astype(BF16)
    for r in range(regions):
        out, to = (mine_ref, r) if r < half else (other_ref, r - half)
        out[to, WF_AT:G2_AT] = feat_grad[r * feats : (r + 1) * feats]
    hot = seg_hot(wanted, regions).astype(BF16)
    for part in range(2):
        later = jnp.zeros((1, LANES), F32)
        for k in reversed(range(segs)):
            row_ref[2 * k + part] = -later
            pulled = jnp.sum(att_hw_ref[2 * k + part] * q_ref[2 * k + part], axis=0, keepdims=True)
            later = later + pulled

    def step(tile, carry):
        att = jnp.broadcast_to(att_ref[tile], (8, LANES))
        sums = [jnp.zeros((8, LANES), F32)] * samples
        for ht in range(16):
            rows = slice(ht * 8, ht * 8 + 8)
            q = q_ref[tile, rows, :] * att
            q_ref[tile, rows, :] = q
            for s in range(samples):
                sums[s] = sums[s] + h_in[tile, s, rows, :] * q
        along = jnp.concatenate([jnp.sum(v, axis=0, keepdims=True) for v in sums], axis=0)
        weight = weight_ref[tile]
        through = running_sum(along * weight)
        later = through[samples - 1 : samples, :] - through
        grad_thick = row_ref[tile] + along * pass_ref[tile] - later
        grad_density = (grad_thick * slope_ref[tile]).astype(BF16).astype(F32)
        scale = [jnp.broadcast_to(weight[s : s + 1, :], (8, LANES)) for s in range(samples)]
        slant = [jnp.broadcast_to(grad_density[s : s + 1, :], (8, LANES)) for s in range(samples)]
        lanes = pl.ds(pl.multiple_of(tile * LANES, LANES), LANES)
        for pair in range(8):
            at = [slice((2 * pair + u) * 8, (2 * pair + u) * 8 + 8) for u in range(2)]
            q = [q_ref[tile, rows, :] for rows in at]
            wd = [wd_ref[tile, rows, :] for rows in at]
            g1 = [jnp.zeros((8, LANES), F32)] * 2
            hd = [jnp.zeros((8, LANES), F32)] * 2
            for s in range(samples):
                both = []
                for u in range(2):
                    h = h_in[tile, s, at[u], :]
                    gp = jnp.where(h > 0.0, scale[s] * q[u] + slant[s] * wd[u], 0.0)
                    g1[u] = g1[u] + gp
                    hd[u] = hd[u] + slant[s] * h
                    both.append(gp)
                gp_ref[s, 16 * pair : 16 * pair + 16, lanes] = jnp.concatenate(both, axis=0).astype(BF16)
            g1_ref[16 * pair : 16 * pair + 16, lanes] = jnp.concatenate(g1, axis=0).astype(BF16)
            hd_ref[16 * pair : 16 * pair + 16, lanes] = jnp.concatenate(hd, axis=0).astype(BF16)
        return carry

    lax.fori_loop(0, 2 * segs, step, 0)
    codes = codes_ref[...].astype(F32)
    tail_ref[...] = jnp.zeros(tail_ref.shape, F32)
    for s in range(samples):
        tail_ref[:, s, :] = dot(hot, gp_ref[s], 1, 1)
    tail_ref[:, samples, :] = dot(hot, hd_ref[...], 1, 1)
    g1 = g1_ref[...]
    for r in range(regions):
        out, to = (mine_ref, r) if r < half else (other_ref, r - half)
        held = jnp.concatenate([jnp.where(row == r, codes, 0.0).astype(BF16) for row in wanted], axis=1)
        out[to, 0:WF_AT] = dot(held, g1, 1, 1).astype(BF16)
        out[to, G2_AT:PART_ROWS] = tail_ref[r].astype(BF16)


def flip_kernel(target_ref, decoder_ref, target_out, decoder_out, same_out):
    same_out[...] = decoder_ref[...]
    target_out[...] = target_ref[...].astype(F32).T.astype(BF16)
    decoder_out[...] = decoder_ref[...].astype(F32).T.astype(BF16)


def merge_kernel(mine_ref, theirs_ref, *outs):
    for k, out in enumerate(outs):
        for side in range(2):
            at = side * len(outs) + k
            out[side] = (mine_ref[at].astype(F32) + theirs_ref[at].astype(F32)).astype(BF16)


def reduce_kernel(*refs):
    parts, (keep_ref, send_ref) = refs[:-2], refs[-2:]
    for side, out in enumerate((keep_ref, send_ref)):
        total = parts[0][side].astype(F32)
        for part in parts[1:]:
            total = total + part[side].astype(F32)
        out[...] = total.astype(out.dtype)


def finish_kernel(keep_ref, part_ref, samp_ref, wh_ref, hid_ref, feat_ref, dens_ref, code_ref):
    total = keep_ref[...] + part_ref[...].astype(F32)
    high, low = split(total[G2_AT:DG_AT])
    samples = samp_ref[0]
    wh = wh_ref[0]
    hid_ref[0] = total[0:WF_AT] + dot(samples, high, 0, 0) + dot(samples, low, 0, 0)
    feat_ref[0] = total[WF_AT:G2_AT]
    dens_ref[...] = total[DG_AT : DG_AT + 1]
    code_ref[0] = dot(high, wh, 1, 1) + dot(low, wh, 1, 1)


def local(ray_code, seg_region, seg_count, pixel_of_ray, sample_code, w_hidden, w_feat, w_density, decoder, target):
    regions = lax.axis_size("region")
    half = regions // 2
    rays, segs = seg_region.shape
    code_width = ray_code.shape[1]
    hid_width = w_hidden.shape[2]
    feat_width = w_feat.shape[2]
    dino_width = target.shape[1]
    samples = sample_code.shape[1]
    group = rays // regions
    room = max(16, 2 * group)
    tiles = 2 * segs
    lanes = segs * rays
    inner = [(i, i ^ 1) for i in range(regions)]
    cross = [(i, i + 1) for i in range(1, regions - 1, 2)] + [(i + 1, i) for i in range(1, regions - 1, 2)]

    def shape(*dims, kind=F32):
        return jax.ShapeDtypeStruct(dims, kind)

    quarter = half // 2
    pack_rows = RAYS_AT + room

    def to_chip(block, k):
        return lax.ppermute(block, "region", [(i, i ^ (2 * k)) for i in range(regions)])

    def to_half(blocks):
        return [blocks[0]] + [to_chip(blocks[k], k) for k in range(1, quarter)]

    pack_args = (
        pixel_of_ray.reshape(1, rays), seg_region.T, seg_count.T,
        ray_code, sample_code, w_hidden, w_feat.swapaxes(1, 2), w_density,
    )
    near, far = pl.pallas_call(
        functools.partial(pack_kernel, half, group, room),
        out_shape=(
            shape(quarter, pack_rows, LANES, kind=BF16),
            shape(META_AT + quarter * (16 + room), LANES, kind=BF16),
        ),
        in_specs=[pl.BlockSpec(memory_space=pltpu.HBM)] * 8,
        scratch_shapes=[pltpu.VMEM(x.shape, x.dtype) for x in pack_args]
        + [
            pltpu.SemaphoreType.DMA((8,)),
            pltpu.VMEM((16, rays), F32),
            pltpu.VMEM((half * room, LANES), BF16),
        ],
        compiler_params=grant(60),
        name="pack",
    )(*pack_args)
    far = to_chip(far, quarter)
    flipped = pl.pallas_call(
        flip_kernel,
        out_shape=(
            shape(dino_width, rays, kind=BF16),
            shape(*decoder.shape[::-1], kind=BF16),
            shape(*decoder.shape, kind=BF16),
        ),
        compiler_params=grant(8),
        name="flip",
    )(target, decoder)
    far, (target_t, decoder_t, decoder) = lax.optimization_barrier((far, flipped))
    blocks = to_half(
        pl.pallas_call(
            relay_kernel,
            out_shape=[shape(2, pack_rows, LANES, kind=BF16)] * quarter,
            compiler_params=grant(8 + regions / 8),
            name="relay",
        )(near, far)
    )
    blocks = blocks + [lax.ppermute(block, "region", inner) for block in blocks]

    image, halo_in, halo_cr, *kept = pl.pallas_call(
        functools.partial(forward_kernel, half, group, room),
        out_shape=(
            shape(feat_width, rays, kind=BF16),
            shape(feat_width + dino_width // 2, rays, kind=BF16),
            shape(feat_width + dino_width // 2, rays, kind=BF16),
            shape(tiles, samples, hid_width, LANES),
            shape(tiles, hid_width, LANES),
            shape(tiles, hid_width, LANES),
            shape(hid_width, lanes, kind=BF16),
            shape(tiles, samples, LANES),
            shape(tiles, samples, LANES),
            shape(tiles, samples, LANES),
            shape(tiles, 1, LANES),
            shape(segs, rays, kind=jnp.int32),
            shape(code_width, rays, kind=BF16),
            shape(regions * feat_width, hid_width, kind=BF16),
        ),
        scratch_shapes=[
            pltpu.VMEM((16, regions * room), F32),
            pltpu.VMEM((samples + 1, regions, hid_width), F32),
            pltpu.VMEM((samples + 1, hid_width, 2 * regions), BF16),
            pltpu.VMEM((regions, hid_width, rays), F32),
            pltpu.VMEM((tiles, hid_width, LANES), F32),
            pltpu.VMEM((tiles, 2 * regions, LANES), BF16),
            pltpu.VMEM((tiles, 1, LANES), F32),
            pltpu.VMEM((2, 1, LANES), F32),
        ],
        compiler_params=grant(10 + regions / 4),
        name="forward",
    )(*blocks, target_t)

    halo_in = lax.ppermute(halo_in, "region", inner)
    halo_cr = lax.ppermute(halo_cr, "region", cross)

    part = shape(half, PART_ROWS, LANES, kind=BF16)
    mine, other = pl.pallas_call(
        functools.partial(backward_kernel, half),
        out_shape=(part, part),
        scratch_shapes=[
            pltpu.VMEM((decoder.shape[0], 4 * IW), BF16),
            pltpu.VMEM((regions * feat_width, lanes), BF16),
            pltpu.VMEM((tiles, hid_width, LANES), F32),
            pltpu.VMEM((samples, hid_width, lanes), BF16),
            pltpu.VMEM((hid_width, lanes), BF16),
            pltpu.VMEM((hid_width, lanes), BF16),
            pltpu.VMEM((regions, PART_ROWS - G2_AT, hid_width), F32),
            pltpu.VMEM((tiles, 1, LANES), F32),
        ],
        compiler_params=grant(16 + regions / 4),
        name="backward",
    )(image, halo_in, halo_cr, target_t, decoder, decoder_t, *kept)

    theirs = lax.ppermute(other, "region", inner)
    parts = pl.pallas_call(
        merge_kernel,
        out_shape=[shape(2, PART_ROWS, LANES, kind=BF16)] * quarter,
        compiler_params=grant(8 + regions / 8),
        name="merge",
    )(mine, theirs)
    keep, send = pl.pallas_call(
        reduce_kernel,
        out_shape=(shape(PART_ROWS, LANES), shape(PART_ROWS, LANES, kind=BF16)),
        compiler_params=grant(8 + regions / 8),
        name="reduce",
    )(*to_half(parts))
    hid_grad, feat_grad, dens_grad, code_grad = pl.pallas_call(
        finish_kernel,
        out_shape=(
            shape(1, code_width, hid_width),
            shape(1, feat_width, hid_width),
            shape(1, hid_width),
            shape(1, samples, code_width),
        ),
        compiler_params=grant(8 + regions / 8),
        name="finish",
    )(keep, to_chip(send, quarter), sample_code, w_hidden)
    return hid_grad, feat_grad.swapaxes(1, 2), dens_grad, code_grad


def solution(mesh):
    in_specs = (
        P(("groups", "region"), None),
        P(("groups", "region"), None),
        P(("groups", "region"), None),
        P(("groups", "region")),
        P("region", None, None),
        P("region", None, None),
        P("region", None, None),
        P("region", None),
        P(),
        P(("groups", "region"), None),
    )
    out_specs = (
        P("region", "groups", None),
        P("region", "groups", None),
        P("region", "groups"),
        P("region", "groups", None),
    )
    return jax.shard_map(local, mesh=mesh, in_specs=in_specs, out_specs=out_specs, check_vma=False)
```

```python
import functools

import jax
import jax.numpy as jnp
from jax import lax
from jax.experimental import pallas as pl
from jax.experimental.pallas import tpu as pltpu
from jax.sharding import PartitionSpec as P

IW = 128
STEP = 0.08
F32 = jnp.float32
BF16 = jnp.bfloat16
LANES = 128

WF_AT = 128
SAMPLE_AT = 192
META_AT = 208
RAYS_AT = 224
G2_AT = 192
DG_AT = 208
PART_ROWS = 216


def grant(mib):
    return pltpu.CompilerParams(vmem_limit_bytes=int(mib * (1 << 20)))


def iota(shape, dim):
    return lax.broadcasted_iota(jnp.int32, shape, dim)


def dot(lhs, rhs, left=1, right=0):
    return lax.dot_general(lhs, rhs, (((left,), (right,)), ((), ())), preferred_element_type=F32)


def split(values):
    high = values.astype(BF16)
    return high, (values - high.astype(F32)).astype(BF16)


def running_sum(values):
    rows = values.shape[0]
    row = iota(values.shape, 0)
    step = 1
    while step < rows:
        values = values + jnp.where(row >= step, pltpu.roll(values, step, 0), 0.0)
        step *= 2
    return values


def pack_kernel(half, group, room, *refs):
    hbm, (near_ref, far_ref), held, sems = refs[:8], refs[8:10], refs[10:18], refs[18]
    meta_ref, codes_ref = refs[19:]
    me = lax.axis_index("region")
    mine = lax.shift_right_logical(me, 1)
    copies = [pltpu.make_async_copy(hbm[i], held[i], sems.at[i]) for i in range(8)]
    for copy in copies:
        copy.start()
    for copy in copies:
        copy.wait()
    pix_ref, reg_ref, cnt_ref, code_ref, samp_ref, wh_ref, wf_ref, wd_ref = held
    rays = code_ref.shape[0]
    regions = 2 * half
    shift = rays.bit_length() - 1
    pix = pix_ref[...]
    tile = lax.shift_right_logical(pix, shift)
    spot = pix & (rays - 1)
    same = jnp.where(iota((regions, rays), 0) == tile, 1.0, 0.0)
    earlier = jnp.where(iota((rays, rays), 0) < iota((rays, rays), 1), 1.0, 0.0).astype(BF16)
    counts = dot(same.astype(BF16), earlier)
    rank = jnp.sum(counts * same, axis=0, keepdims=True).astype(jnp.int32)
    row_place = lax.shift_right_logical(tile, 1) * room + (tile & 1) * group + rank
    lane_place = tile * group + rank
    meta_ref[...] = jnp.zeros(meta_ref.shape, F32)
    meta_ref[1:2, :] = spot.astype(F32)
    meta_ref[2:6, :] = reg_ref[...].astype(F32)
    meta_ref[6:10, :] = cnt_ref[...].astype(F32)
    row_hot = jnp.where(iota((half * room, rays), 0) == row_place, 1.0, 0.0).astype(BF16)
    codes_ref[...] = dot(row_hot, code_ref[...]).astype(BF16)
    lane_hot = jnp.where(iota((rays, rays), 0) == lane_place, 1.0, 0.0).astype(BF16)
    meta = dot(meta_ref[...].astype(BF16), lane_hot, 1, 1)
    wh_t = wh_ref[0].astype(F32).T.astype(BF16)
    density = wd_ref[...].astype(F32)
    first = iota((16, LANES), 0) == 0

    def rays_for(k):
        chip = jnp.bitwise_xor(mine, k)
        here = pltpu.roll(meta, (rays - chip * 2 * group) & (rays - 1), 1)[:, :LANES]
        codes = codes_ref[pl.ds(pl.multiple_of(chip * room, 16), room), :]
        return jnp.where(first, density, here).astype(BF16), codes

    for ref in [near_ref.at[k] for k in range(half // 2)] + [far_ref]:
        ref[0:WF_AT] = wh_t
        ref[WF_AT:SAMPLE_AT] = wf_ref[0]
        ref[SAMPLE_AT:META_AT] = samp_ref[0]
    for k in range(half // 2):
        near_ref[k, META_AT:RAYS_AT], near_ref[k, RAYS_AT:] = rays_for(k)
        at = META_AT + k * (16 + room)
        far_ref[at : at + 16], far_ref[at + 16 : at + 16 + room] = rays_for(k + half // 2)


def relay_kernel(near_ref, far_ref, *outs):
    for k, out in enumerate(outs):
        out[0] = near_ref[k]
        out[1, 0:META_AT] = far_ref[0:META_AT]
        rows = near_ref.shape[1] - META_AT
        out[1, META_AT:] = far_ref[META_AT + k * rows : META_AT + (k + 1) * rows]


def bits_of(row, regions):
    count = regions.bit_length() - 1
    row = jnp.broadcast_to(row, (8, LANES))
    return [(lax.shift_right_logical(row, b) & 1) == 1 for b in range(count)]


def choose(values, bits):
    for bit in bits:
        values = [jnp.where(bit, values[i + 1], values[i]) for i in range(0, len(values), 2)]
    return values[0]


def seg_hot(wanted, regions):
    return jnp.concatenate(
        [jnp.where(iota((regions, row.shape[1]), 0) == row, 1.0, 0.0) for row in wanted], axis=1
    )


def forward_kernel(half, group, room, *refs):
    regions = 2 * half
    quarter = half // 2
    received, target_ref = refs[:half], refs[half]
    blocks = [received[c * quarter + k].at[side] for c in range(2) for side in range(2) for k in range(quarter)]
    (
        image_ref, halo_in_ref, halo_cr_ref, h_ref, wd_ref, att_hw_ref, wide_hw_ref, weight_ref, pass_ref, slope_ref, att_ref, rel_ref, codes_ref, wf_out,
        meta_ref, plain_ref, table_ref, proj_ref, a_ref, picked_ref, row_ref, density_ref,
    ) = refs[half + 1 :]
    rays = codes_ref.shape[1]
    segs = rel_ref.shape[0]
    samples = weight_ref.shape[0]
    feats = image_ref.shape[0]
    hids = table_ref.shape[1]
    me = lax.axis_index("region")
    core = me & 1
    chip = lax.shift_right_logical(me, 1)
    per_tile = LANES // room
    lane = iota((16, LANES), 1)
    chunk = lax.div(lane, room)
    inside = lane - chunk * room
    mine = (inside < 2 * group) & (lax.div(inside, group) == core)
    for tile in range(regions // per_tile):
        total = jnp.zeros((16, LANES), F32)
        for spot in range(per_tile):
            block = blocks[tile * per_tile + spot][META_AT:RAYS_AT].astype(F32)
            total = jnp.where(chunk == spot, pltpu.roll(block, spot * room, 1), total)
        meta_ref[:, tile * LANES : (tile + 1) * LANES] = jnp.where(mine, total, -1.0)
    meta_src = meta_ref[...]
    places = regions * room
    to_pixel = jnp.where(
        iota((rays, places), 0).astype(F32) == meta_src[1:2, :], 1.0, 0.0
    ).astype(BF16)
    sources = jnp.concatenate([block[RAYS_AT : RAYS_AT + room] for block in blocks], axis=0)
    codes_t = dot(to_pixel, sources).T.astype(BF16)
    codes_ref[...] = codes_t
    meta = dot(meta_src.astype(BF16), to_pixel, 1, 1)
    region = meta[2 : 2 + segs].astype(jnp.int32)
    rel = jnp.bitwise_xor(region & 1, core) * half + jnp.bitwise_xor(lax.shift_right_logical(region, 1), chip)
    rel_ref[...] = rel
    for k in range(segs):
        row_ref[:, k * rays : (k + 1) * rays] = meta[6 + k : 7 + k]
    wanted = [rel_ref[k : k + 1, :] for k in range(segs)]
    for r, block in enumerate(blocks):
        w_t = block[0:WF_AT]
        proj_ref[r] = dot(w_t, codes_t)
        plain_ref[0:samples, r, :] = dot(block[SAMPLE_AT:META_AT], w_t, 1, 1)
        plain_ref[samples, r : r + 1, :] = block[META_AT:RAYS_AT].astype(F32)[0:1, :]
        wf_out[r * feats : (r + 1) * feats] = block[WF_AT:SAMPLE_AT]
    for s in range(samples + 1):
        high, low = split(plain_ref[s])
        table_ref[s] = jnp.concatenate([high.astype(F32), low.astype(F32)], axis=0).T.astype(BF16)
    for part in range(2):
        lanes = slice(part * LANES, (part + 1) * LANES)

        def pick_rows(index, carry):
            rows = pl.ds(pl.multiple_of(index * 8, 8), 8)
            bits = [bits_of(row[:, lanes], regions) for row in wanted]
            values = [proj_ref[r, rows, lanes] for r in range(regions)]
            for k in range(segs):
                a_ref[2 * k + part, rows, :] = choose(values, bits[k])
            return carry

        lax.fori_loop(0, 16, pick_rows, 0, unroll=4)
    hot = seg_hot(wanted, regions).astype(BF16)
    hot2 = jnp.concatenate([hot, hot], axis=0)
    for tile in range(2 * segs):
        picked_ref[tile] = hot2[:, tile * LANES : (tile + 1) * LANES]

    def densities(tile, carry):
        here = picked_ref[tile]
        wd_ref[tile] = dot(table_ref[samples], here)
        sums = []
        for s in range(samples):
            h = jnp.maximum(a_ref[tile] + dot(table_ref[s], here), 0.0)
            h_ref[tile, s] = h
            sums.append(jnp.sum(h * wd_ref[tile], axis=0, keepdims=True))
        lanes = pl.ds(pl.multiple_of(tile * LANES, LANES), LANES)
        density_ref[:, lanes] = jnp.concatenate(sums, axis=0)
        return carry

    lax.fori_loop(0, 2 * segs, densities, 0, unroll=4)
    density = density_ref[...]
    live = iota(density.shape, 0).astype(F32) < row_ref[...]
    soft = jnp.maximum(density, 0.0) + jnp.log1p(jnp.exp(-jnp.abs(density)))
    thick = jnp.where(live, STEP * soft, 0.0)
    through = running_sum(thick)
    passing = jnp.exp(-(through - thick))
    keeping = jnp.exp(-thick)
    weight = passing * (1.0 - keeping)
    weight_ref[...] = weight
    pass_ref[...] = passing * keeping
    slope_ref[...] = jnp.where(live, STEP / (1.0 + jnp.exp(-density)), 0.0)
    ahead = jnp.zeros((1, rays), F32)
    for k in range(segs):
        att_ref[:, k * rays : (k + 1) * rays] = jnp.exp(-ahead)
        ahead = ahead + through[samples - 1 : samples, k * rays : (k + 1) * rays]
    density_ref[...] = weight * att_ref[...]

    def compose(tile, carry):
        lanes = pl.ds(pl.multiple_of(tile * LANES, LANES), LANES)
        faded = density_ref[:, lanes]
        scale = [jnp.broadcast_to(faded[s : s + 1, :], (8, LANES)) for s in range(samples)]
        for pair in range(8):
            both = []
            for ht in (2 * pair, 2 * pair + 1):
                rows = slice(ht * 8, ht * 8 + 8)
                total = scale[0] * h_ref[tile, 0, rows, :]
                for s in range(1, samples):
                    total = total + scale[s] * h_ref[tile, s, rows, :]
                both.append(total)
            both = jnp.concatenate(both, axis=0)
            high, low = split(both)
            att_hw_ref[pair * 16 : pair * 16 + 16, lanes] = both
            wide_hw_ref[pair * 16 : pair * 16 + 16, lanes] = high
            wide_hw_ref[hids + pair * 16 : hids + pair * 16 + 16, lanes] = low
        return carry

    lax.fori_loop(0, 2 * segs, compose, 0, unroll=2)
    wf_twice = jnp.concatenate([wf_out[...], wf_out[...]], axis=1)
    feat = [jnp.zeros((8, LANES), F32)] * (2 * (feats // 8))
    for k in range(segs):
        values = dot(wf_twice, wide_hw_ref[:, k * rays : (k + 1) * rays])
        for r in range(regions * feats // LANES):
            proj_ref[r] = values[r * LANES : (r + 1) * LANES]
        for part in range(2):
            lanes = slice(part * LANES, (part + 1) * LANES)
            bits = bits_of(wanted[k][:, lanes], regions)
            for ft in range(feats // 8):
                found = []
                for r in range(regions):
                    at = r * feats + ft * 8
                    found.append(proj_ref[at // LANES, at % LANES : at % LANES + 8, lanes])
                feat[2 * ft + part] = feat[2 * ft + part] + choose(found, bits)
    for part in range(2):
        image_ref[:, part * LANES : (part + 1) * LANES] = jnp.concatenate(feat[part::2], axis=0).astype(BF16)
    near, far = target_ref[:, :IW].astype(F32), target_ref[:, rays - IW :].astype(F32)
    for out_ref, row in ((halo_in_ref, jnp.where(core == 0, far, near)), (halo_cr_ref, jnp.where(core == 0, near, far))):
        out_ref[0:feats] = image_ref[...]
        depth = target_ref.shape[0] // 2
        out_ref[feats:, 0:IW] = row[:depth].astype(BF16)
        out_ref[feats:, rays - IW :] = row[depth:].astype(BF16)


def shifted(values, by):
    lane = iota(values.shape, 1)
    if by == 0:
        return values
    if by > 0:
        return jnp.where(lane == 0, 0.0, pltpu.roll(values, 1, 1))
    return jnp.where(lane == LANES - 1, 0.0, pltpu.roll(values, LANES - 1, 1))


def backward_kernel(
    half, own_ref, inner_ref, cross_ref, tgt_ref, dec_ref, dect_ref,
    h_in, wd_ref, att_hw_ref, wide_hw_ref, weight_ref, pass_ref, slope_ref, att_ref, rel_ref, codes_ref, wf_ref,
    mine_ref, other_ref,
    patch_ref, masked_ref, q_ref, gp_ref, g1_ref, hd_ref, tail_ref, row_ref, along_ref, hot_ref,
):
    regions = 2 * half
    feats, rays = own_ref.shape
    segs = rel_ref.shape[0]
    samples = weight_ref.shape[0]
    hids = wd_ref.shape[1]
    unroll = min(regions, 16)
    me = lax.axis_index("region")
    core = me & 1
    own = own_ref[...].astype(F32)
    halo_in = inner_ref[...].astype(F32)
    halo_cr = cross_ref[...].astype(F32)
    inner, tin = halo_in[:feats], jnp.concatenate([halo_in[feats:, :IW], halo_in[feats:, rays - IW :]], axis=0)
    cross, tcr = halo_cr[:feats], jnp.concatenate([halo_cr[feats:, :IW], halo_cr[feats:, rays - IW :]], axis=0)
    top = jnp.where(core == 0, cross, inner)
    bottom = jnp.where(core == 0, inner, cross)
    rows = [v[:, i * IW : (i + 1) * IW] for v in (top, own, bottom) for i in range(2)]
    for at, row in enumerate(rows):
        for dx in range(3):
            piece = shifted(row, 1 - dx).astype(BF16)
            for dy in range(3):
                if 0 <= at - dy < 4:
                    patch_ref[(3 * dy + dx) * feats : (3 * dy + dx + 1) * feats, (at - dy) * IW : (at - dy + 1) * IW] = piece
    t_top = jnp.where(core == 0, tcr, tin)
    t_bottom = jnp.where(core == 0, tin, tcr)
    decoded = dot(dect_ref[...], patch_ref[...])
    tgt = tgt_ref[...].astype(F32)
    g_top = jnp.where(me > 0, decoded[:, 0:IW] - t_top, 0.0)
    g_own = decoded[:, IW : 3 * IW] - tgt
    g_bottom = jnp.where(me < regions - 1, decoded[:, 3 * IW :] - t_bottom, 0.0)
    grad_dec = jnp.concatenate([g_top, g_own, g_bottom], axis=1).astype(BF16)
    grad_patch = dot(dec_ref[...], grad_dec)
    image_rows = []
    for i in range(2):
        total = jnp.zeros((feats, IW), F32)
        for dx in range(3):
            term = jnp.zeros((feats, IW), F32)
            for dy in range(3):
                at = (3 * dy + dx) * feats
                term = term + grad_patch[at : at + feats, (i - dy + 2) * IW : (i - dy + 3) * IW]
            total = total + shifted(term, dx - 1)
        image_rows.append(total)
    grad_ray = jnp.concatenate(image_rows, axis=1)
    wanted = [rel_ref[k : k + 1, :] for k in range(segs)]
    hot = seg_hot(wanted, regions)
    for r in range(regions):
        hot_ref[r] = jnp.broadcast_to(hot[r : r + 1], (16, segs * rays)).astype(BF16)
    hot = hot.astype(BF16)
    grad_narrow = grad_ray.astype(BF16)

    def mask_grads(r, carry):
        for k in range(segs):
            mask = hot_ref[r, :, k * rays : (k + 1) * rays]
            for at in range(0, feats, 16):
                rows = pl.ds(pl.multiple_of(r * feats + at, 16), 16)
                masked_ref[rows, k * rays : (k + 1) * rays] = grad_narrow[at : at + 16] * mask
        return carry

    lax.fori_loop(0, regions, mask_grads, 0, unroll=unroll)
    q_ref[...] = dot(wf_ref[...], masked_ref[...], 0, 0)
    feat_grad = dot(masked_ref[...], wide_hw_ref[0:hids], 1, 1).astype(BF16)
    for r in range(regions):
        out, to = (mine_ref, r) if r < half else (other_ref, r - half)
        out[to, WF_AT:G2_AT] = feat_grad[r * feats : (r + 1) * feats]
    later = jnp.zeros((1, rays), F32)
    for k in reversed(range(segs)):
        lanes = slice(k * rays, (k + 1) * rays)
        row_ref[:, lanes] = -later
        later = later + jnp.sum(att_hw_ref[:, lanes] * q_ref[:, lanes], axis=0, keepdims=True)

    def project(tile, carry):
        lanes = pl.ds(pl.multiple_of(tile * LANES, LANES), LANES)
        att = jnp.broadcast_to(att_ref[:, lanes], (8, LANES))
        sums = [jnp.zeros((8, LANES), F32)] * samples
        for ht in range(16):
            rows = slice(ht * 8, ht * 8 + 8)
            q = q_ref[rows, lanes] * att
            q_ref[rows, lanes] = q
            for s in range(samples):
                sums[s] = sums[s] + h_in[tile, s, rows, :] * q
        along_ref[:, lanes] = jnp.concatenate([jnp.sum(v, axis=0, keepdims=True) for v in sums], axis=0)
        return carry

    lax.fori_loop(0, 2 * segs, project, 0)
    along = along_ref[...]
    through = running_sum(along * weight_ref[...])
    later = through[samples - 1 : samples, :] - through
    grad_thick = row_ref[...] + along * pass_ref[...] - later
    along_ref[...] = (grad_thick * slope_ref[...]).astype(BF16).astype(F32)

    def descend(tile, carry):
        lanes = pl.ds(pl.multiple_of(tile * LANES, LANES), LANES)
        weight = weight_ref[:, lanes]
        grad_density = along_ref[:, lanes]
        scale = [jnp.broadcast_to(weight[s : s + 1, :], (8, LANES)) for s in range(samples)]
        slant = [jnp.broadcast_to(grad_density[s : s + 1, :], (8, LANES)) for s in range(samples)]
        for pair in range(8):
            at = [slice((2 * pair + u) * 8, (2 * pair + u) * 8 + 8) for u in range(2)]
            q = [q_ref[rows, lanes] for rows in at]
            wd = [wd_ref[tile, rows, :] for rows in at]
            g1 = [jnp.zeros((8, LANES), F32)] * 2
            hd = [jnp.zeros((8, LANES), F32)] * 2
            for s in range(samples):
                both = []
                for u in range(2):
                    h = h_in[tile, s, at[u], :]
                    gp = jnp.where(h > 0.0, scale[s] * q[u] + slant[s] * wd[u], 0.0)
                    g1[u] = g1[u] + gp
                    hd[u] = hd[u] + slant[s] * h
                    both.append(gp)
                gp_ref[s * hids + 16 * pair : s * hids + 16 * pair + 16, lanes] = jnp.concatenate(both, axis=0).astype(BF16)
            g1_ref[16 * pair : 16 * pair + 16, lanes] = jnp.concatenate(g1, axis=0).astype(BF16)
            hd_ref[16 * pair : 16 * pair + 16, lanes] = jnp.concatenate(hd, axis=0).astype(BF16)
        return carry

    lax.fori_loop(0, 2 * segs, descend, 0)
    tail_ref[...] = jnp.zeros(tail_ref.shape, F32)
    for s in range(samples):
        tail_ref[:, s, :] = dot(hot, gp_ref[s * hids : (s + 1) * hids], 1, 1)
    tail_ref[:, samples, :] = dot(hot, hd_ref[...], 1, 1)
    codes = codes_ref[...].astype(F32)
    g1 = g1_ref[...]
    for r in range(regions):
        out, to = (mine_ref, r) if r < half else (other_ref, r - half)
        held = jnp.concatenate([jnp.where(row == r, codes, 0.0).astype(BF16) for row in wanted], axis=1)
        out[to, 0:WF_AT] = dot(held, g1, 1, 1).astype(BF16)
        out[to, G2_AT:PART_ROWS] = tail_ref[r].astype(BF16)


def flip_kernel(target_ref, decoder_ref, near_ref, target_out, decoder_out, same_out, near_out):
    near_out[...] = near_ref[...]
    same_out[...] = decoder_ref[...]
    target_out[...] = target_ref[...].astype(F32).T.astype(BF16)
    decoder_out[...] = decoder_ref[...].astype(F32).T.astype(BF16)


def merge_kernel(mine_ref, theirs_ref, *outs):
    for k, out in enumerate(outs):
        for side in range(2):
            at = side * len(outs) + k
            out[side] = (mine_ref[at].astype(F32) + theirs_ref[at].astype(F32)).astype(BF16)


def reduce_kernel(*refs):
    parts, (keep_ref, send_ref) = refs[:-2], refs[-2:]
    for side, out in enumerate((keep_ref, send_ref)):
        total = parts[0][side].astype(F32)
        for part in parts[1:]:
            total = total + part[side].astype(F32)
        out[...] = total.astype(out.dtype)


def finish_kernel(keep_ref, part_ref, samp_ref, wh_ref, hid_ref, feat_ref, dens_ref, code_ref):
    total = keep_ref[...] + part_ref[...].astype(F32)
    high, low = split(total[G2_AT:DG_AT])
    samples = samp_ref[0]
    wh = wh_ref[0]
    hid_ref[0] = total[0:WF_AT] + dot(samples, high, 0, 0) + dot(samples, low, 0, 0)
    feat_ref[0] = total[WF_AT:G2_AT]
    dens_ref[...] = total[DG_AT : DG_AT + 1]
    code_ref[0] = dot(high, wh, 1, 1) + dot(low, wh, 1, 1)


def local(ray_code, seg_region, seg_count, pixel_of_ray, sample_code, w_hidden, w_feat, w_density, decoder, target):
    regions = lax.axis_size("region")
    half = regions // 2
    rays, segs = seg_region.shape
    code_width = ray_code.shape[1]
    hid_width = w_hidden.shape[2]
    feat_width = w_feat.shape[2]
    dino_width = target.shape[1]
    samples = sample_code.shape[1]
    group = rays // regions
    room = max(16, 2 * group)
    tiles = 2 * segs
    lanes = segs * rays
    inner = [(i, i ^ 1) for i in range(regions)]
    cross = [(i, i + 1) for i in range(1, regions - 1, 2)] + [(i + 1, i) for i in range(1, regions - 1, 2)]

    def shape(*dims, kind=F32):
        return jax.ShapeDtypeStruct(dims, kind)

    quarter = half // 2
    pack_rows = RAYS_AT + room

    def to_chip(block, k):
        return lax.ppermute(block, "region", [(i, i ^ (2 * k)) for i in range(regions)])

    def to_half(blocks):
        return [blocks[0]] + [to_chip(blocks[k], k) for k in range(1, quarter)]

    pack_args = (
        pixel_of_ray.reshape(1, rays), seg_region.T, seg_count.T,
        ray_code, sample_code, w_hidden, w_feat.swapaxes(1, 2), w_density,
    )
    near, far = pl.pallas_call(
        functools.partial(pack_kernel, half, group, room),
        out_shape=(
            shape(quarter, pack_rows, LANES, kind=BF16),
            shape(META_AT + quarter * (16 + room), LANES, kind=BF16),
        ),
        in_specs=[pl.BlockSpec(memory_space=pltpu.HBM)] * 8,
        scratch_shapes=[pltpu.VMEM(x.shape, x.dtype) for x in pack_args]
        + [
            pltpu.SemaphoreType.DMA((8,)),
            pltpu.VMEM((16, rays), F32),
            pltpu.VMEM((half * room, LANES), BF16),
        ],
        compiler_params=grant(60),
        name="pack",
    )(*pack_args)
    far = to_chip(far, quarter)
    flipped = pl.pallas_call(
        flip_kernel,
        out_shape=(
            shape(dino_width, rays, kind=BF16),
            shape(*decoder.shape[::-1], kind=BF16),
            shape(*decoder.shape, kind=BF16),
            shape(*near.shape, kind=BF16),
        ),
        compiler_params=grant(8 + regions / 8),
        name="flip",
    )(target, decoder, near)
    far, (target_t, decoder_t, decoder, near) = lax.optimization_barrier((far, flipped))
    blocks = to_half(
        pl.pallas_call(
            relay_kernel,
            out_shape=[shape(2, pack_rows, LANES, kind=BF16)] * quarter,
            compiler_params=grant(8 + regions / 8),
            name="relay",
        )(near, far)
    )
    blocks = blocks + [lax.ppermute(block, "region", inner) for block in blocks]

    image, halo_in, halo_cr, *kept = pl.pallas_call(
        functools.partial(forward_kernel, half, group, room),
        out_shape=(
            shape(feat_width, rays, kind=BF16),
            shape(feat_width + dino_width // 2, rays, kind=BF16),
            shape(feat_width + dino_width // 2, rays, kind=BF16),
            shape(tiles, samples, hid_width, LANES),
            shape(tiles, hid_width, LANES),
            shape(hid_width, lanes),
            shape(2 * hid_width, lanes, kind=BF16),
            shape(samples, lanes),
            shape(samples, lanes),
            shape(samples, lanes),
            shape(1, lanes),
            shape(segs, rays, kind=jnp.int32),
            shape(code_width, rays, kind=BF16),
            shape(regions * feat_width, hid_width, kind=BF16),
        ),
        scratch_shapes=[
            pltpu.VMEM((16, regions * room), F32),
            pltpu.VMEM((samples + 1, regions, hid_width), F32),
            pltpu.VMEM((samples + 1, hid_width, 2 * regions), BF16),
            pltpu.VMEM((regions, hid_width, rays), F32),
            pltpu.VMEM((tiles, hid_width, LANES), F32),
            pltpu.VMEM((tiles, 2 * regions, LANES), BF16),
            pltpu.VMEM((1, lanes), F32),
            pltpu.VMEM((samples, lanes), F32),
        ],
        compiler_params=grant(10 + regions / 4),
        name="forward",
    )(*blocks, target_t)

    halo_in = lax.ppermute(halo_in, "region", inner)
    halo_cr = lax.ppermute(halo_cr, "region", cross)

    part = shape(half, PART_ROWS, LANES, kind=BF16)
    mine, other = pl.pallas_call(
        functools.partial(backward_kernel, half),
        out_shape=(part, part),
        scratch_shapes=[
            pltpu.VMEM((decoder.shape[0], 4 * IW), BF16),
            pltpu.VMEM((regions * feat_width, lanes), BF16),
            pltpu.VMEM((hid_width, lanes), F32),
            pltpu.VMEM((samples * hid_width, lanes), BF16),
            pltpu.VMEM((hid_width, lanes), BF16),
            pltpu.VMEM((hid_width, lanes), BF16),
            pltpu.VMEM((regions, PART_ROWS - G2_AT, hid_width), F32),
            pltpu.VMEM((1, lanes), F32),
            pltpu.VMEM((samples, lanes), F32),
            pltpu.VMEM((regions, 16, lanes), BF16),
        ],
        compiler_params=grant(22 + regions / 4),
        name="backward",
    )(image, halo_in, halo_cr, target_t, decoder, decoder_t, *kept)

    theirs = lax.ppermute(other, "region", inner)
    parts = pl.pallas_call(
        merge_kernel,
        out_shape=[shape(2, PART_ROWS, LANES, kind=BF16)] * quarter,
        compiler_params=grant(8 + regions / 8),
        name="merge",
    )(mine, theirs)
    keep, send = pl.pallas_call(
        reduce_kernel,
        out_shape=(shape(PART_ROWS, LANES), shape(PART_ROWS, LANES, kind=BF16)),
        compiler_params=grant(8 + regions / 8),
        name="reduce",
    )(*to_half(parts))
    hid_grad, feat_grad, dens_grad, code_grad = pl.pallas_call(
        finish_kernel,
        out_shape=(
            shape(1, code_width, hid_width),
            shape(1, feat_width, hid_width),
            shape(1, hid_width),
            shape(1, samples, code_width),
        ),
        compiler_params=grant(8 + regions / 8),
        name="finish",
    )(keep, to_chip(send, quarter), sample_code, w_hidden)
    return hid_grad, feat_grad.swapaxes(1, 2), dens_grad, code_grad


def solution(mesh):
    in_specs = (
        P(("groups", "region"), None),
        P(("groups", "region"), None),
        P(("groups", "region"), None),
        P(("groups", "region")),
        P("region", None, None),
        P("region", None, None),
        P("region", None, None),
        P("region", None),
        P(),
        P(("groups", "region"), None),
    )
    out_specs = (
        P("region", "groups", None),
        P("region", "groups", None),
        P("region", "groups"),
        P("region", "groups", None),
    )
    return jax.shard_map(local, mesh=mesh, in_specs=in_specs, out_specs=out_specs, check_vma=False)
```

```python
import functools

import jax
import jax.numpy as jnp
from jax import lax
from jax.experimental import pallas as pl
from jax.experimental.pallas import tpu as pltpu
from jax.sharding import PartitionSpec as P

IW = 128
STEP = 0.08
F32 = jnp.float32
BF16 = jnp.bfloat16
LANES = 128

WF_AT = 128
SAMPLE_AT = 192
META_AT = 208
RAYS_AT = 224
G2_AT = 192
DG_AT = 208
PART_ROWS = 216


def grant(mib):
    return pltpu.CompilerParams(vmem_limit_bytes=int(mib * (1 << 20)))


def iota(shape, dim):
    return lax.broadcasted_iota(jnp.int32, shape, dim)


def dot(lhs, rhs, left=1, right=0):
    return lax.dot_general(lhs, rhs, (((left,), (right,)), ((), ())), preferred_element_type=F32)


def split(values):
    high = values.astype(BF16)
    return high, (values - high.astype(F32)).astype(BF16)


def running_sum(values):
    rows = values.shape[0]
    row = iota(values.shape, 0)
    step = 1
    while step < rows:
        values = values + jnp.where(row >= step, pltpu.roll(values, step, 0), 0.0)
        step *= 2
    return values


def pack_kernel(half, group, room, *refs):
    hbm, (near_ref, far_ref), held, sems = refs[:8], refs[8:10], refs[10:18], refs[18]
    meta_ref, codes_ref = refs[19:]
    me = lax.axis_index("region")
    mine = lax.shift_right_logical(me, 1)
    copies = [pltpu.make_async_copy(hbm[i], held[i], sems.at[i]) for i in range(8)]
    for copy in copies:
        copy.start()
    for copy in copies:
        copy.wait()
    pix_ref, reg_ref, cnt_ref, code_ref, samp_ref, wh_ref, wf_ref, wd_ref = held
    rays = code_ref.shape[0]
    regions = 2 * half
    shift = rays.bit_length() - 1
    pix = pix_ref[...]
    tile = lax.shift_right_logical(pix, shift)
    spot = pix & (rays - 1)
    same = jnp.where(iota((regions, rays), 0) == tile, 1.0, 0.0)
    earlier = jnp.where(iota((rays, rays), 0) < iota((rays, rays), 1), 1.0, 0.0).astype(BF16)
    counts = dot(same.astype(BF16), earlier)
    rank = jnp.sum(counts * same, axis=0, keepdims=True).astype(jnp.int32)
    row_place = lax.shift_right_logical(tile, 1) * room + (tile & 1) * group + rank
    lane_place = tile * group + rank
    meta_ref[...] = jnp.zeros(meta_ref.shape, F32)
    meta_ref[1:2, :] = spot.astype(F32)
    meta_ref[2:6, :] = reg_ref[...].astype(F32)
    meta_ref[6:10, :] = cnt_ref[...].astype(F32)
    row_hot = jnp.where(iota((half * room, rays), 0) == row_place, 1.0, 0.0).astype(BF16)
    codes_ref[...] = dot(row_hot, code_ref[...]).astype(BF16)
    lane_hot = jnp.where(iota((rays, rays), 0) == lane_place, 1.0, 0.0).astype(BF16)
    meta = dot(meta_ref[...].astype(BF16), lane_hot, 1, 1)
    wh_t = wh_ref[0].astype(F32).T.astype(BF16)
    density = wd_ref[...].astype(F32)
    first = iota((16, LANES), 0) == 0

    def rays_for(k):
        chip = jnp.bitwise_xor(mine, k)
        here = pltpu.roll(meta, (rays - chip * 2 * group) & (rays - 1), 1)[:, :LANES]
        codes = codes_ref[pl.ds(pl.multiple_of(chip * room, 16), room), :]
        return jnp.where(first, density, here).astype(BF16), codes

    for side, ref in enumerate((near_ref, far_ref)):
        ref[0:WF_AT] = wh_t
        ref[WF_AT:SAMPLE_AT] = wf_ref[0]
        ref[SAMPLE_AT:META_AT] = samp_ref[0]
        for k in range(half // 2):
            at = META_AT + k * (16 + room)
            ref[at : at + 16], ref[at + 16 : at + 16 + room] = rays_for(k + side * (half // 2))


def relay_kernel(near_ref, far_ref, *outs):
    for k, out in enumerate(outs):
        rows = out.shape[1] - META_AT
        for side, ref in enumerate((near_ref, far_ref)):
            out[side, 0:META_AT] = ref[0:META_AT]
            out[side, META_AT:] = ref[META_AT + k * rows : META_AT + (k + 1) * rows]


def bits_of(row, regions):
    count = regions.bit_length() - 1
    row = jnp.broadcast_to(row, (8, LANES))
    return [(lax.shift_right_logical(row, b) & 1) == 1 for b in range(count)]


def choose(values, bits):
    for bit in bits:
        values = [jnp.where(bit, values[i + 1], values[i]) for i in range(0, len(values), 2)]
    return values[0]


def fold(source_ref, rel_ref, out_ref):
    segs, rays = rel_ref.shape
    regions = out_ref.shape[0]

    def step(pair, carry):
        rows = pl.ds(pl.multiple_of(pair * 16, 16), 16)
        for part in range(rays // LANES):
            lanes = slice(part * LANES, (part + 1) * LANES)
            rel = [jnp.broadcast_to(rel_ref[k : k + 1, lanes], (16, LANES)) for k in range(segs)]
            held = [source_ref[rows, k * rays + part * LANES : k * rays + (part + 1) * LANES] for k in range(segs)]
            for r in range(regions):
                total = jnp.where(rel[0] == r, held[0], 0.0)
                for k in range(1, segs):
                    total = jnp.where(rel[k] == r, held[k], total)
                out_ref[r, rows, lanes] = total.astype(BF16)
        return carry

    lax.fori_loop(0, source_ref.shape[0] // 16, step, 0, unroll=2)


def fold_kernel(source_ref, rel_ref, out_ref):
    fold(source_ref, rel_ref, out_ref)


def pick(source_ref, rel_ref, out_ref, first=0):
    segs, rays = rel_ref.shape
    regions = source_ref.shape[0]
    for part in range(rays // LANES):
        lanes = slice(part * LANES, (part + 1) * LANES)

        def step(index, carry):
            rows = pl.ds(pl.multiple_of(index * 8, 8), 8)
            bits = [bits_of(rel_ref[k : k + 1, lanes], regions) for k in range(segs)]
            values = [source_ref[r, rows, lanes] for r in range(regions)]
            for k in range(segs):
                found = choose(values, bits[k])
                at = slice(k * rays + part * LANES, k * rays + (part + 1) * LANES)
                if first > 0:
                    here = lax.shift_right_logical(rel_ref[k : k + 1, lanes], len(bits[k])) == first // regions
                    found = jnp.where(here, found, out_ref[rows, at])
                out_ref[rows, at] = found
            return carry

        lax.fori_loop(0, source_ref.shape[1] // 8, step, 0, unroll=4)


def seg_hot(wanted, regions):
    return jnp.concatenate(
        [jnp.where(iota((regions, row.shape[1]), 0) == row, 1.0, 0.0) for row in wanted], axis=1
    )


def forward_kernel(half, group, room, *refs):
    regions = 2 * half
    quarter = half // 2
    received, target_ref = refs[:half], refs[half]
    blocks = [received[c * quarter + k].at[side] for c in range(2) for side in range(2) for k in range(quarter)]
    (
        image_ref, halo_in_ref, halo_cr_ref, h_ref, wd_ref, att_hw_ref, weight_ref, pass_ref, slope_ref, att_ref, rel_ref, codes_ref, wf_up,
        wide_hw_ref, wf_out,        meta_ref, plain_ref, table_ref, proj_ref, a_ref, picked_ref, row_ref, density_ref,
    ) = refs[half + 1 :]
    rays = codes_ref.shape[1]
    segs = rel_ref.shape[0]
    samples = weight_ref.shape[0]
    feats = image_ref.shape[0]
    hids = table_ref.shape[1]
    me = lax.axis_index("region")
    core = me & 1
    chip = lax.shift_right_logical(me, 1)
    per_tile = LANES // room
    lane = iota((16, LANES), 1)
    chunk = lax.div(lane, room)
    inside = lane - chunk * room
    mine = (inside < 2 * group) & (lax.div(inside, group) == core)
    for tile in range(regions // per_tile):
        total = jnp.zeros((16, LANES), F32)
        for spot in range(per_tile):
            block = blocks[tile * per_tile + spot][META_AT:RAYS_AT].astype(F32)
            total = jnp.where(chunk == spot, pltpu.roll(block, spot * room, 1), total)
        meta_ref[:, tile * LANES : (tile + 1) * LANES] = jnp.where(mine, total, -1.0)
    meta_src = meta_ref[...]
    places = regions * room
    to_pixel = jnp.where(
        iota((rays, places), 0).astype(F32) == meta_src[1:2, :], 1.0, 0.0
    ).astype(BF16)
    sources = jnp.concatenate([block[RAYS_AT : RAYS_AT + room] for block in blocks], axis=0)
    codes_t = dot(to_pixel, sources).T.astype(BF16)
    codes_ref[...] = codes_t
    meta = dot(meta_src.astype(BF16), to_pixel, 1, 1)
    region = meta[2 : 2 + segs].astype(jnp.int32)
    rel = jnp.bitwise_xor(region & 1, core) * half + jnp.bitwise_xor(lax.shift_right_logical(region, 1), chip)
    rel_ref[...] = rel
    for k in range(segs):
        row_ref[:, k * rays : (k + 1) * rays] = meta[6 + k : 7 + k]
    wanted = [rel_ref[k : k + 1, :] for k in range(segs)]
    for r, block in enumerate(blocks):
        w_t = block[0:WF_AT]
        proj_ref[r] = dot(w_t, codes_t)
        plain_ref[0:samples, r, :] = dot(block[SAMPLE_AT:META_AT], w_t, 1, 1)
        plain_ref[samples, r : r + 1, :] = block[META_AT:RAYS_AT].astype(F32)[0:1, :]
        wf_out[r * feats : (r + 1) * feats] = block[WF_AT:SAMPLE_AT]
        wf_up[r] = block[WF_AT:SAMPLE_AT].astype(F32).T.astype(BF16)
    for s in range(samples + 1):
        high, low = split(plain_ref[s])
        table_ref[s] = jnp.concatenate([high.astype(F32), low.astype(F32)], axis=0).T.astype(BF16)
    pick(proj_ref, rel_ref, a_ref)
    hot = seg_hot(wanted, regions).astype(BF16)
    hot2 = jnp.concatenate([hot, hot], axis=0)
    for tile in range(2 * segs):
        picked_ref[tile] = hot2[:, tile * LANES : (tile + 1) * LANES]

    def densities(tile, carry):
        here = picked_ref[tile]
        lanes = pl.ds(pl.multiple_of(tile * LANES, LANES), LANES)
        wd_ref[tile] = dot(table_ref[samples], here)
        sums = []
        for s in range(samples):
            h = jnp.maximum(a_ref[:, lanes] + dot(table_ref[s], here), 0.0)
            h_ref[tile, s] = h
            sums.append(jnp.sum(h * wd_ref[tile], axis=0, keepdims=True))
        density_ref[:, lanes] = jnp.concatenate(sums, axis=0)
        return carry

    lax.fori_loop(0, 2 * segs, densities, 0, unroll=4)
    density = density_ref[...]
    live = iota(density.shape, 0).astype(F32) < row_ref[...]
    soft = jnp.maximum(density, 0.0) + jnp.log1p(jnp.exp(-jnp.abs(density)))
    thick = jnp.where(live, STEP * soft, 0.0)
    through = running_sum(thick)
    passing = jnp.exp(-(through - thick))
    keeping = jnp.exp(-thick)
    weight = passing * (1.0 - keeping)
    weight_ref[...] = weight
    pass_ref[...] = passing * keeping
    slope_ref[...] = jnp.where(live, STEP / (1.0 + jnp.exp(-density)), 0.0)
    ahead = jnp.zeros((1, rays), F32)
    for k in range(segs):
        att_ref[:, k * rays : (k + 1) * rays] = jnp.exp(-ahead)
        ahead = ahead + through[samples - 1 : samples, k * rays : (k + 1) * rays]
    density_ref[...] = weight * att_ref[...]

    def compose(tile, carry):
        lanes = pl.ds(pl.multiple_of(tile * LANES, LANES), LANES)
        faded = density_ref[:, lanes]
        scale = [jnp.broadcast_to(faded[s : s + 1, :], (8, LANES)) for s in range(samples)]
        for pair in range(8):
            both = []
            for ht in (2 * pair, 2 * pair + 1):
                rows = slice(ht * 8, ht * 8 + 8)
                total = scale[0] * h_ref[tile, 0, rows, :]
                for s in range(1, samples):
                    total = total + scale[s] * h_ref[tile, s, rows, :]
                both.append(total)
            both = jnp.concatenate(both, axis=0)
            high, low = split(both)
            att_hw_ref[pair * 16 : pair * 16 + 16, lanes] = both
            wide_hw_ref[pair * 16 : pair * 16 + 16, lanes] = high
            wide_hw_ref[hids + pair * 16 : hids + pair * 16 + 16, lanes] = low
        return carry

    lax.fori_loop(0, 2 * segs, compose, 0, unroll=2)
    wf_twice = jnp.concatenate([wf_out[...], wf_out[...]], axis=1)
    feat = [jnp.zeros((8, LANES), F32)] * (2 * (feats // 8))
    for k in range(segs):
        values = dot(wf_twice, wide_hw_ref[:, k * rays : (k + 1) * rays])
        for r in range(regions * feats // LANES):
            proj_ref[r] = values[r * LANES : (r + 1) * LANES]
        for part in range(2):
            lanes = slice(part * LANES, (part + 1) * LANES)
            bits = bits_of(wanted[k][:, lanes], regions)
            for ft in range(feats // 8):
                found = []
                for r in range(regions):
                    at = r * feats + ft * 8
                    found.append(proj_ref[at // LANES, at % LANES : at % LANES + 8, lanes])
                feat[2 * ft + part] = feat[2 * ft + part] + choose(found, bits)
    for part in range(2):
        image_ref[:, part * LANES : (part + 1) * LANES] = jnp.concatenate(feat[part::2], axis=0).astype(BF16)
    near, far = target_ref[:, :IW].astype(F32), target_ref[:, rays - IW :].astype(F32)
    for out_ref, row in ((halo_in_ref, jnp.where(core == 0, far, near)), (halo_cr_ref, jnp.where(core == 0, near, far))):
        out_ref[0:feats] = image_ref[...]
        depth = target_ref.shape[0] // 2
        out_ref[feats:, 0:IW] = row[:depth].astype(BF16)
        out_ref[feats:, rays - IW :] = row[depth:].astype(BF16)


def shifted(values, by):
    lane = iota(values.shape, 1)
    if by == 0:
        return values
    if by > 0:
        return jnp.where(lane == 0, 0.0, pltpu.roll(values, 1, 1))
    return jnp.where(lane == LANES - 1, 0.0, pltpu.roll(values, LANES - 1, 1))


def backward_kernel(
    half, own_ref, inner_ref, cross_ref, tgt_ref, dec_ref, dect_ref,
    folded_ref, h_in, wd_ref, att_hw_ref, weight_ref, pass_ref, slope_ref, att_ref, rel_ref, codes_ref, wf_ref,
    mine_ref, other_ref,
    patch_ref, proj_ref, q_ref, gp_ref, g1_ref, held_ref, hd_ref, tail_ref, row_ref, along_ref,
):
    regions = 2 * half
    feats, rays = own_ref.shape
    segs = rel_ref.shape[0]
    samples = weight_ref.shape[0]
    hids = wd_ref.shape[1]
    me = lax.axis_index("region")
    core = me & 1
    own = own_ref[...].astype(F32)
    halo_in = inner_ref[...].astype(F32)
    halo_cr = cross_ref[...].astype(F32)
    inner, tin = halo_in[:feats], jnp.concatenate([halo_in[feats:, :IW], halo_in[feats:, rays - IW :]], axis=0)
    cross, tcr = halo_cr[:feats], jnp.concatenate([halo_cr[feats:, :IW], halo_cr[feats:, rays - IW :]], axis=0)
    top = jnp.where(core == 0, cross, inner)
    bottom = jnp.where(core == 0, inner, cross)
    rows = [v[:, i * IW : (i + 1) * IW] for v in (top, own, bottom) for i in range(2)]
    for at, row in enumerate(rows):
        for dx in range(3):
            piece = shifted(row, 1 - dx).astype(BF16)
            for dy in range(3):
                if 0 <= at - dy < 4:
                    patch_ref[(3 * dy + dx) * feats : (3 * dy + dx + 1) * feats, (at - dy) * IW : (at - dy + 1) * IW] = piece
    t_top = jnp.where(core == 0, tcr, tin)
    t_bottom = jnp.where(core == 0, tin, tcr)
    decoded = dot(dect_ref[...], patch_ref[...])
    tgt = tgt_ref[...].astype(F32)
    g_top = jnp.where(me > 0, decoded[:, 0:IW] - t_top, 0.0)
    g_own = decoded[:, IW : 3 * IW] - tgt
    g_bottom = jnp.where(me < regions - 1, decoded[:, 3 * IW :] - t_bottom, 0.0)
    grad_dec = jnp.concatenate([g_top, g_own, g_bottom], axis=1).astype(BF16)
    grad_patch = dot(dec_ref[...], grad_dec)
    image_rows = []
    for i in range(2):
        total = jnp.zeros((feats, IW), F32)
        for dx in range(3):
            term = jnp.zeros((feats, IW), F32)
            for dy in range(3):
                at = (3 * dy + dx) * feats
                term = term + grad_patch[at : at + feats, (i - dy + 2) * IW : (i - dy + 3) * IW]
            total = total + shifted(term, dx - 1)
        image_rows.append(total)
    grad_ray = jnp.concatenate(image_rows, axis=1)
    wanted = [rel_ref[k : k + 1, :] for k in range(segs)]
    hot = seg_hot(wanted, regions).astype(BF16)
    grad_narrow = grad_ray.astype(BF16)
    group = proj_ref.shape[0]
    for r in range(regions):
        proj_ref[r % group] = dot(wf_ref[r], grad_narrow)
        out, to = (mine_ref, r) if r < half else (other_ref, r - half)
        out[to, WF_AT:G2_AT] = dot(grad_narrow, folded_ref[r], 1, 1).astype(BF16)
        if (r + 1) % group == 0:
            pick(proj_ref, rel_ref, q_ref, r + 1 - group)
    later = jnp.zeros((1, rays), F32)
    for k in reversed(range(segs)):
        lanes = slice(k * rays, (k + 1) * rays)
        row_ref[:, lanes] = -later
        later = later + jnp.sum(att_hw_ref[:, lanes] * q_ref[:, lanes], axis=0, keepdims=True)

    def project(tile, carry):
        lanes = pl.ds(pl.multiple_of(tile * LANES, LANES), LANES)
        att = jnp.broadcast_to(att_ref[:, lanes], (8, LANES))
        sums = [jnp.zeros((8, LANES), F32)] * samples
        for ht in range(16):
            rows = slice(ht * 8, ht * 8 + 8)
            q = q_ref[rows, lanes] * att
            q_ref[rows, lanes] = q
            for s in range(samples):
                sums[s] = sums[s] + h_in[tile, s, rows, :] * q
        along_ref[:, lanes] = jnp.concatenate([jnp.sum(v, axis=0, keepdims=True) for v in sums], axis=0)
        return carry

    lax.fori_loop(0, 2 * segs, project, 0)
    along = along_ref[...]
    through = running_sum(along * weight_ref[...])
    later = through[samples - 1 : samples, :] - through
    grad_thick = row_ref[...] + along * pass_ref[...] - later
    along_ref[...] = (grad_thick * slope_ref[...]).astype(BF16).astype(F32)

    def descend(tile, carry):
        lanes = pl.ds(pl.multiple_of(tile * LANES, LANES), LANES)
        weight = weight_ref[:, lanes]
        grad_density = along_ref[:, lanes]
        scale = [jnp.broadcast_to(weight[s : s + 1, :], (8, LANES)) for s in range(samples)]
        slant = [jnp.broadcast_to(grad_density[s : s + 1, :], (8, LANES)) for s in range(samples)]
        for pair in range(8):
            at = [slice((2 * pair + u) * 8, (2 * pair + u) * 8 + 8) for u in range(2)]
            q = [q_ref[rows, lanes] for rows in at]
            wd = [wd_ref[tile, rows, :] for rows in at]
            g1 = [jnp.zeros((8, LANES), F32)] * 2
            hd = [jnp.zeros((8, LANES), F32)] * 2
            for s in range(samples):
                both = []
                for u in range(2):
                    h = h_in[tile, s, at[u], :]
                    gp = jnp.where(h > 0.0, scale[s] * q[u] + slant[s] * wd[u], 0.0)
                    g1[u] = g1[u] + gp
                    hd[u] = hd[u] + slant[s] * h
                    both.append(gp)
                gp_ref[s * hids + 16 * pair : s * hids + 16 * pair + 16, lanes] = jnp.concatenate(both, axis=0).astype(BF16)
            g1_ref[16 * pair : 16 * pair + 16, lanes] = jnp.concatenate(g1, axis=0)
            hd_ref[16 * pair : 16 * pair + 16, lanes] = jnp.concatenate(hd, axis=0).astype(BF16)
        return carry

    lax.fori_loop(0, 2 * segs, descend, 0)
    tail_ref[...] = jnp.zeros(tail_ref.shape, F32)
    for s in range(samples):
        tail_ref[:, s, :] = dot(hot, gp_ref[s * hids : (s + 1) * hids], 1, 1)
    tail_ref[:, samples, :] = dot(hot, hd_ref[...], 1, 1)
    codes = codes_ref[...]
    fold(g1_ref, rel_ref, held_ref)
    for r in range(regions):
        out, to = (mine_ref, r) if r < half else (other_ref, r - half)
        out[to, 0:WF_AT] = dot(codes, held_ref[r], 1, 1).astype(BF16)
        out[to, G2_AT:PART_ROWS] = tail_ref[r].astype(BF16)


def flip_kernel(target_ref, decoder_ref, near_ref, target_out, decoder_out, same_out, near_out):
    near_out[...] = near_ref[...]
    same_out[...] = decoder_ref[...]
    target_out[...] = target_ref[...].astype(F32).T.astype(BF16)
    decoder_out[...] = decoder_ref[...].astype(F32).T.astype(BF16)


def merge_kernel(mine_ref, theirs_ref, *outs):
    for k, out in enumerate(outs):
        for side in range(2):
            at = side * len(outs) + k
            out[side] = (mine_ref[at].astype(F32) + theirs_ref[at].astype(F32)).astype(BF16)


def reduce_kernel(*refs):
    parts, (keep_ref, send_ref) = refs[:-2], refs[-2:]
    for side, out in enumerate((keep_ref, send_ref)):
        total = parts[0][side].astype(F32)
        for part in parts[1:]:
            total = total + part[side].astype(F32)
        out[...] = total.astype(out.dtype)


def finish_kernel(keep_ref, part_ref, samp_ref, wh_ref, hid_ref, feat_ref, dens_ref, code_ref):
    total = keep_ref[...] + part_ref[...].astype(F32)
    high, low = split(total[G2_AT:DG_AT])
    samples = samp_ref[0]
    wh = wh_ref[0]
    hid_ref[0] = total[0:WF_AT] + dot(samples, high, 0, 0) + dot(samples, low, 0, 0)
    feat_ref[0] = total[WF_AT:G2_AT]
    dens_ref[...] = total[DG_AT : DG_AT + 1]
    code_ref[0] = dot(high, wh, 1, 1) + dot(low, wh, 1, 1)


def local(ray_code, seg_region, seg_count, pixel_of_ray, sample_code, w_hidden, w_feat, w_density, decoder, target):
    regions = lax.axis_size("region")
    half = regions // 2
    rays, segs = seg_region.shape
    code_width = ray_code.shape[1]
    hid_width = w_hidden.shape[2]
    feat_width = w_feat.shape[2]
    dino_width = target.shape[1]
    samples = sample_code.shape[1]
    group = rays // regions
    room = max(16, 2 * group)
    tiles = 2 * segs
    lanes = segs * rays
    inner = [(i, i ^ 1) for i in range(regions)]
    cross = [(i, i + 1) for i in range(1, regions - 1, 2)] + [(i + 1, i) for i in range(1, regions - 1, 2)]

    def shape(*dims, kind=F32):
        return jax.ShapeDtypeStruct(dims, kind)

    quarter = half // 2
    pack_rows = RAYS_AT + room

    def to_chip(block, k):
        return lax.ppermute(block, "region", [(i, i ^ (2 * k)) for i in range(regions)])

    def to_half(blocks):
        return [blocks[0]] + [to_chip(blocks[k], k) for k in range(1, quarter)]

    pack_args = (
        pixel_of_ray.reshape(1, rays), seg_region.T, seg_count.T,
        ray_code, sample_code, w_hidden, w_feat.swapaxes(1, 2), w_density,
    )
    near, far = pl.pallas_call(
        functools.partial(pack_kernel, half, group, room),
        out_shape=(
            shape(META_AT + quarter * (16 + room), LANES, kind=BF16),
            shape(META_AT + quarter * (16 + room), LANES, kind=BF16),
        ),
        in_specs=[pl.BlockSpec(memory_space=pltpu.HBM)] * 8,
        scratch_shapes=[pltpu.VMEM(x.shape, x.dtype) for x in pack_args]
        + [
            pltpu.SemaphoreType.DMA((8,)),
            pltpu.VMEM((16, rays), F32),
            pltpu.VMEM((half * room, LANES), BF16),
        ],
        compiler_params=grant(60),
        name="pack",
    )(*pack_args)
    far = to_chip(far, quarter)
    flipped = pl.pallas_call(
        flip_kernel,
        out_shape=(
            shape(dino_width, rays, kind=BF16),
            shape(*decoder.shape[::-1], kind=BF16),
            shape(*decoder.shape, kind=BF16),
            shape(*near.shape, kind=BF16),
        ),
        compiler_params=grant(8 + regions / 8),
        name="flip",
    )(target, decoder, near)
    far, (target_t, decoder_t, decoder, near) = lax.optimization_barrier((far, flipped))
    blocks = to_half(
        pl.pallas_call(
            relay_kernel,
            out_shape=[shape(2, pack_rows, LANES, kind=BF16)] * quarter,
            compiler_params=grant(8 + regions / 8),
            name="relay",
        )(near, far)
    )
    blocks = blocks + [lax.ppermute(block, "region", inner) for block in blocks]

    image, halo_in, halo_cr, *kept = pl.pallas_call(
        functools.partial(forward_kernel, half, group, room),
        out_shape=(
            shape(feat_width, rays, kind=BF16),
            shape(feat_width + dino_width // 2, rays, kind=BF16),
            shape(feat_width + dino_width // 2, rays, kind=BF16),
            shape(tiles, samples, hid_width, LANES),
            shape(tiles, hid_width, LANES),
            shape(hid_width, lanes),
            shape(samples, lanes),
            shape(samples, lanes),
            shape(samples, lanes),
            shape(1, lanes),
            shape(segs, rays, kind=jnp.int32),
            shape(code_width, rays, kind=BF16),
            shape(regions, hid_width, feat_width, kind=BF16),
        ),
        scratch_shapes=[
            pltpu.VMEM((2 * hid_width, lanes), BF16),
            pltpu.VMEM((regions * feat_width, hid_width), BF16),
            pltpu.VMEM((16, regions * room), F32),
            pltpu.VMEM((samples + 1, regions, hid_width), F32),
            pltpu.VMEM((samples + 1, hid_width, 2 * regions), BF16),
            pltpu.VMEM((regions, hid_width, rays), F32),
            pltpu.VMEM((hid_width, lanes), F32),
            pltpu.VMEM((tiles, 2 * regions, LANES), BF16),
            pltpu.VMEM((1, lanes), F32),
            pltpu.VMEM((samples, lanes), F32),
        ],
        compiler_params=grant(10 + regions / 4),
        name="forward",
    )(*blocks, target_t)

    halo_in = lax.ppermute(halo_in, "region", inner)
    halo_cr = lax.ppermute(halo_cr, "region", cross)
    folded = pl.pallas_call(
        fold_kernel,
        out_shape=shape(regions, hid_width, rays, kind=BF16),
        compiler_params=grant(8 + regions / 4),
        name="fold",
    )(kept[2], kept[7])

    part = shape(half, PART_ROWS, LANES, kind=BF16)
    mine, other = pl.pallas_call(
        functools.partial(backward_kernel, half),
        out_shape=(part, part),
        scratch_shapes=[
            pltpu.VMEM((decoder.shape[0], 4 * IW), BF16),
            pltpu.VMEM((min(regions, 16), hid_width, rays), F32),
            pltpu.VMEM((hid_width, lanes), F32),
            pltpu.VMEM((samples * hid_width, lanes), BF16),
            pltpu.VMEM((hid_width, lanes), F32),
            pltpu.VMEM((regions, hid_width, rays), BF16),
            pltpu.VMEM((hid_width, lanes), BF16),
            pltpu.VMEM((regions, PART_ROWS - G2_AT, hid_width), F32),
            pltpu.VMEM((1, lanes), F32),
            pltpu.VMEM((samples, lanes), F32),
        ],
        compiler_params=grant(22 + regions / 4),
        name="backward",
    )(image, halo_in, halo_cr, target_t, decoder, decoder_t, folded, *kept)

    theirs = lax.ppermute(other, "region", inner)
    parts = pl.pallas_call(
        merge_kernel,
        out_shape=[shape(2, PART_ROWS, LANES, kind=BF16)] * quarter,
        compiler_params=grant(8 + regions / 8),
        name="merge",
    )(mine, theirs)
    keep, send = pl.pallas_call(
        reduce_kernel,
        out_shape=(shape(PART_ROWS, LANES), shape(PART_ROWS, LANES, kind=BF16)),
        compiler_params=grant(8 + regions / 8),
        name="reduce",
    )(*to_half(parts))
    hid_grad, feat_grad, dens_grad, code_grad = pl.pallas_call(
        finish_kernel,
        out_shape=(
            shape(1, code_width, hid_width),
            shape(1, feat_width, hid_width),
            shape(1, hid_width),
            shape(1, samples, code_width),
        ),
        compiler_params=grant(8 + regions / 8),
        name="finish",
    )(keep, to_chip(send, quarter), sample_code, w_hidden)
    return hid_grad, feat_grad.swapaxes(1, 2), dens_grad, code_grad


def solution(mesh):
    in_specs = (
        P(("groups", "region"), None),
        P(("groups", "region"), None),
        P(("groups", "region"), None),
        P(("groups", "region")),
        P("region", None, None),
        P("region", None, None),
        P("region", None, None),
        P("region", None),
        P(),
        P(("groups", "region"), None),
    )
    out_specs = (
        P("region", "groups", None),
        P("region", "groups", None),
        P("region", "groups"),
        P("region", "groups", None),
    )
    return jax.shard_map(local, mesh=mesh, in_specs=in_specs, out_specs=out_specs, check_vma=False)
```

```python
import functools

import jax
import jax.numpy as jnp
from jax import lax
from jax.experimental import pallas as pl
from jax.experimental.pallas import tpu as pltpu
from jax.sharding import PartitionSpec as P

IW = 128
STEP = 0.08
F32 = jnp.float32
BF16 = jnp.bfloat16
LANES = 128

WF_AT = 128
SAMPLE_AT = 192
META_AT = 208
RAYS_AT = 224
G2_AT = 192
DG_AT = 208
PART_ROWS = 216


def grant(mib):
    return pltpu.CompilerParams(vmem_limit_bytes=int(mib * (1 << 20)))


def iota(shape, dim):
    return lax.broadcasted_iota(jnp.int32, shape, dim)


def dot(lhs, rhs, left=1, right=0):
    return lax.dot_general(lhs, rhs, (((left,), (right,)), ((), ())), preferred_element_type=F32)


def split(values):
    high = values.astype(BF16)
    return high, (values - high.astype(F32)).astype(BF16)


def running_sum(values):
    rows = values.shape[0]
    row = iota(values.shape, 0)
    step = 1
    while step < rows:
        values = values + jnp.where(row >= step, pltpu.roll(values, step, 0), 0.0)
        step *= 2
    return values


def pack_kernel(half, group, room, *refs):
    hbm, (near_ref, far_ref), held, sems = refs[:8], refs[8:10], refs[10:18], refs[18]
    meta_ref, codes_ref = refs[19:]
    me = lax.axis_index("region")
    mine = lax.shift_right_logical(me, 1)
    copies = [pltpu.make_async_copy(hbm[i], held[i], sems.at[i]) for i in range(8)]
    for copy in copies:
        copy.start()
    for copy in copies:
        copy.wait()
    pix_ref, reg_ref, cnt_ref, code_ref, samp_ref, wh_ref, wf_ref, wd_ref = held
    rays = code_ref.shape[0]
    regions = 2 * half
    shift = rays.bit_length() - 1
    pix = pix_ref[...]
    tile = lax.shift_right_logical(pix, shift)
    spot = pix & (rays - 1)
    same = jnp.where(iota((regions, rays), 0) == tile, 1.0, 0.0)
    earlier = jnp.where(iota((rays, rays), 0) < iota((rays, rays), 1), 1.0, 0.0).astype(BF16)
    counts = dot(same.astype(BF16), earlier)
    rank = jnp.sum(counts * same, axis=0, keepdims=True).astype(jnp.int32)
    row_place = lax.shift_right_logical(tile, 1) * room + (tile & 1) * group + rank
    lane_place = tile * group + rank
    meta_ref[...] = jnp.zeros(meta_ref.shape, F32)
    meta_ref[1:2, :] = spot.astype(F32)
    meta_ref[2:6, :] = reg_ref[...].astype(F32)
    meta_ref[6:10, :] = cnt_ref[...].astype(F32)
    row_hot = jnp.where(iota((half * room, rays), 0) == row_place, 1.0, 0.0).astype(BF16)
    codes_ref[...] = dot(row_hot, code_ref[...]).astype(BF16)
    lane_hot = jnp.where(iota((rays, rays), 0) == lane_place, 1.0, 0.0).astype(BF16)
    meta = dot(meta_ref[...].astype(BF16), lane_hot, 1, 1)
    wh_t = wh_ref[0].astype(F32).T.astype(BF16)
    density = wd_ref[...].astype(F32)
    first = iota((16, LANES), 0) == 0

    def rays_for(k):
        chip = jnp.bitwise_xor(mine, k)
        here = pltpu.roll(meta, (rays - chip * 2 * group) & (rays - 1), 1)[:, :LANES]
        codes = codes_ref[pl.ds(pl.multiple_of(chip * room, 16), room), :]
        return jnp.where(first, density, here).astype(BF16), codes

    for side, ref in enumerate((near_ref, far_ref)):
        ref[0:WF_AT] = wh_t
        ref[WF_AT:SAMPLE_AT] = wf_ref[0]
        ref[SAMPLE_AT:META_AT] = samp_ref[0]
        for k in range(half // 2):
            at = META_AT + k * (16 + room)
            ref[at : at + 16], ref[at + 16 : at + 16 + room] = rays_for(k + side * (half // 2))


def relay_kernel(near_ref, far_ref, *outs):
    for k, out in enumerate(outs):
        rows = out.shape[1] - META_AT
        for side, ref in enumerate((near_ref, far_ref)):
            out[side, 0:META_AT] = ref[0:META_AT]
            out[side, META_AT:] = ref[META_AT + k * rows : META_AT + (k + 1) * rows]


def bits_of(row, regions):
    count = regions.bit_length() - 1
    row = jnp.broadcast_to(row, (8, LANES))
    return [(lax.shift_right_logical(row, b) & 1) == 1 for b in range(count)]


def choose(values, bits):
    for bit in bits:
        values = [jnp.where(bit, values[i + 1], values[i]) for i in range(0, len(values), 2)]
    return values[0]


def fold(source_ref, rel_ref, out_ref):
    segs, rays = rel_ref.shape
    regions = out_ref.shape[0]

    def step(pair, carry):
        rows = pl.ds(pl.multiple_of(pair * 16, 16), 16)
        for part in range(rays // LANES):
            lanes = slice(part * LANES, (part + 1) * LANES)
            rel = [jnp.broadcast_to(rel_ref[k : k + 1, lanes], (16, LANES)) for k in range(segs)]
            held = [source_ref[rows, k * rays + part * LANES : k * rays + (part + 1) * LANES] for k in range(segs)]
            for r in range(regions):
                total = jnp.where(rel[0] == r, held[0], 0.0)
                for k in range(1, segs):
                    total = jnp.where(rel[k] == r, held[k], total)
                out_ref[r, rows, lanes] = total.astype(BF16)
        return carry

    lax.fori_loop(0, source_ref.shape[0] // 16, step, 0, unroll=2)


def fold_kernel(source_ref, rel_ref, out_ref):
    fold(source_ref, rel_ref, out_ref)


def pick(source_ref, rel_ref, out_ref, first=0):
    segs, rays = rel_ref.shape
    regions = source_ref.shape[0]
    for part in range(rays // LANES):
        lanes = slice(part * LANES, (part + 1) * LANES)

        def step(index, carry):
            rows = pl.ds(pl.multiple_of(index * 8, 8), 8)
            bits = [bits_of(rel_ref[k : k + 1, lanes], regions) for k in range(segs)]
            values = [source_ref[r, rows, lanes] for r in range(regions)]
            for k in range(segs):
                found = choose(values, bits[k])
                at = slice(k * rays + part * LANES, k * rays + (part + 1) * LANES)
                if first > 0:
                    here = lax.shift_right_logical(rel_ref[k : k + 1, lanes], len(bits[k])) == first // regions
                    found = jnp.where(here, found, out_ref[rows, at])
                out_ref[rows, at] = found
            return carry

        lax.fori_loop(0, source_ref.shape[1] // 8, step, 0, unroll=4)


def seg_hot(wanted, regions):
    return jnp.concatenate(
        [jnp.where(iota((regions, row.shape[1]), 0) == row, 1.0, 0.0) for row in wanted], axis=1
    )


def forward_kernel(half, group, room, *refs):
    regions = 2 * half
    quarter = half // 2
    received, target_ref = refs[:half], refs[half]
    blocks = [received[c * quarter + k].at[side] for c in range(2) for side in range(2) for k in range(quarter)]
    (
        image_ref, halo_in_ref, halo_cr_ref, h_ref, wd_ref, att_hw_ref, weight_ref, pass_ref, slope_ref, att_ref, rel_ref, codes_ref, wf_up,
        wide_hw_ref, wf_out,        meta_ref, plain_ref, table_ref, proj_ref, a_ref, picked_ref, row_ref, density_ref,
    ) = refs[half + 1 :]
    rays = codes_ref.shape[1]
    segs = rel_ref.shape[0]
    samples = weight_ref.shape[0]
    feats = image_ref.shape[0]
    hids = table_ref.shape[1]
    me = lax.axis_index("region")
    core = me & 1
    chip = lax.shift_right_logical(me, 1)
    per_tile = LANES // room
    lane = iota((16, LANES), 1)
    chunk = lax.div(lane, room)
    inside = lane - chunk * room
    mine = (inside < 2 * group) & (lax.div(inside, group) == core)
    for tile in range(regions // per_tile):
        total = jnp.zeros((16, LANES), F32)
        for spot in range(per_tile):
            block = blocks[tile * per_tile + spot][META_AT:RAYS_AT].astype(F32)
            total = jnp.where(chunk == spot, pltpu.roll(block, spot * room, 1), total)
        meta_ref[:, tile * LANES : (tile + 1) * LANES] = jnp.where(mine, total, -1.0)
    meta_src = meta_ref[...]
    places = regions * room
    to_pixel = jnp.where(
        iota((rays, places), 0).astype(F32) == meta_src[1:2, :], 1.0, 0.0
    ).astype(BF16)
    sources = jnp.concatenate([block[RAYS_AT : RAYS_AT + room] for block in blocks], axis=0)
    codes_t = dot(to_pixel, sources).T.astype(BF16)
    codes_ref[...] = codes_t
    meta = dot(meta_src.astype(BF16), to_pixel, 1, 1)
    region = meta[2 : 2 + segs].astype(jnp.int32)
    rel = jnp.bitwise_xor(region & 1, core) * half + jnp.bitwise_xor(lax.shift_right_logical(region, 1), chip)
    rel_ref[...] = rel
    for k in range(segs):
        row_ref[:, k * rays : (k + 1) * rays] = meta[6 + k : 7 + k]
    wanted = [rel_ref[k : k + 1, :] for k in range(segs)]
    for r, block in enumerate(blocks):
        w_t = block[0:WF_AT]
        proj_ref[r] = dot(w_t, codes_t)
        plain_ref[0:samples, r, :] = dot(block[SAMPLE_AT:META_AT], w_t, 1, 1)
        plain_ref[samples, r : r + 1, :] = block[META_AT:RAYS_AT].astype(F32)[0:1, :]
        wf_out[r * feats : (r + 1) * feats] = block[WF_AT:SAMPLE_AT]
        wf_up[r] = block[WF_AT:SAMPLE_AT].astype(F32).T.astype(BF16)
    for s in range(samples + 1):
        high, low = split(plain_ref[s])
        table_ref[s] = jnp.concatenate([high.astype(F32), low.astype(F32)], axis=0).T.astype(BF16)
    pick(proj_ref, rel_ref, a_ref)
    hot = seg_hot(wanted, regions).astype(BF16)
    hot2 = jnp.concatenate([hot, hot], axis=0)
    for tile in range(2 * segs):
        picked_ref[tile] = hot2[:, tile * LANES : (tile + 1) * LANES]

    def densities(tile, carry):
        here = picked_ref[tile]
        lanes = pl.ds(pl.multiple_of(tile * LANES, LANES), LANES)
        wd_ref[tile] = dot(table_ref[samples], here)
        sums = []
        for s in range(samples):
            h = jnp.maximum(a_ref[:, lanes] + dot(table_ref[s], here), 0.0)
            h_ref[tile, s] = h
            sums.append(jnp.sum(h * wd_ref[tile], axis=0, keepdims=True))
        density_ref[:, lanes] = jnp.concatenate(sums, axis=0)
        return carry

    lax.fori_loop(0, 2 * segs, densities, 0, unroll=4)
    density = density_ref[...]
    live = iota(density.shape, 0).astype(F32) < row_ref[...]
    soft = jnp.maximum(density, 0.0) + jnp.log1p(jnp.exp(-jnp.abs(density)))
    thick = jnp.where(live, STEP * soft, 0.0)
    through = running_sum(thick)
    passing = jnp.exp(-(through - thick))
    keeping = jnp.exp(-thick)
    weight = passing * (1.0 - keeping)
    weight_ref[...] = weight
    pass_ref[...] = passing * keeping
    slope_ref[...] = jnp.where(live, STEP / (1.0 + jnp.exp(-density)), 0.0)
    ahead = jnp.zeros((1, rays), F32)
    for k in range(segs):
        att_ref[:, k * rays : (k + 1) * rays] = jnp.exp(-ahead)
        ahead = ahead + through[samples - 1 : samples, k * rays : (k + 1) * rays]
    density_ref[...] = weight * att_ref[...]

    def compose(tile, carry):
        lanes = pl.ds(pl.multiple_of(tile * LANES, LANES), LANES)
        faded = density_ref[:, lanes]
        scale = [jnp.broadcast_to(faded[s : s + 1, :], (8, LANES)) for s in range(samples)]
        for pair in range(8):
            both = []
            for ht in (2 * pair, 2 * pair + 1):
                rows = slice(ht * 8, ht * 8 + 8)
                total = scale[0] * h_ref[tile, 0, rows, :]
                for s in range(1, samples):
                    total = total + scale[s] * h_ref[tile, s, rows, :]
                both.append(total)
            both = jnp.concatenate(both, axis=0)
            high, low = split(both)
            att_hw_ref[pair * 16 : pair * 16 + 16, lanes] = both
            wide_hw_ref[pair * 16 : pair * 16 + 16, lanes] = high
            wide_hw_ref[hids + pair * 16 : hids + pair * 16 + 16, lanes] = low
        return carry

    lax.fori_loop(0, 2 * segs, compose, 0, unroll=2)
    wf_twice = jnp.concatenate([wf_out[...], wf_out[...]], axis=1)
    feat = [jnp.zeros((8, LANES), F32)] * (2 * (feats // 8))
    for k in range(segs):
        values = dot(wf_twice, wide_hw_ref[:, k * rays : (k + 1) * rays])
        for r in range(regions * feats // LANES):
            proj_ref[r] = values[r * LANES : (r + 1) * LANES]
        for part in range(2):
            lanes = slice(part * LANES, (part + 1) * LANES)
            bits = bits_of(wanted[k][:, lanes], regions)
            for ft in range(feats // 8):
                found = []
                for r in range(regions):
                    at = r * feats + ft * 8
                    found.append(proj_ref[at // LANES, at % LANES : at % LANES + 8, lanes])
                feat[2 * ft + part] = feat[2 * ft + part] + choose(found, bits)
    for part in range(2):
        image_ref[:, part * LANES : (part + 1) * LANES] = jnp.concatenate(feat[part::2], axis=0).astype(BF16)
    near, far = target_ref[:, :IW].astype(F32), target_ref[:, rays - IW :].astype(F32)
    for out_ref, row in ((halo_in_ref, jnp.where(core == 0, far, near)), (halo_cr_ref, jnp.where(core == 0, near, far))):
        out_ref[0:feats] = image_ref[...]
        depth = target_ref.shape[0] // 2
        out_ref[feats:, 0:IW] = row[:depth].astype(BF16)
        out_ref[feats:, rays - IW :] = row[depth:].astype(BF16)


def shifted(values, by):
    lane = iota(values.shape, 1)
    if by == 0:
        return values
    if by > 0:
        return jnp.where(lane == 0, 0.0, pltpu.roll(values, 1, 1))
    return jnp.where(lane == LANES - 1, 0.0, pltpu.roll(values, LANES - 1, 1))


def backward_kernel(
    half, own_ref, inner_ref, cross_ref, tgt_ref, dec_ref, dect_ref,
    folded_ref, h_in, wd_ref, att_hw_ref, weight_ref, pass_ref, slope_ref, att_ref, rel_ref, codes_ref, wf_ref,
    mine_ref, other_ref,
    patch_ref, proj_ref, q_ref, gp_ref, g1_ref, held_ref, hd_ref, tail_ref, row_ref, along_ref,
):
    regions = 2 * half
    feats, rays = own_ref.shape
    segs = rel_ref.shape[0]
    samples = weight_ref.shape[0]
    hids = wd_ref.shape[1]
    me = lax.axis_index("region")
    core = me & 1
    own = own_ref[...].astype(F32)
    halo_in = inner_ref[...].astype(F32)
    halo_cr = cross_ref[...].astype(F32)
    inner, tin = halo_in[:feats], jnp.concatenate([halo_in[feats:, :IW], halo_in[feats:, rays - IW :]], axis=0)
    cross, tcr = halo_cr[:feats], jnp.concatenate([halo_cr[feats:, :IW], halo_cr[feats:, rays - IW :]], axis=0)
    top = jnp.where(core == 0, cross, inner)
    bottom = jnp.where(core == 0, inner, cross)
    rows = [v[:, i * IW : (i + 1) * IW] for v in (top, own, bottom) for i in range(2)]
    for at, row in enumerate(rows):
        for dx in range(3):
            piece = shifted(row, 1 - dx).astype(BF16)
            for dy in range(3):
                if 0 <= at - dy < 4:
                    patch_ref[(3 * dy + dx) * feats : (3 * dy + dx + 1) * feats, (at - dy) * IW : (at - dy + 1) * IW] = piece
    t_top = jnp.where(core == 0, tcr, tin)
    t_bottom = jnp.where(core == 0, tin, tcr)
    decoded = dot(dect_ref[...], patch_ref[...])
    tgt = tgt_ref[...].astype(F32)
    g_top = jnp.where(me > 0, decoded[:, 0:IW] - t_top, 0.0)
    g_own = decoded[:, IW : 3 * IW] - tgt
    g_bottom = jnp.where(me < regions - 1, decoded[:, 3 * IW :] - t_bottom, 0.0)
    grad_dec = jnp.concatenate([g_top, g_own, g_bottom], axis=1).astype(BF16)
    grad_patch = dot(dec_ref[...], grad_dec)
    image_rows = []
    for i in range(2):
        total = jnp.zeros((feats, IW), F32)
        for dx in range(3):
            term = jnp.zeros((feats, IW), F32)
            for dy in range(3):
                at = (3 * dy + dx) * feats
                term = term + grad_patch[at : at + feats, (i - dy + 2) * IW : (i - dy + 3) * IW]
            total = total + shifted(term, dx - 1)
        image_rows.append(total)
    grad_ray = jnp.concatenate(image_rows, axis=1)
    wanted = [rel_ref[k : k + 1, :] for k in range(segs)]
    hot = seg_hot(wanted, regions).astype(BF16)
    grad_narrow = grad_ray.astype(BF16)
    group = proj_ref.shape[0]
    for r in range(regions):
        proj_ref[r % group] = dot(wf_ref[r], grad_narrow)
        out, to = (mine_ref, r) if r < half else (other_ref, r - half)
        out[to, WF_AT:G2_AT] = dot(grad_narrow, folded_ref[r], 1, 1).astype(BF16)
        if (r + 1) % group == 0:
            pick(proj_ref, rel_ref, q_ref, r + 1 - group)
    later = jnp.zeros((1, rays), F32)
    for k in reversed(range(segs)):
        lanes = slice(k * rays, (k + 1) * rays)
        row_ref[:, lanes] = -later
        later = later + jnp.sum(att_hw_ref[:, lanes] * q_ref[:, lanes], axis=0, keepdims=True)

    def project(tile, carry):
        lanes = pl.ds(pl.multiple_of(tile * LANES, LANES), LANES)
        att = jnp.broadcast_to(att_ref[:, lanes], (8, LANES))
        sums = [jnp.zeros((8, LANES), F32)] * samples
        for ht in range(16):
            rows = slice(ht * 8, ht * 8 + 8)
            q = q_ref[rows, lanes] * att
            q_ref[rows, lanes] = q
            for s in range(samples):
                sums[s] = sums[s] + h_in[tile, s, rows, :] * q
        along_ref[:, lanes] = jnp.concatenate([jnp.sum(v, axis=0, keepdims=True) for v in sums], axis=0)
        return carry

    lax.fori_loop(0, 2 * segs, project, 0)
    along = along_ref[...]
    through = running_sum(along * weight_ref[...])
    later = through[samples - 1 : samples, :] - through
    grad_thick = row_ref[...] + along * pass_ref[...] - later
    along_ref[...] = (grad_thick * slope_ref[...]).astype(BF16).astype(F32)

    def descend(tile, carry):
        lanes = pl.ds(pl.multiple_of(tile * LANES, LANES), LANES)
        weight = weight_ref[:, lanes]
        grad_density = along_ref[:, lanes]
        scale = [jnp.broadcast_to(weight[s : s + 1, :], (8, LANES)) for s in range(samples)]
        slant = [jnp.broadcast_to(grad_density[s : s + 1, :], (8, LANES)) for s in range(samples)]
        for pair in range(8):
            at = [slice((2 * pair + u) * 8, (2 * pair + u) * 8 + 8) for u in range(2)]
            q = [q_ref[rows, lanes] for rows in at]
            wd = [wd_ref[tile, rows, :] for rows in at]
            g1 = [jnp.zeros((8, LANES), F32)] * 2
            hd = [jnp.zeros((8, LANES), F32)] * 2
            for s in range(samples):
                both = []
                for u in range(2):
                    h = h_in[tile, s, at[u], :]
                    gp = jnp.where(h > 0.0, scale[s] * q[u] + slant[s] * wd[u], 0.0)
                    g1[u] = g1[u] + gp
                    hd[u] = hd[u] + slant[s] * h
                    both.append(gp)
                gp_ref[s * hids + 16 * pair : s * hids + 16 * pair + 16, lanes] = jnp.concatenate(both, axis=0).astype(BF16)
            g1_ref[16 * pair : 16 * pair + 16, lanes] = jnp.concatenate(g1, axis=0)
            hd_ref[16 * pair : 16 * pair + 16, lanes] = jnp.concatenate(hd, axis=0).astype(BF16)
        return carry

    lax.fori_loop(0, 2 * segs, descend, 0)
    tail_ref[...] = jnp.zeros(tail_ref.shape, F32)
    for s in range(samples):
        tail_ref[:, s, :] = dot(hot, gp_ref[s * hids : (s + 1) * hids], 1, 1)
    tail_ref[:, samples, :] = dot(hot, hd_ref[...], 1, 1)
    codes = codes_ref[...]
    fold(g1_ref, rel_ref, held_ref)
    for r in range(regions):
        out, to = (mine_ref, r) if r < half else (other_ref, r - half)
        out[to, 0:WF_AT] = dot(codes, held_ref[r], 1, 1).astype(BF16)
        out[to, G2_AT:PART_ROWS] = tail_ref[r].astype(BF16)


def flip_target_kernel(target_ref, near_ref, target_out, near_out):
    near_out[...] = near_ref[...]
    target_out[...] = target_ref[...].astype(F32).T.astype(BF16)


def flip_decoder_kernel(decoder_ref, decoder_out, same_out):
    same_out[...] = decoder_ref[...]
    decoder_out[...] = decoder_ref[...].astype(F32).T.astype(BF16)


def merge_kernel(mine_ref, theirs_ref, *outs):
    for k, out in enumerate(outs):
        for side in range(2):
            at = side * len(outs) + k
            out[side] = (mine_ref[at].astype(F32) + theirs_ref[at].astype(F32)).astype(BF16)


def reduce_kernel(*refs):
    parts, (keep_ref, send_ref) = refs[:-2], refs[-2:]
    for side, out in enumerate((keep_ref, send_ref)):
        total = parts[0][side].astype(F32)
        for part in parts[1:]:
            total = total + part[side].astype(F32)
        out[...] = total.astype(out.dtype)


def finish_kernel(keep_ref, part_ref, samp_ref, wh_ref, hid_ref, feat_ref, dens_ref, code_ref):
    total = keep_ref[...] + part_ref[...].astype(F32)
    high, low = split(total[G2_AT:DG_AT])
    samples = samp_ref[0]
    wh = wh_ref[0]
    hid_ref[0] = total[0:WF_AT] + dot(samples, high, 0, 0) + dot(samples, low, 0, 0)
    feat_ref[0] = total[WF_AT:G2_AT]
    dens_ref[...] = total[DG_AT : DG_AT + 1]
    code_ref[0] = dot(high, wh, 1, 1) + dot(low, wh, 1, 1)


def local(ray_code, seg_region, seg_count, pixel_of_ray, sample_code, w_hidden, w_feat, w_density, decoder, target):
    regions = lax.axis_size("region")
    half = regions // 2
    rays, segs = seg_region.shape
    code_width = ray_code.shape[1]
    hid_width = w_hidden.shape[2]
    feat_width = w_feat.shape[2]
    dino_width = target.shape[1]
    samples = sample_code.shape[1]
    group = rays // regions
    room = max(16, 2 * group)
    tiles = 2 * segs
    lanes = segs * rays
    inner = [(i, i ^ 1) for i in range(regions)]
    cross = [(i, i + 1) for i in range(1, regions - 1, 2)] + [(i + 1, i) for i in range(1, regions - 1, 2)]

    def shape(*dims, kind=F32):
        return jax.ShapeDtypeStruct(dims, kind)

    quarter = half // 2
    pack_rows = RAYS_AT + room

    def to_chip(block, k):
        return lax.ppermute(block, "region", [(i, i ^ (2 * k)) for i in range(regions)])

    def to_half(blocks):
        sent = {k: to_chip(blocks[k], k) for k in reversed(range(1, quarter))}
        return [blocks[0]] + [sent[k] for k in range(1, quarter)]

    pack_args = (
        pixel_of_ray.reshape(1, rays), seg_region.T, seg_count.T,
        ray_code, sample_code, w_hidden, w_feat.swapaxes(1, 2), w_density,
    )
    near, far = pl.pallas_call(
        functools.partial(pack_kernel, half, group, room),
        out_shape=(
            shape(META_AT + quarter * (16 + room), LANES, kind=BF16),
            shape(META_AT + quarter * (16 + room), LANES, kind=BF16),
        ),
        in_specs=[pl.BlockSpec(memory_space=pltpu.HBM)] * 8,
        scratch_shapes=[pltpu.VMEM(x.shape, x.dtype) for x in pack_args]
        + [
            pltpu.SemaphoreType.DMA((8,)),
            pltpu.VMEM((16, rays), F32),
            pltpu.VMEM((half * room, LANES), BF16),
        ],
        compiler_params=grant(60),
        name="pack",
    )(*pack_args)
    far = to_chip(far, quarter)
    flipped = pl.pallas_call(
        flip_target_kernel,
        out_shape=(shape(dino_width, rays, kind=BF16), shape(*near.shape, kind=BF16)),
        compiler_params=grant(8 + regions / 8),
        name="flip_target",
    )(target, near)
    far, (target_t, near) = lax.optimization_barrier((far, flipped))
    blocks = to_half(
        pl.pallas_call(
            relay_kernel,
            out_shape=[shape(2, pack_rows, LANES, kind=BF16)] * quarter,
            compiler_params=grant(8 + regions / 8),
            name="relay",
        )(near, far)
    )
    blocks = blocks + [lax.ppermute(block, "region", inner) for block in blocks]

    image, halo_in, halo_cr, *kept = pl.pallas_call(
        functools.partial(forward_kernel, half, group, room),
        out_shape=(
            shape(feat_width, rays, kind=BF16),
            shape(feat_width + dino_width // 2, rays, kind=BF16),
            shape(feat_width + dino_width // 2, rays, kind=BF16),
            shape(tiles, samples, hid_width, LANES),
            shape(tiles, hid_width, LANES),
            shape(hid_width, lanes),
            shape(samples, lanes),
            shape(samples, lanes),
            shape(samples, lanes),
            shape(1, lanes),
            shape(segs, rays, kind=jnp.int32),
            shape(code_width, rays, kind=BF16),
            shape(regions, hid_width, feat_width, kind=BF16),
        ),
        scratch_shapes=[
            pltpu.VMEM((2 * hid_width, lanes), BF16),
            pltpu.VMEM((regions * feat_width, hid_width), BF16),
            pltpu.VMEM((16, regions * room), F32),
            pltpu.VMEM((samples + 1, regions, hid_width), F32),
            pltpu.VMEM((samples + 1, hid_width, 2 * regions), BF16),
            pltpu.VMEM((regions, hid_width, rays), F32),
            pltpu.VMEM((hid_width, lanes), F32),
            pltpu.VMEM((tiles, 2 * regions, LANES), BF16),
            pltpu.VMEM((1, lanes), F32),
            pltpu.VMEM((samples, lanes), F32),
        ],
        compiler_params=grant(10 + regions / 4),
        name="forward",
    )(*blocks, target_t)

    halo_in = lax.ppermute(halo_in, "region", inner)
    halo_cr = lax.ppermute(halo_cr, "region", cross)
    decoder, sums = lax.optimization_barrier((decoder, kept[2]))
    decoder_t, decoder = pl.pallas_call(
        flip_decoder_kernel,
        out_shape=(shape(*decoder.shape[::-1], kind=BF16), shape(*decoder.shape, kind=BF16)),
        compiler_params=grant(8),
        name="flip_decoder",
    )(decoder)
    folded = pl.pallas_call(
        fold_kernel,
        out_shape=shape(regions, hid_width, rays, kind=BF16),
        compiler_params=grant(8 + regions / 4),
        name="fold",
    )(sums, kept[7])

    part = shape(half, PART_ROWS, LANES, kind=BF16)
    mine, other = pl.pallas_call(
        functools.partial(backward_kernel, half),
        out_shape=(part, part),
        scratch_shapes=[
            pltpu.VMEM((decoder.shape[0], 4 * IW), BF16),
            pltpu.VMEM((min(regions, 16), hid_width, rays), F32),
            pltpu.VMEM((hid_width, lanes), F32),
            pltpu.VMEM((samples * hid_width, lanes), BF16),
            pltpu.VMEM((hid_width, lanes), F32),
            pltpu.VMEM((regions, hid_width, rays), BF16),
            pltpu.VMEM((hid_width, lanes), BF16),
            pltpu.VMEM((regions, PART_ROWS - G2_AT, hid_width), F32),
            pltpu.VMEM((1, lanes), F32),
            pltpu.VMEM((samples, lanes), F32),
        ],
        compiler_params=grant(22 + regions / 4),
        name="backward",
    )(image, halo_in, halo_cr, target_t, decoder, decoder_t, folded, *kept)

    theirs = lax.ppermute(other, "region", inner)
    parts = pl.pallas_call(
        merge_kernel,
        out_shape=[shape(2, PART_ROWS, LANES, kind=BF16)] * quarter,
        compiler_params=grant(8 + regions / 8),
        name="merge",
    )(mine, theirs)
    keep, send = pl.pallas_call(
        reduce_kernel,
        out_shape=(shape(PART_ROWS, LANES), shape(PART_ROWS, LANES, kind=BF16)),
        compiler_params=grant(8 + regions / 8),
        name="reduce",
    )(*to_half(parts))
    hid_grad, feat_grad, dens_grad, code_grad = pl.pallas_call(
        finish_kernel,
        out_shape=(
            shape(1, code_width, hid_width),
            shape(1, feat_width, hid_width),
            shape(1, hid_width),
            shape(1, samples, code_width),
        ),
        compiler_params=grant(8 + regions / 8),
        name="finish",
    )(keep, to_chip(send, quarter), sample_code, w_hidden)
    return hid_grad, feat_grad.swapaxes(1, 2), dens_grad, code_grad


def solution(mesh):
    in_specs = (
        P(("groups", "region"), None),
        P(("groups", "region"), None),
        P(("groups", "region"), None),
        P(("groups", "region")),
        P("region", None, None),
        P("region", None, None),
        P("region", None, None),
        P("region", None),
        P(),
        P(("groups", "region"), None),
    )
    out_specs = (
        P("region", "groups", None),
        P("region", "groups", None),
        P("region", "groups"),
        P("region", "groups", None),
    )
    return jax.shard_map(local, mesh=mesh, in_specs=in_specs, out_specs=out_specs, check_vma=False)
```
